32 devices in a mesh: dp: 8 (over z, x), seq: 4 (over y, core).
Axes of the slice: x: 2, y: 2, z: 4, core: 2. Of those that a mesh axis runs over, the one named last changes fastest.
Arguments:
- tokens: bfloat16 [16384, 1024], P(('dp', 'seq')), may hold values from -6 to 6
- out_grad: bfloat16 [16384, 1024], P(('dp', 'seq')), may hold values from -6 to 6
- qkv_weight: bfloat16 [1024, 3072], P('dp'), may hold values from -0.25 to 0.25
- qv_bias: bfloat16 [2, 1024], P(None, 'dp'), may hold values from -3 to 3
- proj_weight: bfloat16 [1024, 1024], P('dp'), may hold values from -0.1875 to 0.1875
- fc1_weight: bfloat16 [1024, 4096], P('dp'), may hold values from -0.1875 to 0.1875
- fc1_bias: bfloat16 [4096], P('dp'), may hold values from -3 to 3
- fc2_weight: bfloat16 [4096, 1024], P('dp'), may hold values from -0.09375 to 0.09375
- out_bias: bfloat16 [2, 1024], P(None, 'dp'), may hold values from -3 to 3
- norm_gains: bfloat16 [4, 1024], P(None, 'dp'), may hold values from 0.5 to 1.5
- norm_shifts: bfloat16 [4, 1024], P(None, 'dp'), may hold values from -2 to 2
Outputs:
- layer_out: bfloat16 [16384, 1024], P(('dp', 'seq'))
- tokens_grad: bfloat16 [16384, 1024], P(('dp', 'seq'))
- qkv_weight_grad: float32 [1024, 3072], P('dp')
- qv_bias_grad: float32 [2, 1024], P(None, 'dp')
- proj_weight_grad: float32 [1024, 1024], P('dp')
- fc1_weight_grad: float32 [1024, 4096], P('dp')
- fc1_bias_grad: float32 [4096], P('dp')
- fc2_weight_grad: float32 [4096, 1024], P('dp')
- out_bias_grad: float32 [2, 1024], P(None, 'dp')
- norm_gains_grad: float32 [4, 1024], P(None, 'dp')
- norm_shifts_grad: float32 [4, 1024], P(None, 'dp')
The draws below stay inside these ranges and needn't reach their ends.
All inputs are finite; a program needn't handle non-finite values.
Results may differ from the reference program's by a relative error of at most 0.015.
The reference program's roundings to bfloat16 on the way count: a program that leaves them out, or rounds other values in their place, can miss the bound.
Values may be sent and summed in bfloat16 or wider, within the bound.
No kernel may reach another device: no remote copies, remote signals or barrier semaphores. Data moves between devices by JAX's collectives and lax.ppermute only.
A program may use at most 192 MiB of HBM per device.

```python
import math
import jax
import jax.numpy as jnp
from jax import lax

D = 1024
HEADS = 16
HEAD_DIM = 64
FF = 4096
SEQ_LEN = 2048
TOKENS = 16384


def level_of(key, dims, pieces, smallest, top_value):
    level, own = 1.0, jax.random.fold_in(key, 6)
    for dim, parts in pieces:
        draws = jnp.exp(jax.random.uniform(jax.random.fold_in(own, dim), (parts,), jnp.float32, smallest / len(pieces), top_value / len(pieces)))
        level = level * jnp.repeat(draws, dims[dim] // parts).reshape([-1 if axis == dim else 1 for axis in range(len(dims))])
    return level


def scatter_about(own_key, dims, spread, most, cuts=(), held_as=jnp.bfloat16):
    drawn = jax.random.normal(own_key, dims, jnp.float32) * spread
    if len(cuts) > 0:
        drawn = level_of(own_key, dims, cuts, -0.22, 0.18) * drawn
    return jnp.clip(drawn, min=-most, max=most).astype(held_as)


def setup_inputs(seed: int = 0) -> dict:
    keys = jax.random.split(jax.random.key(seed), 12)
    tokens = scatter_about(keys[0], (TOKENS, D), 1.0, 6.0, ((0, 32),))
    out_grad = scatter_about(keys[1], (TOKENS, D), 1.0, 6.0, ((0, 32),))
    qkv_weight = scatter_about(keys[2], (D, 3 * D), (D // 2) ** -0.5, 0.25, ((0, 8),))
    qv_bias = scatter_about(keys[3], (2, D), 0.5, 3.0, ((1, 8),))
    proj_weight = scatter_about(keys[4], (D, D), D ** -0.5, 0.1875, ((0, 8),))
    fc1_weight = scatter_about(keys[5], (D, FF), D ** -0.5, 0.1875, ((0, 8),))
    fc1_bias = scatter_about(keys[6], (FF,), 0.5, 3.0, ((0, 8),))
    fc2_weight = scatter_about(keys[7], (FF, D), FF ** -0.5, 0.09375, ((0, 8),))
    out_bias = scatter_about(keys[8], (2, D), 0.5, 3.0, ((1, 8),))
    norm_gains = jnp.clip(1.0 + 0.1 * jax.random.normal(keys[9], (4, D), jnp.float32), 0.5, 1.5).astype(jnp.bfloat16)
    norm_shifts = scatter_about(keys[10], (4, D), 0.3, 2.0, ((1, 8),))
    return dict(tokens=tokens, out_grad=out_grad, qkv_weight=qkv_weight, qv_bias=qv_bias, proj_weight=proj_weight, fc1_weight=fc1_weight, fc1_bias=fc1_bias, fc2_weight=fc2_weight, out_bias=out_bias, norm_gains=norm_gains, norm_shifts=norm_shifts)


@jax.custom_vjp
def low(v):
    return lax.optimization_barrier(v.astype(jnp.bfloat16)).astype(jnp.float32)

@jax.custom_vjp
def low_back(v):
    return v

def low_keep(v):
    return (low(v), None)

def low_pass(kept, grad):
    return (grad,)

def back_keep(v):
    return (v, None)

def back_low(kept, grad):
    return (low(grad),)
low.defvjp(low_keep, low_pass)
low_back.defvjp(back_keep, back_low)
RELAX_ALPHA = 32.0
NORM_EPS = 1e-05
PREC_HIGH = lax.Precision.HIGHEST

def narrow_both(values):
    return low_back(low(values))

def layer_norm(values, gain_vec, shift_vec):
    centred = values - lax.optimization_barrier(jnp.mean(values, axis=-1, keepdims=True))
    variance = lax.optimization_barrier(jnp.mean(centred * centred, axis=-1, keepdims=True))
    return centred * lax.rsqrt(variance + NORM_EPS) * gain_vec + shift_vec

def matmul(left, right):
    return jnp.dot(left, right, precision=PREC_HIGH)

def attend_sequence(queries, key_rows, values):
    seq_len = queries.shape[0]
    block_rows = min(512, seq_len)
    blocks = seq_len // block_rows
    q_heads = queries.reshape(blocks, block_rows, HEADS, HEAD_DIM)
    k_heads = key_rows.reshape(seq_len, HEADS, HEAD_DIM)
    v_heads = values.reshape(seq_len, HEADS, HEAD_DIM)
    starts = jnp.arange(blocks, dtype=jnp.int32) * block_rows

    def one_block(block_pair):
        block_start, q_block = block_pair
        scores = low_back(jnp.einsum('qhd,khd->hqk', q_block, k_heads, precision=PREC_HIGH))
        row_index = block_start + jnp.arange(block_rows, dtype=jnp.int32)
        col_index = jnp.arange(seq_len, dtype=jnp.int32)
        causal = (row_index[:, None] >= col_index[None, :])[None]
        logits = jnp.where(causal, RELAX_ALPHA * scores, -1e+30)
        probs = low(jax.nn.softmax(logits, axis=-1))
        return jnp.einsum('hqk,khd->qhd', probs, v_heads, precision=PREC_HIGH)
    out_blocks = lax.map(jax.checkpoint(one_block), (starts, q_heads))
    return out_blocks.reshape(seq_len, HEADS * HEAD_DIM)

def full_layer(weights, tok_one):
    qkv_w, qv_b, proj_w, fc1_w, fc1_b, fc2_w, out_b, gain_rows, shift_rows = weights
    normed = low(layer_norm(tok_one, gain_rows[0], shift_rows[0]))
    mixed_cols = matmul(normed, qkv_w)
    query_scale = 1.0 / (RELAX_ALPHA * math.sqrt(HEAD_DIM))
    queries = narrow_both((mixed_cols[:, :D] + qv_b[0]) * query_scale)
    key_rows = narrow_both(mixed_cols[:, D:2 * D])
    values = narrow_both(mixed_cols[:, 2 * D:] + qv_b[1])
    attended = narrow_both(attend_sequence(queries, key_rows, values))
    branch = low_back(matmul(attended, proj_w) + out_b[0])
    residual = tok_one + layer_norm(branch, gain_rows[1], shift_rows[1])
    normed_two = low(layer_norm(residual, gain_rows[2], shift_rows[2]))
    hidden = low_back(matmul(normed_two, fc1_w) + fc1_b)
    active = low(jax.nn.gelu(hidden, approximate=True))
    second = low_back(matmul(active, fc2_w) + out_b[1])
    return residual + layer_norm(second, gain_rows[3], shift_rows[3])

def reference(tokens, out_grad, qkv_weight, qv_bias, proj_weight, fc1_weight, fc1_bias, fc2_weight, out_bias, norm_gains, norm_shifts):
    weights = tuple((array_item.astype(jnp.float32) for array_item in (qkv_weight, qv_bias, proj_weight, fc1_weight, fc1_bias, fc2_weight, out_bias, norm_gains, norm_shifts)))
    seq_count = tokens.shape[0] // SEQ_LEN
    tok_seqs = tokens.astype(jnp.float32).reshape(seq_count, SEQ_LEN, D)
    grad_seqs = out_grad.astype(jnp.float32).reshape(seq_count, SEQ_LEN, D)
    zero_totals = jax.tree.map(jnp.zeros_like, weights)

    def per_sequence(grad_totals, seq_pair):
        tok_one, grad_one = seq_pair
        result, pullback = jax.vjp(full_layer, weights, tok_one)
        weight_grads, tok_grad = pullback(grad_one)
        return (jax.tree.map(jnp.add, grad_totals, weight_grads), (result, tok_grad))
    grad_totals, (results, tok_grads) = lax.scan(per_sequence, zero_totals, (tok_seqs, grad_seqs))
    layer_out = results.reshape(seq_count * SEQ_LEN, D).astype(jnp.bfloat16)
    tokens_grad = tok_grads.reshape(seq_count * SEQ_LEN, D).astype(jnp.bfloat16)
    return (layer_out, tokens_grad, grad_totals[0], grad_totals[1], grad_totals[2], grad_totals[3], grad_totals[4], grad_totals[5], grad_totals[6], grad_totals[7], grad_totals[8])
```

```python
import functools
import math

import jax
import jax.numpy as jnp
from jax.sharding import Mesh
from jax.sharding import PartitionSpec as P
from jax import lax
from jax.experimental import pallas as pl
from jax.experimental.pallas import tpu as pltpu
HD=64
RELAX=32.0
C2=RELAX*math.log2(math.e)
NEG=-1e30

def _nt(a,b):
    return lax.dot_general(a,b,(((1,),(1,)),((),())),preferred_element_type=jnp.float32)
def _nn(a,b):
    return lax.dot_general(a,b,(((1,),(0,)),((),())),preferred_element_type=jnp.float32)

def _tr(x):
    return jnp.transpose(x.astype(jnp.float32)).astype(jnp.bfloat16)

def fwd_kernel(q_ref,k_ref,v_ref,o_ref,ot_ref,lse_ref,vt_ref,*,nh,blk):
    seq=q_ref.shape[0]; w=nh*HD
    nb=seq//blk
    for b in range(nb):
        vt_ref[:,b*blk:(b+1)*blk]=_tr(v_ref[b*blk:(b+1)*blk,:])
    lane=lax.broadcasted_iota(jnp.int32,(1,w),1)//HD
    tri=lax.broadcasted_iota(jnp.int32,(blk,blk),0)<=lax.broadcasted_iota(jnp.int32,(blk,blk),1)
    def qstep(qb,_):
        q0=pl.multiple_of(qb*blk,blk)
        q=q_ref[pl.ds(q0,blk),:]
        qm=[jnp.where(lane==h,q,jnp.zeros_like(q)) for h in range(nh)]
        def kv(kb,carry,diag):
            k0=pl.multiple_of(kb*blk,blk)
            k=k_ref[pl.ds(k0,blk),:]
            out=[]
            for h in range(nh):
                m,l,acc=carry[3*h:3*h+3]
                s=_nt(k,qm[h])*C2
                if diag: s=jnp.where(tri,s,NEG)
                mn=jnp.maximum(m,jnp.max(s,axis=0,keepdims=True))
                a=jnp.exp2(m-mn)
                p=jnp.exp2(s-mn)
                l=l*a+jnp.sum(p,axis=0,keepdims=True)
                acc=acc*a+_nn(vt_ref[h*HD:(h+1)*HD,pl.ds(k0,blk)],p.astype(jnp.bfloat16))
                out+= [mn,l,acc]
            return tuple(out)
        init=[]
        for h in range(nh):
            init+=[jnp.full((1,blk),NEG,jnp.float32),jnp.zeros((1,blk),jnp.float32),jnp.zeros((HD,blk),jnp.float32)]
        c=kv(qb,tuple(init),True)
        c=lax.fori_loop(0,qb,lambda kb,cc: kv(kb,cc,False),c)
        for h in range(nh):
            m,l,acc=c[3*h:3*h+3]
            ot_ref[h*HD:(h+1)*HD,pl.ds(q0,blk)]=acc/l
            lse_ref[h:h+1,pl.ds(q0,blk)]=m+jnp.log2(l)
        o_ref[pl.ds(q0,blk),:]=jnp.transpose(ot_ref[:,pl.ds(q0,blk)]).astype(jnp.bfloat16)
        return 0
    lax.fori_loop(0,nb,qstep,0)

def attn_fwd(qkv, nh, blk=512):
    seq=qkv.shape[0]; w=nh*HD
    blk=min(blk,seq)
    vm=pl.BlockSpec(memory_space=pltpu.VMEM)
    return pl.pallas_call(functools.partial(fwd_kernel,nh=nh,blk=blk),
      grid=(1,),
      in_specs=[pl.BlockSpec((seq,w),lambda i,j=j:(0,j)) for j in range(3)],
      out_specs=[pl.BlockSpec((seq,w),lambda i:(0,0)),pl.BlockSpec((w,seq),lambda i:(0,0)),pl.BlockSpec((8,seq),lambda i:(0,0))],
      out_shape=[jax.ShapeDtypeStruct((seq,w),jnp.bfloat16),jax.ShapeDtypeStruct((w,seq),jnp.float32),jax.ShapeDtypeStruct((8,seq),jnp.float32)],
      scratch_shapes=[pltpu.VMEM((w,seq),jnp.bfloat16)],
      compiler_params=pltpu.CompilerParams(vmem_limit_bytes=48<<20),
      name="attn_fwd")(qkv,qkv,qkv)

def bwd_kernel(q_ref,k_ref,v_ref,do_ref,ot_ref,lse_ref,d_ref,kt_ref,dl_ref,dqt_ref,*,nh,blk):
    seq=q_ref.shape[0]; w=nh*HD
    nb=seq//blk
    for b in range(nb):
        sl=slice(b*blk,(b+1)*blk)
        kt_ref[:,sl]=_tr(k_ref[sl,:])
        dot_=jnp.transpose(do_ref[sl,:].astype(jnp.float32))
        pr=dot_*ot_ref[:,sl]
        for h in range(nh):
            dl_ref[h:h+1,sl]=jnp.sum(pr[h*HD:(h+1)*HD],axis=0,keepdims=True)
    dqt_ref[...]=jnp.zeros_like(dqt_ref)
    lane=lax.broadcasted_iota(jnp.int32,(1,w),1)//HD
    tri=lax.broadcasted_iota(jnp.int32,(blk,blk),0)<=lax.broadcasted_iota(jnp.int32,(blk,blk),1)
    def kstep(kb,_):
        k0=pl.multiple_of(kb*blk,blk)
        k=k_ref[pl.ds(k0,blk),:]
        v=v_ref[pl.ds(k0,blk),:]
        def qs(qb,carry,diag):
            dk,dv=carry
            q0=pl.multiple_of(qb*blk,blk)
            q=q_ref[pl.ds(q0,blk),:]
            do=do_ref[pl.ds(q0,blk),:]
            for h in range(nh):
                qm=jnp.where(lane==h,q,jnp.zeros_like(q))
                dom=jnp.where(lane==h,do,jnp.zeros_like(do))
                s=_nt(k,qm)
                dp=_nt(v,dom)
                p=jnp.exp2(s*C2-lse_ref[h:h+1,pl.ds(q0,blk)])
                if diag: p=jnp.where(tri,p,0.0)
                ds=(p*(dp-dl_ref[h:h+1,pl.ds(q0,blk)])).astype(jnp.bfloat16)
                dv=dv+_nn(p.astype(jnp.bfloat16),dom)
                dk=dk+_nn(ds,qm)
                dqt_ref[h*HD:(h+1)*HD,pl.ds(q0,blk)]+=_nn(kt_ref[h*HD:(h+1)*HD,pl.ds(k0,blk)],ds)
            return dk,dv
        z=jnp.zeros((blk,w),jnp.float32)
        c=qs(kb,(z,z),True)
        dk,dv=lax.fori_loop(kb+1,nb,lambda qb,cc: qs(qb,cc,False),c)
        d_ref[pl.ds(k0,blk),w:2*w]=(dk*RELAX).astype(jnp.bfloat16)
        d_ref[pl.ds(k0,blk),2*w:3*w]=dv.astype(jnp.bfloat16)
        return 0
    lax.fori_loop(0,nb,kstep,0)
    for b in range(nb):
        sl=slice(b*blk,(b+1)*blk)
        d_ref[sl,0:w]=(jnp.transpose(dqt_ref[:,sl])*(1.0/math.sqrt(HD))).astype(jnp.bfloat16)

def attn_bwd(qkv, do, ot, lse, nh, blk=512):
    seq=qkv.shape[0]; w=nh*HD
    blk=min(blk,seq)
    f=lambda s:pl.BlockSpec(s,lambda i:(0,0))
    return pl.pallas_call(functools.partial(bwd_kernel,nh=nh,blk=blk),
      grid=(1,),
      in_specs=[pl.BlockSpec((seq,w),lambda i,j=j:(0,j)) for j in range(3)]+[f((seq,w)),f((w,seq)),f((8,seq))],
      out_specs=f((seq,3*w)),
      out_shape=jax.ShapeDtypeStruct((seq,3*w),jnp.bfloat16),
      scratch_shapes=[pltpu.VMEM((w,seq),jnp.bfloat16),pltpu.VMEM((8,seq),jnp.float32),pltpu.VMEM((w,seq),jnp.float32)],
      compiler_params=pltpu.CompilerParams(vmem_limit_bytes=56<<20),
      name="attn_bwd")(qkv,qkv,qkv,do,ot,lse)


NORM_EPS = 1e-05
F32 = jnp.float32
BF16 = jnp.bfloat16
SWAP = [(0, 1), (1, 0)]
SEQ_AXES = ("y", "c")
DP_AXES = ("z", "x")


def layer_norm(values, gain_vec, shift_vec):
    centred = values - jnp.mean(values, axis=-1, keepdims=True)
    variance = jnp.mean(centred * centred, axis=-1, keepdims=True)
    return centred * lax.rsqrt(variance + NORM_EPS) * gain_vec + shift_vec


def contract_rows(left, right, out=F32):
    return lax.dot_general(
        left, right, (((0,), (0,)), ((), ())), preferred_element_type=F32
    ).astype(out)


def contract_cols(left, right):
    return lax.dot_general(left, right, (((1,), (1,)), ((), ())), preferred_element_type=F32)


def dot_halves(left, halves):
    return jnp.concatenate([jnp.dot(left, halves[i], preferred_element_type=F32) for i in range(2)], axis=1)


def back_halves(left, halves):
    half = halves.shape[2]
    return contract_cols(left[:, :half], halves[0]) + contract_cols(left[:, half:], halves[1])


def norm_backward(values, gain_vec, shift_vec, upstream):
    unused_out, pullback = jax.vjp(layer_norm, values, gain_vec, shift_vec)
    return pullback(upstream)


def column_sums(values):
    return jnp.sum(values.astype(F32), axis=0)


def add_low(a, b):
    return (a.astype(F32) + b.astype(F32)).astype(BF16)


def ring(n):
    return [(i, (i + 1) % n) for i in range(n)]


def gather_pieces(shard, by_core):
    rows, cols = shard.shape
    nz = lax.axis_size("z")
    cur = shard
    if by_core:
        cur = lax.dynamic_slice(shard, (0, lax.axis_index("c") * (cols // 2)), (rows, cols // 2))
    pieces = []
    for step in range(nz):
        if step > 0:
            cur = lax.ppermute(cur, "z", ring(nz))
        pair = [cur, lax.ppermute(cur, "x", SWAP)]
        pieces += pair
    if by_core:
        pieces += [lax.ppermute(piece, "c", SWAP) for piece in pieces]
    return pieces


def owner_of(index, nz, z, x):
    step, side = index // 2 % nz, index % 2
    return lax.rem(z + nz - step, nz) * 2 + (x if side == 0 else 1 - x)


def place_kernel(where_ref, *refs, nz):
    pieces, out, sems = refs[:-2], refs[-2], refs[-1]
    rows, half = pieces[0].shape
    z, x, c = where_ref[0], where_ref[1], where_ref[2]
    copies = []
    for i, piece in enumerate(pieces):
        row = pl.multiple_of(owner_of(i, nz, z, x) * rows, rows)
        side = c if i < 2 * nz else 1 - c
        copies.append(
            pltpu.make_async_copy(piece, out.at[side, pl.ds(row, rows), :], sems.at[i])
        )
    for copy in copies:
        copy.start()
    for copy in copies:
        copy.wait()


def here():
    return jnp.stack([lax.axis_index(a) for a in ("z", "x", "c")]).astype(jnp.int32)


def gather_weight(shard):
    rows, cols = shard.shape
    nz = lax.axis_size("z")
    pieces = gather_pieces(shard, True)
    return pl.pallas_call(
        functools.partial(place_kernel, nz=nz),
        grid_spec=pltpu.PrefetchScalarGridSpec(
            num_scalar_prefetch=1,
            grid=(1,),
            in_specs=[pl.BlockSpec(memory_space=pl.ANY)] * len(pieces),
            out_specs=pl.BlockSpec(memory_space=pltpu.VMEM),
            scratch_shapes=[pltpu.SemaphoreType.DMA((len(pieces),))],
        ),
        compiler_params=pltpu.CompilerParams(vmem_limit_bytes=40 << 20),
        out_shape=jax.ShapeDtypeStruct((2, 2 * nz * rows, cols // 2), BF16),
        name="place",
    )(here(), *pieces)


def gather_small(small, n_vec):
    nz = lax.axis_size("z")
    n, own = small.shape
    pieces = gather_pieces(small, False)
    z, x, unused_c = here()
    order = jnp.stack([owner_of(i, nz, z, x) for i in range(2 * nz)])
    stacked = jnp.stack(pieces).astype(F32)
    pick = (order[None, :] == jnp.arange(2 * nz)[:, None]).astype(F32)
    placed = jnp.einsum("oi,ird->ord", pick, stacked, precision=lax.Precision.HIGHEST)
    return placed


def reduce_grad(grad):
    all_rows, cols = grad.shape
    nz = lax.axis_size("z")
    z, x, c = (lax.axis_index(a) for a in ("z", "x", "c"))
    half = cols // 2
    rows = all_rows // (2 * nz)
    send = lax.dynamic_slice(grad, (0, (1 - c) * half), (all_rows, half))
    keep = lax.dynamic_slice(grad, (0, c * half), (all_rows, half))
    mine = add_low(keep, lax.ppermute(send, "c", SWAP)).reshape(nz, 2, rows, half)
    send = lax.dynamic_slice(mine, (0, 1 - x, 0, 0), (nz, 1, rows, half))[:, 0]
    keep = lax.dynamic_slice(mine, (0, x, 0, 0), (nz, 1, rows, half))[:, 0]
    got = lax.ppermute(send, "x", SWAP)

    def part(i):
        at = (i % nz, 0, 0)
        return add_low(
            lax.dynamic_slice(keep, at, (1, rows, half))[0],
            lax.dynamic_slice(got, at, (1, rows, half))[0],
        )

    cur = part(z - 1)
    for step in range(nz - 1):
        cur = add_low(lax.ppermute(cur, "z", ring(nz)), part(z - 2 - step))
    own = cur.astype(F32) + lax.ppermute(cur, "y", SWAP).astype(F32)
    low = own.astype(BF16)
    other = lax.ppermute(low, "c", SWAP)
    first = jnp.where(c == 0, low, other)
    second = jnp.where(c == 0, other, low)
    return jnp.concatenate((first, second), axis=1).astype(F32)


def reduce_small(grads):
    nz = lax.axis_size("z")
    z, x = lax.axis_index("z"), lax.axis_index("x")
    cur = grads.astype(BF16)
    for axis in ("c", "y"):
        cur = add_low(cur, lax.ppermute(cur, axis, SWAP))
    cur = cur.reshape((nz, 2) + cur.shape[1:])
    keep = lax.dynamic_index_in_dim(cur, x, 1, False)
    keep = add_low(keep, lax.ppermute(lax.dynamic_index_in_dim(cur, 1 - x, 1, False), "x", SWAP))
    cur = lax.dynamic_index_in_dim(keep, (z + nz - 1) % nz, 0, False)
    for step in range(nz - 1):
        own = lax.dynamic_index_in_dim(keep, (z + 2 * nz - 2 - step) % nz, 0, False)
        cur = add_low(lax.ppermute(cur, "z", ring(nz)), own)
    return cur.astype(F32)


def per_device(
    tokens,
    out_grad,
    qkv_weight,
    qv_bias,
    proj_weight,
    fc1_weight,
    fc1_bias,
    fc2_weight,
    out_bias,
    norm_gains,
    norm_shifts,
):
    n_dp = lax.axis_size("z") * lax.axis_size("x")
    n_seq = lax.axis_size("y") * lax.axis_size("c")
    width = tokens.shape[1]
    rows = tokens.shape[0]
    own = qv_bias.shape[1]
    grp = width // n_seq
    heads = grp // HD
    qkv_shard = (
        qkv_weight.reshape(-1, 3, n_seq, grp).transpose(0, 2, 1, 3).reshape(-1, 3 * width)
    )
    small = jnp.concatenate(
        (qv_bias, out_bias, norm_gains, norm_shifts, fc1_bias.reshape(-1, own)), axis=0
    )
    small = gather_small(small, 12)
    vecs = small[:, :12].transpose(1, 0, 2).reshape(12, width)
    qv_b, out_b, gain_rows, shift_rows = vecs[:2], vecs[2:4], vecs[4:8], vecs[8:12]
    fc1_b = small[:, 12:].reshape(-1)
    qkv_w = gather_weight(qkv_shard)
    proj_w = gather_weight(proj_weight)
    fc1_w = gather_weight(fc1_weight)
    fc2_w = gather_weight(fc2_weight)

    tok_vals = tokens.astype(F32)
    normed = layer_norm(tok_vals, gain_rows[0], shift_rows[0]).astype(BF16)
    bias_row = jnp.stack((qv_b[0], jnp.zeros_like(qv_b[0]), qv_b[1])).reshape(3, n_seq, grp)
    bias_row = bias_row.transpose(1, 0, 2).reshape(-1)
    scale = 1.0 / (RELAX * math.sqrt(HD))
    scale_row = jnp.tile(
        jnp.concatenate((jnp.full((grp,), scale, F32), jnp.ones((2 * grp,), F32))), n_seq
    )
    mixed = dot_halves(normed, qkv_w)
    stacked = ((mixed + bias_row) * scale_row).astype(BF16)
    by_heads = lax.all_to_all(stacked, SEQ_AXES, split_axis=1, concat_axis=0, tiled=True)
    out_heads, out_cols, lse = attn_fwd(by_heads, heads, 1024)
    attended = lax.all_to_all(out_heads, SEQ_AXES, split_axis=0, concat_axis=1, tiled=True)
    branch = dot_halves(attended, proj_w) + out_b[0]
    residual = tok_vals + layer_norm(branch, gain_rows[1], shift_rows[1])
    normed_two = layer_norm(residual, gain_rows[2], shift_rows[2]).astype(BF16)
    hidden = dot_halves(normed_two, fc1_w) + fc1_b
    active, gelu_back = jax.vjp(functools.partial(jax.nn.gelu, approximate=True), hidden)
    active = active.astype(BF16)
    second = dot_halves(active, fc2_w) + out_b[1]
    layer_out = residual + layer_norm(second, gain_rows[3], shift_rows[3])

    upstream = out_grad.astype(F32)
    d_second, grad_gain_three, grad_shift_three = norm_backward(
        second, gain_rows[3], shift_rows[3], upstream
    )
    d_second = d_second.astype(BF16)
    total_fc2 = reduce_grad(contract_rows(active, d_second, BF16))
    grad_bias_two = column_sums(d_second)
    d_active = back_halves(d_second, fc2_w)
    d_hidden = gelu_back(d_active)[0].astype(BF16)
    total_fc1 = reduce_grad(contract_rows(normed_two, d_hidden, BF16))
    grad_fc1_bias = column_sums(d_hidden)
    d_normed_two = back_halves(d_hidden, fc1_w)
    d_resid_part, grad_gain_two, grad_shift_two = norm_backward(
        residual, gain_rows[2], shift_rows[2], d_normed_two
    )
    d_residual = upstream + d_resid_part
    d_branch, grad_gain_one, grad_shift_one = norm_backward(
        branch, gain_rows[1], shift_rows[1], d_residual
    )
    d_branch = d_branch.astype(BF16)
    total_proj = reduce_grad(contract_rows(attended, d_branch, BF16))
    grad_bias_one = column_sums(d_branch)
    d_attended = back_halves(d_branch, proj_w).astype(BF16)
    d_heads = lax.all_to_all(d_attended, SEQ_AXES, split_axis=1, concat_axis=0, tiled=True)
    d_by_heads = attn_bwd(by_heads, d_heads, out_cols, lse, heads, 512)
    d_mixed = lax.all_to_all(d_by_heads, SEQ_AXES, split_axis=0, concat_axis=1, tiled=True)
    grad_qkv = contract_rows(normed, d_mixed, BF16)
    mixed_sums = column_sums(d_mixed).reshape(n_seq, 3, grp).transpose(1, 0, 2).reshape(3, width)
    d_normed = back_halves(d_mixed, qkv_w)
    d_tok_part, grad_gain_zero, grad_shift_zero = norm_backward(
        tok_vals, gain_rows[0], shift_rows[0], d_normed
    )
    tokens_grad = (d_residual + d_tok_part).astype(BF16)
    vec_grads = jnp.stack(
        (
            mixed_sums[0],
            mixed_sums[2],
            grad_bias_one,
            grad_bias_two,
            grad_gain_zero,
            grad_gain_one,
            grad_gain_two,
            grad_gain_three,
            grad_shift_zero,
            grad_shift_one,
            grad_shift_two,
            grad_shift_three,
        )
    )
    small_grads = jnp.concatenate(
        (
            vec_grads.reshape(12, n_dp, own).transpose(1, 0, 2),
            grad_fc1_bias.reshape(n_dp, -1, own),
        ),
        axis=1,
    )
    n_small = small_grads.shape[1]
    total_qkv = reduce_grad(grad_qkv)
    total_small = reduce_small(small_grads)
    total_qkv = total_qkv.reshape(-1, n_seq, 3, grp).transpose(0, 2, 1, 3).reshape(-1, 3 * width)
    return (
        layer_out.astype(BF16),
        tokens_grad,
        total_qkv,
        total_small[0:2],
        total_proj,
        total_fc1,
        total_small[12:n_small].reshape(-1),
        total_fc2,
        total_small[2:4],
        total_small[4:8],
        total_small[8:12],
    )


def solution(mesh):
    n_dp, n_seq = mesh.devices.shape
    fine = Mesh(mesh.devices.reshape(n_dp // 2, 2, n_seq // 2, 2), DP_AXES + SEQ_AXES)
    tok = P(DP_AXES + SEQ_AXES, None)
    by_row = P(DP_AXES, None)
    by_col = P(None, DP_AXES)
    weights = (by_row, by_col, by_row, by_row, P(DP_AXES), by_row, by_col, by_col, by_col)
    return jax.shard_map(
        per_device,
        mesh=fine,
        in_specs=(tok, tok) + weights,
        out_specs=(tok, tok) + weights,
        check_vma=False,
    )
```

```python
import functools
import math

import jax
import jax.numpy as jnp
from jax.sharding import Mesh
from jax.sharding import PartitionSpec as P
from jax import lax
from jax.experimental import pallas as pl
from jax.experimental.pallas import tpu as pltpu
HD=64
RELAX=32.0
C2=RELAX*math.log2(math.e)
NEG=-1e30

def _nt(a,b):
    return lax.dot_general(a,b,(((1,),(1,)),((),())),preferred_element_type=jnp.float32)
def _nn(a,b):
    return lax.dot_general(a,b,(((1,),(0,)),((),())),preferred_element_type=jnp.float32)

def _tr(x):
    return jnp.transpose(x.astype(jnp.float32)).astype(jnp.bfloat16)

def by_source(where, refs, dst, sems):
    rows = refs[0].shape[0]
    copies = []
    for i, ref in enumerate(refs):
        at = pl.multiple_of(jnp.bitwise_xor(where[3], i) * rows, rows)
        copies.append(pltpu.make_async_copy(ref, dst.at[pl.ds(at, rows), :], sems.at[i]))
    return copies

def by_target(where, src, refs, sems):
    rows = refs[0].shape[0]
    copies = []
    for i, ref in enumerate(refs):
        at = pl.multiple_of(jnp.bitwise_xor(where[3], i) * rows, rows)
        copies.append(pltpu.make_async_copy(src.at[pl.ds(at, rows), :], ref, sems.at[i]))
    return copies

def run_copies(copies):
    for copy in copies:
        copy.start()
    for copy in copies:
        copy.wait()

def fwd_kernel(where,*refs,nh,blk,n):
    ins,outs=refs[:n],refs[n:2*n]
    ot_ref,lse_ref,vt_ref,qkv_ref,o_ref,sems=refs[2*n:]
    seq=qkv_ref.shape[0]; w=nh*HD
    nb=seq//blk
    run_copies(by_source(where,ins,qkv_ref,sems))
    q_ref,k_ref,v_ref=(qkv_ref.at[:,i*w:(i+1)*w] for i in range(3))
    for b in range(nb):
        vt_ref[:,b*blk:(b+1)*blk]=_tr(v_ref[b*blk:(b+1)*blk,:])
    lane=lax.broadcasted_iota(jnp.int32,(1,w),1)//HD
    tri=lax.broadcasted_iota(jnp.int32,(blk,blk),0)<=lax.broadcasted_iota(jnp.int32,(blk,blk),1)
    def qstep(qb,_):
        q0=pl.multiple_of(qb*blk,blk)
        q=q_ref[pl.ds(q0,blk),:]
        qm=[jnp.where(lane==h,q,jnp.zeros_like(q)) for h in range(nh)]
        def kv(kb,carry,diag):
            k0=pl.multiple_of(kb*blk,blk)
            k=k_ref[pl.ds(k0,blk),:]
            out=[]
            for h in range(nh):
                m,l,acc=carry[3*h:3*h+3]
                s=_nt(k,qm[h])*C2
                if diag: s=jnp.where(tri,s,NEG)
                mn=jnp.maximum(m,jnp.max(s,axis=0,keepdims=True))
                a=jnp.exp2(m-mn)
                p=jnp.exp2(s-mn)
                l=l*a+jnp.sum(p,axis=0,keepdims=True)
                acc=acc*a+_nn(vt_ref[h*HD:(h+1)*HD,pl.ds(k0,blk)],p.astype(jnp.bfloat16))
                out+= [mn,l,acc]
            return tuple(out)
        init=[]
        for h in range(nh):
            init+=[jnp.full((1,blk),NEG,jnp.float32),jnp.zeros((1,blk),jnp.float32),jnp.zeros((HD,blk),jnp.float32)]
        c=kv(qb,tuple(init),True)
        c=lax.fori_loop(0,qb,lambda kb,cc: kv(kb,cc,False),c)
        for h in range(nh):
            m,l,acc=c[3*h:3*h+3]
            ot_ref[h*HD:(h+1)*HD,pl.ds(q0,blk)]=acc/l
            lse_ref[h:h+1,pl.ds(q0,blk)]=m+jnp.log2(l)
        o_ref[pl.ds(q0,blk),:]=jnp.transpose(ot_ref[:,pl.ds(q0,blk)]).astype(jnp.bfloat16)
        return 0
    lax.fori_loop(0,nb,qstep,0)
    run_copies(by_target(where,o_ref,outs,sems))

def attn_fwd(where, qkv, nh, blk=512):
    n=len(qkv); rows=qkv[0].shape[0]
    seq=n*rows; w=nh*HD
    blk=min(blk,seq)
    vm=pl.BlockSpec(memory_space=pltpu.VMEM)
    an=pl.BlockSpec(memory_space=pl.ANY)
    outs=pl.pallas_call(functools.partial(fwd_kernel,nh=nh,blk=blk,n=n),
      grid_spec=pltpu.PrefetchScalarGridSpec(num_scalar_prefetch=1,
        in_specs=[an]*n,out_specs=[an]*n+[vm]*2,
        scratch_shapes=[pltpu.VMEM((w,seq),jnp.bfloat16),pltpu.VMEM((seq,3*w),jnp.bfloat16),pltpu.VMEM((seq,w),jnp.bfloat16),pltpu.SemaphoreType.DMA((n,))]),
      out_shape=[jax.ShapeDtypeStruct((rows,w),jnp.bfloat16)]*n+[jax.ShapeDtypeStruct((w,seq),jnp.float32),jax.ShapeDtypeStruct((8,seq),jnp.float32)],
      compiler_params=pltpu.CompilerParams(vmem_limit_bytes=48<<20),
      cost_estimate=pl.CostEstimate(flops=int(nh*4.5*1.1e9), transcendentals=0, bytes_accessed=1<<20),
      name="attn_fwd")(where,*qkv)
    return outs[:n],outs[n],outs[n+1]

def bwd_kernel(where,*refs,nh,blk,n):
    ins,dos,outs=refs[:n],refs[n:2*n],refs[2*n+2:3*n+2]
    ot_ref,lse_ref=refs[2*n:2*n+2]
    kt_ref,dl_ref,dqt_ref,qkv_ref,do_ref,d_ref,sems,do_sems=refs[3*n+2:]
    seq=qkv_ref.shape[0]; w=nh*HD
    nb=seq//blk
    run_copies(by_source(where,ins,qkv_ref,sems)+by_source(where,dos,do_ref,do_sems))
    q_ref,k_ref,v_ref=(qkv_ref.at[:,i*w:(i+1)*w] for i in range(3))
    for b in range(nb):
        sl=slice(b*blk,(b+1)*blk)
        kt_ref[:,sl]=_tr(k_ref[sl,:])
        dot_=jnp.transpose(do_ref[sl,:].astype(jnp.float32))
        pr=dot_*ot_ref[:,sl]
        for h in range(nh):
            dl_ref[h:h+1,sl]=jnp.sum(pr[h*HD:(h+1)*HD],axis=0,keepdims=True)
    dqt_ref[...]=jnp.zeros_like(dqt_ref)
    lane=lax.broadcasted_iota(jnp.int32,(1,w),1)//HD
    tri=lax.broadcasted_iota(jnp.int32,(blk,blk),0)<=lax.broadcasted_iota(jnp.int32,(blk,blk),1)
    def kstep(kb,_):
        k0=pl.multiple_of(kb*blk,blk)
        k=k_ref[pl.ds(k0,blk),:]
        v=v_ref[pl.ds(k0,blk),:]
        def qs(qb,carry,diag):
            dk,dv=carry
            q0=pl.multiple_of(qb*blk,blk)
            q=q_ref[pl.ds(q0,blk),:]
            do=do_ref[pl.ds(q0,blk),:]
            for h in range(nh):
                qm=jnp.where(lane==h,q,jnp.zeros_like(q))
                dom=jnp.where(lane==h,do,jnp.zeros_like(do))
                s=_nt(k,qm)
                dp=_nt(v,dom)
                p=jnp.exp2(s*C2-lse_ref[h:h+1,pl.ds(q0,blk)])
                if diag: p=jnp.where(tri,p,0.0)
                ds=(p*(dp-dl_ref[h:h+1,pl.ds(q0,blk)])).astype(jnp.bfloat16)
                dv=dv+_nn(p.astype(jnp.bfloat16),dom)
                dk=dk+_nn(ds,qm)
                dqt_ref[h*HD:(h+1)*HD,pl.ds(q0,blk)]+=_nn(kt_ref[h*HD:(h+1)*HD,pl.ds(k0,blk)],ds)
            return dk,dv
        z=jnp.zeros((blk,w),jnp.float32)
        c=qs(kb,(z,z),True)
        dk,dv=lax.fori_loop(kb+1,nb,lambda qb,cc: qs(qb,cc,False),c)
        d_ref[pl.ds(k0,blk),w:2*w]=(dk*RELAX).astype(jnp.bfloat16)
        d_ref[pl.ds(k0,blk),2*w:3*w]=dv.astype(jnp.bfloat16)
        return 0
    lax.fori_loop(0,nb,kstep,0)
    for b in range(nb):
        sl=slice(b*blk,(b+1)*blk)
        d_ref[sl,0:w]=(jnp.transpose(dqt_ref[:,sl])*(1.0/math.sqrt(HD))).astype(jnp.bfloat16)
    run_copies(by_target(where,d_ref,outs,sems))

def attn_bwd(where, qkv, do, ot, lse, nh, blk=512):
    n=len(qkv); rows=qkv[0].shape[0]
    seq=n*rows; w=nh*HD
    blk=min(blk,seq)
    vm=pl.BlockSpec(memory_space=pltpu.VMEM)
    an=pl.BlockSpec(memory_space=pl.ANY)
    return pl.pallas_call(functools.partial(bwd_kernel,nh=nh,blk=blk,n=n),
      grid_spec=pltpu.PrefetchScalarGridSpec(num_scalar_prefetch=1,
        in_specs=[an]*(2*n)+[vm]*2,out_specs=[an]*n,
        scratch_shapes=[pltpu.VMEM((w,seq),jnp.bfloat16),pltpu.VMEM((8,seq),jnp.float32),pltpu.VMEM((w,seq),jnp.float32),
          pltpu.VMEM((seq,3*w),jnp.bfloat16),pltpu.VMEM((seq,w),jnp.bfloat16),pltpu.VMEM((seq,3*w),jnp.bfloat16),
          pltpu.SemaphoreType.DMA((n,)),pltpu.SemaphoreType.DMA((n,))]),
      out_shape=[jax.ShapeDtypeStruct((rows,3*w),jnp.bfloat16)]*n,
      compiler_params=pltpu.CompilerParams(vmem_limit_bytes=56<<20),
      cost_estimate=pl.CostEstimate(flops=int(nh*9.5*1.1e9), transcendentals=0, bytes_accessed=1<<20),
      name="attn_bwd")(where,*qkv,*do,ot,lse)


NORM_EPS = 1e-05
F32 = jnp.float32
BF16 = jnp.bfloat16
SWAP = [(0, 1), (1, 0)]
SEQ_AXES = ("y", "c")
DP_AXES = ("z", "x")
ANY = pl.BlockSpec(memory_space=pl.ANY)
VMEM = pl.BlockSpec(memory_space=pltpu.VMEM)
GELU_K = math.sqrt(2.0 / math.pi)
GELU_A = 0.044715
N_VEC = 12
N_SEQ = 4


def add_low(*terms):
    return sum(t.astype(F32) for t in terms).astype(BF16)


def ring(n):
    return [(i, (i + 1) % n) for i in range(n)]


def uses_rings():
    return lax.axis_size("z") * lax.axis_size("x") <= 8


def here():
    seq = lax.axis_index("y") * lax.axis_size("c") + lax.axis_index("c")
    return jnp.stack([lax.axis_index(a) for a in ("z", "x", "c")] + [seq]).astype(jnp.int32)


def call(kernel, name, where, args, specs, outs, scratch=(), grid=(), out_specs=None, cost=None):
    if out_specs is None:
        out_specs = [VMEM] * len(outs)
    return pl.pallas_call(
        kernel,
        grid_spec=pltpu.PrefetchScalarGridSpec(
            num_scalar_prefetch=1,
            grid=grid,
            in_specs=specs,
            out_specs=out_specs,
            scratch_shapes=list(scratch),
        ),
        out_shape=[jax.ShapeDtypeStruct(s, d) for s, d in outs],
        compiler_params=pltpu.CompilerParams(vmem_limit_bytes=60 << 20),
        cost_estimate=cost,
        name=name,
    )(where, *args)


def cost_of(microseconds):
    return pl.CostEstimate(flops=int(microseconds * 1.1e9), transcendentals=0, bytes_accessed=1 << 20)


def tie(value, *others):
    return lax.optimization_barrier((value,) + others)[0]


def together(*values):
    return list(lax.optimization_barrier(tuple(values)))


class Gather:
    def __init__(self, shards, core_halves=True):
        self.shards = shards
        self.core_halves = core_halves
        self.cur = shards
        if core_halves:
            self.cur = lax.dynamic_index_in_dim(shards, lax.axis_index("c"), 0, False)
        self.mine = []
        self.hops = 0

    def hop(self, *after):
        nz = lax.axis_size("z")
        if self.hops > 0:
            after = after + (self.mine[2 * self.hops - 2],)
        cur = tie(self.cur, *after) if after else self.cur
        if self.hops < nz - 1:
            self.cur = lax.ppermute(cur, "z", ring(nz))
        other = lax.ppermute(cur, "x", SWAP)
        self.mine.append(other)
        self.hops += 1
        if self.hops < nz:
            self.mine.append(self.cur)

    def arrive(self, value):
        value, self.cur, self.mine[-1], self.mine[2 * self.hops - 2] = together(
            value, self.cur, self.mine[-1], self.mine[2 * self.hops - 2]
        )
        return value

    def pieces(self):
        if not self.core_halves:
            return [self.shards] + self.mine
        return [self.shards] + self.mine + [lax.ppermute(piece, "c", SWAP) for piece in self.mine]


def in_halves(weight):
    rows, cols = weight.shape
    return weight.reshape(rows, 2, cols // 2).transpose(1, 0, 2)


def owner_of(index, nz, z, x):
    step, side = (index + 1) // 2, (index + 1) % 2
    return lax.rem(z + nz - step, nz) * 2 + (x if side == 0 else 1 - x)


class Loader:
    def __init__(self, where, pieces, dsts, sems, nz, first=0, col=0):
        self.copies = []
        self.sems, self.first = sems, first
        if not isinstance(dsts, (list, tuple)):
            dsts = [dsts]
        if len(pieces) == len(dsts) and len(pieces[0].shape) == 2:
            for piece, dst in zip(pieces, dsts):
                half = dst.shape[2]
                for side in range(2):
                    at = side * (piece.shape[1] // 2) + col
                    self.add(piece.at[:, at : at + half], dst.at[side])
            return
        z, x, c = where[0], where[1], where[2]
        rows = pieces[0].shape[1]
        others = (len(pieces) - 1) // 2
        self.marks = []
        for dst in dsts:
            half = dst.shape[2]
            groups = dst.shape[1] // (2 * nz * rows)
            for g in range(groups):
                cols = slice(col, col + half)
                col += half

                def to(side, owner):
                    row = pl.multiple_of((owner * groups + g) * rows, rows)
                    return dst.at[side, pl.ds(row, rows), :]

                for side in range(2):
                    self.add(pieces[0].at[side, :, cols], to(side, z * 2 + x))
                for i, piece in enumerate(pieces[1:]):
                    side = c if i < others else 1 - c
                    self.add(piece.at[:, cols], to(side, owner_of(i % others, nz, z, x)))
            self.marks.append(len(self.copies))

    def add(self, src, to):
        self.copies.append(
            pltpu.make_async_copy(src, to, self.sems.at[self.first + len(self.copies)])
        )

    def start(self):
        for copy in self.copies:
            copy.start()

    def wait(self, upto=None, since=0):
        for copy in self.copies[since:upto]:
            copy.wait()


def n_copies(pieces, groups=1):
    return (len(pieces) + 1) * groups


def norm_parts(v):
    c = v - jnp.mean(v, axis=-1, keepdims=True)
    inv = lax.rsqrt(jnp.mean(c * c, axis=-1, keepdims=True) + NORM_EPS)
    return c * inv, inv


def norm_back(n, inv, gain, e):
    ge = g_e = gain * e
    return (g_e - jnp.mean(ge, axis=-1, keepdims=True) - n * jnp.mean(ge * n, axis=-1, keepdims=True)) * inv


def rowsum(v):
    return jnp.sum(v, axis=0, keepdims=True)


def vectors_kernel(where, *refs, nz):
    pieces, vec, bias = refs[:-2], refs[-2], refs[-1]
    z, x = where[0], where[1]
    n_bias = pieces[0].shape[0] - N_VEC
    own = pieces[0].shape[1]
    order = [z * 2 + x] + [owner_of(i, nz, z, x) for i in range(2 * nz - 1)]
    tmp = refs[-2]
    for o in range(2 * nz):
        acc = jnp.zeros(pieces[0].shape, F32)
        for at, piece in zip(order, pieces):
            acc = jnp.where(at == o, piece[...].astype(F32), acc)
        vec[0:N_VEC, o * own : (o + 1) * own] = acc[:N_VEC]
        for j in range(n_bias):
            lo = (o * n_bias + j) * own
            bias[0:1, lo : lo + own] = acc[N_VEC + j : N_VEC + j + 1]


def small_vectors(pieces, width):
    nz = lax.axis_size("z")
    n, own = pieces[0].shape
    return call(
        functools.partial(vectors_kernel, nz=nz),
        "vectors",
        here(),
        pieces,
        [VMEM] * len(pieces),
        [((16, width), F32), ((1, (n - N_VEC) * 2 * nz * own), F32)],
        cost=cost_of(2),
    )


def plain_vectors(small, width):
    placed = lax.all_gather(small, DP_AXES, axis=0, tiled=False).astype(F32)
    vec = placed[:, :N_VEC].transpose(1, 0, 2).reshape(N_VEC, width)
    return jnp.pad(vec, ((0, 4), (0, 0))), placed[:, N_VEC:].reshape(1, -1)


def first_norm(tok, vec, normed):
    rows = min(64, tok.shape[0])

    def body(i, carry):
        at = pl.ds(pl.multiple_of(i * rows, rows), rows)
        n, inv = norm_parts(tok[at, :].astype(F32))
        normed[at, :] = (n * vec[4:5, :] + vec[8:9, :]).astype(BF16)
        return carry

    lax.fori_loop(0, tok.shape[0] // rows, body, 0)


def qkv_kernel(where, first, vec, *refs, nz, chunk, chunks, n_pieces):
    pieces, refs = refs[:n_pieces], list(refs[n_pieces:])
    n_seq = N_SEQ
    outs = [refs.pop(0) for _ in range(n_seq)]
    normed = refs.pop(0) if chunk == 0 else first
    w, stage, sems, out_sems = refs
    rows, cols = outs[0].shape
    per_side = n_seq // 2
    load = Loader(where, pieces, w, sems, nz, 0, chunk * per_side * cols)
    load.start()
    if chunk == 0:
        first_norm(first, vec, normed)
    load.wait()
    wide = cols // 3
    grp = wide * chunks
    scale = 1.0 / (RELAX * math.sqrt(HD))
    for side in range(2):
        mixed = _nn(normed[...], w[side])
        for j in range(per_side):
            s = side * per_side + j
            lo = s * grp + chunk * wide
            block = mixed[:, j * cols : (j + 1) * cols]
            at = slice(s * rows, (s + 1) * rows)
            stage[at, 0:wide] = ((block[:, 0:wide] + vec[0:1, lo : lo + wide]) * scale).astype(BF16)
            stage[at, wide : 2 * wide] = block[:, wide : 2 * wide].astype(BF16)
            stage[at, 2 * wide :] = (block[:, 2 * wide :] + vec[1:2, lo : lo + wide]).astype(BF16)
    run_copies(by_target(where, stage, outs, out_sems))


def gelu_parts(h):
    t = jnp.tanh(GELU_K * (h + GELU_A * (h * h * h)))
    return t


def mlp_kernel(where, *refs, nz, n_att, n_pieces):
    refs = list(refs)
    att_in = [[refs.pop(0) for _ in range(N_SEQ)] for _ in range(n_att)]
    tok, out_grad, vec, fc1_b = [refs.pop(0) for _ in range(4)]
    sets = [[refs.pop(0) for _ in range(n)] for n in n_pieces]
    layer_out, d_residual, d_second, active, d_hidden, normed_two, d_branch, attended, sums, fc1_sum = [
        refs.pop(0) for _ in range(10)
    ]
    d_att = [[refs.pop(0) for _ in range(N_SEQ)] for _ in range(n_att)]
    proj_w, fc1_w, fc2_w, hidden, branch, residual, wide = [refs.pop(0) for _ in range(7)]
    stages = [refs.pop(0) for _ in range(n_att)]
    out_sems = refs.pop(0)
    sems = refs
    dsts = (proj_w, fc1_w, fc2_w)
    if len(sets) == 2:
        ups = Loader(where, sets[0], dsts[:2], sems[0], nz)
        downs = Loader(where, sets[1], dsts[2:], sems[1], nz)
        ups.start()
        downs.start()
        mark = ups.marks[0]
        waits = [functools.partial(ups.wait, mark), functools.partial(ups.wait, None, mark), downs.wait]
    else:
        loads = [Loader(where, p, d, sem, nz) for p, d, sem in zip(sets, dsts, sems)]
        for load in loads:
            load.start()
        waits = [load.wait for load in loads]
    rows, width = tok.shape
    n_seq, part = N_SEQ, att_in[0][0].shape[1]
    for i in range(n_seq):
        s = jnp.bitwise_xor(where[3], i)
        for j in range(n_att):
            lo = pl.multiple_of((s * n_att + j) * part, part)
            attended[:, pl.ds(lo, part)] = att_in[j][i][...]
    waits[0]()
    half = width // 2
    for side in range(2):
        cols = slice(side * half, (side + 1) * half)
        branch[:, cols] = _nn(attended[...], proj_w[side]) + vec[2:3, cols]
    step = min(64, rows)

    def norms(i, carry):
        at = pl.ds(pl.multiple_of(i * step, step), step)
        n, inv = norm_parts(branch[at, :])
        r = tok[at, :].astype(F32) + (n * vec[5:6, :] + vec[9:10, :])
        residual[at, :] = r
        n, inv = norm_parts(r)
        normed_two[at, :] = (n * vec[6:7, :] + vec[10:11, :]).astype(BF16)
        return carry

    lax.fori_loop(0, rows // step, norms, 0)
    waits[1]()
    ff = hidden.shape[1]
    blk = 512
    per_side = ff // 2 // blk

    def up(i, carry):
        lo = pl.multiple_of(i * blk, blk)
        col = pl.multiple_of(lax.rem(i, per_side) * blk, blk)
        h = _nn(normed_two[...], fc1_w[i // per_side, :, pl.ds(col, blk)]) + fc1_b[:, pl.ds(lo, blk)]
        hidden[:, pl.ds(lo, blk)] = h
        active[:, pl.ds(lo, blk)] = (0.5 * h * (1.0 + gelu_parts(h))).astype(BF16)
        return carry

    lax.fori_loop(0, ff // blk, up, 0)
    waits[2]()
    for side in range(2):
        cols = slice(side * half, (side + 1) * half)
        wide[:, cols] = _nn(active[...], fc2_w[side]) + vec[3:4, cols]

    def top(i, carry):
        g_sum, s_sum, b_sum = carry
        at = pl.ds(pl.multiple_of(i * step, step), step)
        n, inv = norm_parts(wide[at, :])
        e = out_grad[at, :].astype(F32)
        layer_out[at, :] = (residual[at, :] + (n * vec[7:8, :] + vec[11:12, :])).astype(BF16)
        d = norm_back(n, inv, vec[7:8, :], e).astype(BF16)
        d_second[at, :] = d
        return g_sum + rowsum(e * n), s_sum + rowsum(e), b_sum + rowsum(d.astype(F32))

    zero = jnp.zeros((1, width), F32)
    g_sum, s_sum, b_sum = lax.fori_loop(0, rows // step, top, (zero, zero, zero))
    sums[3:4, :] = b_sum
    sums[7:8, :] = g_sum
    sums[11:12, :] = s_sum

    def down(i, carry):
        at = pl.ds(pl.multiple_of(i * blk, blk), blk)
        d = _nt(d_second[:, 0:half], fc2_w[0, at, :]) + _nt(d_second[:, half:], fc2_w[1, at, :])
        h = hidden[:, at]
        t = gelu_parts(h)
        slope = 0.5 * (1.0 + t) + (0.5 * h) * (1.0 - t * t) * (GELU_K * (1.0 + 3.0 * GELU_A * (h * h)))
        low = (d * slope).astype(BF16)
        d_hidden[:, at] = low
        fc1_sum[:, at] = rowsum(low.astype(F32))
        return carry

    lax.fori_loop(0, ff // blk, down, 0)
    quarter = width // 4
    for q in range(4):
        at = slice(q * quarter, (q + 1) * quarter)
        wide[:, at] = _nt(d_hidden[:, 0 : ff // 2], fc1_w[0, at, :]) + _nt(
            d_hidden[:, ff // 2 :], fc1_w[1, at, :]
        )

    def mid(i, carry):
        g2, s2, g1, s1, b_sum = carry
        at = pl.ds(pl.multiple_of(i * step, step), step)
        e = wide[at, :]
        n, inv = norm_parts(residual[at, :])
        d = out_grad[at, :].astype(F32) + norm_back(n, inv, vec[6:7, :], e)
        d_residual[at, :] = d
        g2, s2 = g2 + rowsum(e * n), s2 + rowsum(e)
        n, inv = norm_parts(branch[at, :])
        low = norm_back(n, inv, vec[5:6, :], d).astype(BF16)
        d_branch[at, :] = low
        return g2, s2, g1 + rowsum(d * n), s1 + rowsum(d), b_sum + rowsum(low.astype(F32))

    g2, s2, g1, s1, b_sum = lax.fori_loop(0, rows // step, mid, (zero,) * 5)
    for row, v in ((6, g2), (10, s2), (5, g1), (9, s1), (2, b_sum)):
        sums[row : row + 1, :] = v
    for row in (0, 1, 4, 8, 12, 13, 14, 15):
        sums[row : row + 1, :] = zero
    for s in range(n_seq):
        at = slice(s * n_att * part, (s + 1) * n_att * part)
        low = (_nt(d_branch[:, 0:half], proj_w[0, at, :]) + _nt(d_branch[:, half:], proj_w[1, at, :])).astype(BF16)
        for j in range(n_att):
            stages[j][s * rows : (s + 1) * rows, :] = low[:, j * part : (j + 1) * part]
    run_copies(
        [
            copy
            for j in range(n_att)
            for copy in by_target(where, stages[j], d_att[j], out_sems.at[j])
        ]
    )


def mlp(where, att, tokens, out_grad, vec, fc1_b, sets):
    nz = lax.axis_size("z")
    rows, width = tokens.shape
    ff = fc1_b.shape[1]
    n_pieces = [len(s) for s in sets]
    flat = [block for blocks in att for block in blocks]
    part = flat[0].shape[1]
    big = (rows, width)
    outs = [
        (big, BF16),
        (big, F32),
        (big, BF16),
        ((rows, ff), BF16),
        ((rows, ff), BF16),
        (big, BF16),
        (big, BF16),
        (big, BF16),
        ((16, width), F32),
        ((1, ff), F32),
    ] + [(a.shape, BF16) for a in flat]
    scratch = [
        pltpu.VMEM((2, width, width // 2), BF16),
        pltpu.VMEM((2, width, ff // 2), BF16),
        pltpu.VMEM((2, ff, width // 2), BF16),
        pltpu.VMEM((rows, ff), F32),
        pltpu.VMEM(big, F32),
        pltpu.VMEM(big, F32),
        pltpu.VMEM(big, F32),
    ] + [pltpu.VMEM((N_SEQ * rows, part), BF16)] * len(att)
    scratch += [pltpu.SemaphoreType.DMA((len(att), N_SEQ))]
    scratch += [pltpu.SemaphoreType.DMA((n_copies(s, max(2, ff // width)),)) for s in sets]
    args = flat + [tokens, out_grad, vec, fc1_b] + [p for s in sets for p in s]
    specs = [VMEM] * (len(flat) + 4) + [ANY] * sum(n_pieces)
    out_specs = [VMEM] * 10 + [ANY] * len(flat)
    return call(
        functools.partial(mlp_kernel, nz=nz, n_att=len(att), n_pieces=n_pieces),
        "mlp",
        where,
        args,
        specs,
        outs,
        scratch,
        out_specs=out_specs,
        cost=cost_of(45),
    )


def slot_owner(i, nz, where):
    z, x = where[0], where[1]
    return lax.rem(z + 2 * nz - 1 - i % nz, nz) * 2 + (1 - x if i < nz else x)


def contract_rows(left, right):
    return lax.dot_general(left, right, (((0,), (0,)), ((), ())), preferred_element_type=F32)


def halves_of(ref, c):
    half = ref.shape[1] // 2
    return [ref[:, pl.ds(pl.multiple_of(h * half, half), half)] for h in (1 - c, c)]


def columns_of(ref, owner, count):
    return ref[:, pl.ds(pl.multiple_of(owner * count, count), count)]


def up_grad_kernel(where, normed_two, d_hidden, attended, d_branch, *outs, nz):
    c = where[2]
    rows = outs[0].shape[1]
    half = d_branch.shape[1] // 2
    ff_half = d_hidden.shape[1] // 2
    blk = min(1024, ff_half)
    for side in range(2):
        owners = [slot_owner(side * nz + i, nz, where) for i in range(nz)]
        left = jnp.concatenate([columns_of(normed_two, o, rows) for o in owners], axis=1)
        for h in range(2):
            out = outs[2 * side + h]
            base = (1 - c if h == 0 else c) * ff_half
            for n in range(ff_half // blk):
                right = d_hidden[:, pl.ds(pl.multiple_of(base + n * blk, blk), blk)]
                low = contract_rows(left, right).astype(BF16)
                for i in range(nz):
                    out[i, :, half + n * blk : half + (n + 1) * blk] = low[i * rows : (i + 1) * rows]
        left = jnp.concatenate([columns_of(attended, o, rows) for o in owners], axis=1)
        for h, right in enumerate(halves_of(d_branch, c)):
            out = outs[2 * side + h]
            low = contract_rows(left, right).astype(BF16)
            for i in range(nz):
                out[i, :, 0:half] = low[i * rows : (i + 1) * rows]


def down_grad_kernel(where, active, d_second, *outs, nz):
    c = where[2]
    rows = outs[0].shape[1]
    wide = active.shape[1] // (2 * nz)
    half = d_second.shape[1] // 2
    rights = halves_of(d_second, c)
    for side in range(2):
        for i in range(nz):
            left = columns_of(active, slot_owner(side * nz + i, nz, where), wide)
            for h, right in enumerate(rights):
                low = contract_rows(left, right).astype(BF16)
                for g in range(wide // rows):
                    outs[2 * side + h][i, :, g * half : (g + 1) * half] = low[g * rows : (g + 1) * rows]


def grads(kernel, name, where, args, rows, half, specs=None, scratch=(), parts=2, after=()):
    nz = lax.axis_size("z")
    outs = call(
        functools.partial(kernel, nz=nz),
        name,
        where,
        args,
        specs or [VMEM] * len(args),
        [((nz, rows, half), BF16)] * 4,
        scratch,
        cost=cost_of(10),
    )
    outs = list(outs)
    if after:
        outs[0] = tie(outs[0], *after)
    return Reduce(outs[:2], outs[2:], parts)


def qkv_grad_kernel(where, normed, *refs, nz):
    blocks, outs, (stage, sems) = refs[:N_SEQ], refs[N_SEQ:-2], refs[-2:]
    c = where[2]
    rows = outs[0].shape[1]
    tok = normed.shape[0]
    per_side = N_SEQ // 2
    run_copies(by_source(where, blocks, stage, sems))
    for h in range(2):
        base = (1 - c if h == 0 else c) * per_side
        right = jnp.concatenate(
            [stage[pl.ds(pl.multiple_of((base + j) * tok, tok), tok), :] for j in range(per_side)], axis=1
        )
        for side in range(2):
            owners = [slot_owner(side * nz + i, nz, where) for i in range(nz)]
            left = jnp.concatenate([columns_of(normed, o, rows) for o in owners], axis=1)
            low = contract_rows(left, right).astype(BF16)
            for i in range(nz):
                outs[2 * side + h][i] = low[i * rows : (i + 1) * rows]


class Reduce:
    def __init__(self, first, second, parts=2):
        self.own = second[1]
        self.own_got = lax.ppermute(second[0], "c", SWAP)
        got = lax.ppermute(first[0], "c", SWAP)
        size = got.shape[0] // parts
        cuts = [slice(i * size, (i + 1) * size) for i in range(parts)]
        self.size = size
        self.out = [add_low(first[1][cut], got[cut]) for cut in cuts]
        self.from_x = []

    def cross(self, *after):
        block = self.out[len(self.from_x)]
        self.from_x.append(lax.ppermute(tie(block, *after) if after else block, "x", SWAP))
        return self.from_x[-1]

    def add(self, step):
        terms = (self.own[step], self.own_got[step], self.from_x[step // self.size][step % self.size])
        if step > 0:
            terms = (self.passed,) + terms
        self.cur = add_low(*terms)
        return self.cur

    def ring(self, *after):
        nz = lax.axis_size("z")
        self.passed = lax.ppermute(tie(self.cur, *after) if after else self.cur, "z", ring(nz))
        return self.passed

    def finish(self):
        c = lax.axis_index("c")
        low = add_low(self.cur, lax.ppermute(self.cur, "y", SWAP))
        other = lax.ppermute(low, "c", SWAP)
        return jnp.where(c == 0, low, other), jnp.where(c == 0, other, low)


def reduce_plain(lhs, rhs):
    grad = lax.dot_general(
        lhs, rhs, (((0,), (0,)), ((), ())), preferred_element_type=F32
    ).astype(BF16)
    part = lax.psum_scatter(grad, DP_AXES, scatter_dimension=0, tiled=True)
    return lax.psum(part, SEQ_AXES).astype(F32)


def last_kernel(where, *refs, nz, chunks, n_pieces, rings):
    refs = list(refs)
    blocks = [[refs.pop(0) for _ in range(N_SEQ)] for _ in range(chunks)]
    tok, d_residual, vec, sums, fc1_sum = [refs.pop(0) for _ in range(5)]
    pieces = [refs.pop(0) for _ in range(n_pieces)]
    tokens_grad, small = refs.pop(0), refs.pop(0)
    ws = [refs.pop(0) for _ in range(chunks)]
    stages = [refs.pop(0) for _ in range(chunks)]
    wide, total, in_sems = refs.pop(0), refs.pop(0), refs.pop(0)
    loads = [
        Loader(where, pieces, w, sem, nz, 0, j * w.shape[2]) for j, (w, sem) in enumerate(zip(ws, refs))
    ]
    for load in loads:
        load.start()
    rows, width = tok.shape
    n_seq, cols = N_SEQ, stages[0].shape[1]
    run_copies(
        [copy for j in range(chunks) for copy in by_source(where, blocks[j], stages[j], in_sems.at[j])]
    )
    d_mixed = [stage.reshape(n_seq, rows, cols) for stage in stages]
    part = cols // 3
    zero = jnp.zeros((1, width), F32)
    total[...] = sums[...]
    for j in range(chunks):
        for s in range(n_seq):
            lo = (s * chunks + j) * part
            total[0:1, lo : lo + part] = rowsum(d_mixed[j][s, :, 0:part].astype(F32))
            total[1:2, lo : lo + part] = rowsum(d_mixed[j][s, :, 2 * part :].astype(F32))
    for load in loads:
        load.wait()
    quarter = width // 4
    per_side = n_seq // 2
    for q in range(4):
        at = slice(q * quarter, (q + 1) * quarter)
        acc = None
        for j in range(chunks):
            for side in range(2):
                left = jnp.concatenate([d_mixed[j][side * per_side + i] for i in range(per_side)], axis=1)
                term = _nt(left, ws[j][side, at, :])
                acc = term if acc is None else acc + term
        wide[:, at] = acc
    step = min(64, rows)

    def norms(i, carry):
        g, s = carry
        at = pl.ds(pl.multiple_of(i * step, step), step)
        e = wide[at, :]
        n, inv = norm_parts(tok[at, :].astype(F32))
        tokens_grad[at, :] = (d_residual[at, :] + norm_back(n, inv, vec[4:5, :], e)).astype(BF16)
        return g + rowsum(e * n), s + rowsum(e)

    g, s = lax.fori_loop(0, rows // step, norms, (zero, zero))
    total[4:5, :] = g
    total[8:9, :] = s
    if not rings:
        small[...] = total[...]
        return
    z, x = where[0], where[1]
    own = width // (2 * nz)
    n_bias = fc1_sum.shape[1] // width
    for o in range(2 * nz):
        slot = lax.rem(z + 2 * nz - 1 - o // 2, nz) + jnp.where(x == o % 2, nz, 0)
        small[slot, 0:N_VEC, :] = total[0:N_VEC, o * own : (o + 1) * own]
        for j in range(n_bias):
            lo = (o * n_bias + j) * own
            small[slot, N_VEC + j : N_VEC + j + 1, :] = fc1_sum[:, lo : lo + own]


def last(where, d_mixed, tokens, d_residual, vec, sums, fc1_sum, pieces):
    nz = lax.axis_size("z")
    rings = uses_rings()
    rows, width = tokens.shape
    chunks = len(d_mixed)
    small = ((2 * nz, N_VEC + fc1_sum.shape[1] // width, width // (2 * nz)), F32) if rings else ((16, width), F32)
    return call(
        functools.partial(last_kernel, nz=nz, chunks=chunks, n_pieces=len(pieces), rings=rings),
        "last",
        where,
        [b for blocks in d_mixed for b in blocks] + [tokens, d_residual, vec, sums, fc1_sum] + list(pieces),
        [ANY] * (chunks * N_SEQ) + [VMEM] * 5 + [ANY] * len(pieces),
        [((rows, width), BF16), small],
        [pltpu.VMEM((2, width, 3 * width // chunks // 2), BF16)] * chunks
        + [pltpu.VMEM((N_SEQ * rows, 3 * width // chunks // N_SEQ), BF16)] * chunks
        + [pltpu.VMEM((rows, width), F32), pltpu.VMEM((16, width), F32), pltpu.SemaphoreType.DMA((chunks, N_SEQ))]
        + [pltpu.SemaphoreType.DMA((n_copies(pieces),))] * chunks,
        cost=cost_of(12),
    )


def reduce_small(small, fc1_sum, own):
    nz = lax.axis_size("z")
    if not uses_rings():
        n_dp = nz * lax.axis_size("x")
        low = jnp.concatenate(
            (small[:N_VEC].reshape(N_VEC, n_dp, own).transpose(1, 0, 2), fc1_sum.reshape(n_dp, -1, own)),
            axis=1,
        )
        part = lax.psum_scatter(low, DP_AXES, scatter_dimension=0, tiled=False)
        return lax.psum(part.astype(BF16), SEQ_AXES).astype(F32)
    cur = small.astype(BF16)
    for axis in ("c", "y"):
        cur = add_low(cur, lax.ppermute(cur, axis, SWAP))
    keep = add_low(cur[nz:], lax.ppermute(cur[:nz], "x", SWAP))
    cur = keep[0]
    for step in range(1, nz):
        cur = add_low(lax.ppermute(cur, "z", ring(nz)), keep[step])
    return cur.astype(F32)


def exchange(blocks):
    both = [(i, i ^ 3) for i in range(4)]
    return [
        blocks[0],
        lax.ppermute(blocks[1], "c", SWAP),
        lax.ppermute(blocks[2], "y", SWAP),
        lax.ppermute(blocks[3], SEQ_AXES, both),
    ]


def per_device(
    tokens,
    out_grad,
    qkv_weight,
    qv_bias,
    proj_weight,
    fc1_weight,
    fc1_bias,
    fc2_weight,
    out_bias,
    norm_gains,
    norm_shifts,
):
    n_seq = lax.axis_size("y") * lax.axis_size("c")
    rows, width = tokens.shape
    own = qv_bias.shape[1]
    chunks = CHUNKS
    grp = width // n_seq
    part = grp // chunks
    heads = part // HD
    seq_len = n_seq * rows
    nz = lax.axis_size("z")
    where = here()
    qkv_shards = qkv_weight.reshape(-1, 3, n_seq, chunks, part).transpose(3, 0, 2, 1, 4)
    qkv_shards = qkv_shards.reshape(chunks, -1, 3 * width // chunks)
    small = jnp.concatenate(
        (qv_bias, out_bias, norm_gains, norm_shifts, fc1_bias.reshape(-1, own)), axis=0
    )
    rings = uses_rings()
    if rings:
        groups = fc2_weight.shape[0] // proj_weight.shape[0]
        fc2_groups = fc2_weight.reshape(groups, -1, 2, width // 2).transpose(2, 1, 0, 3)
        vec_in = Gather(small, False)
        qkv_in = Gather(jnp.concatenate([in_halves(s) for s in qkv_shards], axis=2))
        up_in = Gather(jnp.concatenate((in_halves(proj_weight), in_halves(fc1_weight)), axis=2))
        down_in = Gather(fc2_groups.reshape(2, -1, groups * width // 2))
        for step in range(nz):
            if step == 1:
                qkv_in.cur, up_in.cur, down_in.cur = lax.optimization_barrier(
                    (qkv_in.cur, up_in.cur, down_in.cur)
                )
            vec_in.hop()
            qkv_in.hop(*vec_in.mine[-3:])
        vec, fc1_b = small_vectors(vec_in.pieces(), width)
        qkv_pieces = qkv_in.pieces()
        up_in.hop(qkv_in.cur)
    else:
        vec, fc1_b = plain_vectors(small, width)
        qkv_pieces = [lax.all_gather(jnp.concatenate(tuple(qkv_shards), axis=1), DP_AXES, axis=0, tiled=True)]
        half = 3 * width // chunks // 2
        order = [2 * j + side for side in range(2) for j in range(chunks)]
        qkv_pieces = [jnp.concatenate([qkv_pieces[0][:, o * half : (o + 1) * half] for o in order], axis=1)]
        rest_sets = [
            [lax.all_gather(w, DP_AXES, axis=0, tiled=True)]
            for w in (proj_weight, fc1_weight, fc2_weight)
        ]
    by_heads, att, kept = [], [], []
    first = tokens
    for j in range(chunks):
        outs = [((rows, 3 * part), BF16)] * n_seq
        if j == 0:
            outs.append(((rows, width), BF16))
        got = call(
            functools.partial(qkv_kernel, nz=nz, chunk=j, chunks=chunks, n_pieces=len(qkv_pieces)),
            "qkv",
            where,
            [first, vec] + qkv_pieces,
            [VMEM] * 2 + [ANY] * len(qkv_pieces),
            outs,
            [
                pltpu.VMEM((2, width, 3 * width // chunks // 2), BF16),
                pltpu.VMEM((seq_len, 3 * part), BF16),
                pltpu.SemaphoreType.DMA((n_copies(qkv_pieces),)),
                pltpu.SemaphoreType.DMA((n_seq,)),
            ],
            out_specs=[ANY] * n_seq + [VMEM] * (j == 0),
            cost=cost_of(7),
        )
        if j == 0:
            first = normed = got[n_seq]
            if rings:
                first = up_in.arrive(first)
                down_in.hop(up_in.cur)
                up_in.hop()
        by_heads.append(exchange(got[:n_seq]))
    for j in range(chunks):
        if rings and j == 0:
            by_heads[0][0] = down_in.arrive(by_heads[0][0])
            down_in.hop()
        if rings and j == 1:
            by_heads[1][0] = up_in.arrive(by_heads[1][0])
            by_heads[1][0] = down_in.arrive(by_heads[1][0])
            up_in.hop()
        out_heads, out_cols, lse = attn_fwd(where, by_heads[j], heads, 1024)
        kept.append((out_cols, lse))
        att.append(exchange(out_heads))
    if rings:
        while down_in.hops < nz:
            for flow in (down_in, up_in):
                if flow.hops < nz:
                    flow.hop()
        rest_sets = [up_in.pieces(), down_in.pieces()]
    outs = mlp(where, att, tokens, out_grad, vec, fc1_b, rest_sets)
    layer_out, d_residual, d_second, active, d_hidden, normed_two, d_branch, attended, sums, fc1_sum = outs[:10]
    d_heads = [exchange(outs[10 + j * n_seq : 10 + (j + 1) * n_seq]) for j in range(chunks)]
    ff = active.shape[1]
    r = proj_weight.shape[0]
    if rings:
        down_out = grads(
            down_grad_kernel, "down_grad", where, (active, d_second), r, groups * width // 2, parts=4
        )
        d_heads[0][0], *down_out.out = together(d_heads[0][0], *down_out.out)
        down_out.cross()
        down_out.cross()
    else:
        grad_fc2 = reduce_plain(active, d_second)
        grad_fc1 = reduce_plain(normed_two, d_hidden)
        grad_proj = reduce_plain(attended, d_branch)
    d_mixed, qkv_out, total_qkv = [], [], []
    for j in range(chunks):
        d_by_heads = list(attn_bwd(where, by_heads[j], d_heads[j], kept[j][0], kept[j][1], heads, 512))
        d_mixed.append(exchange(d_by_heads))
        if rings and j == 0:
            normed_two, d_by_heads[0], down_out.from_x[0], down_out.from_x[1] = together(
                normed_two, d_by_heads[0], down_out.from_x[0], down_out.from_x[1]
            )
            down_out.cross(down_out.from_x[0])
            down_out.add(0)
            down_out.ring()
            up_out = grads(
                up_grad_kernel,
                "up_grad",
                where,
                (normed_two, d_hidden, attended, d_branch),
                r,
                (width + ff) // 2,
                parts=4,
                after=(down_out.from_x[2], down_out.passed),
            )
            d_heads[1][0], *up_out.out = together(d_heads[1][0], *up_out.out)
            down_out.cross(down_out.passed)
            down_out.add(1)
            down_out.ring()
            up_out.cross(down_out.from_x[2])
        if rings and j == 1:
            d_mixed[0][0], down_out.from_x[3], down_out.passed, up_out.from_x[0], unused = together(
                d_mixed[0][0], down_out.from_x[3], down_out.passed, up_out.from_x[0], d_by_heads[0]
            )
            up_out.cross(down_out.from_x[3])
            down_out.add(2)
            down_out.cur = tie(down_out.cur, *d_mixed[1])
            down_out.ring()
            up_out.add(0)
            up_out.cur = tie(up_out.cur, *d_mixed[1])
            up_out.ring()
    for j in range(chunks):
        if rings and j == 1:
            d_mixed[1][0], up_out.from_x[1], down_out.passed, *qkv_out[0].out = together(
                d_mixed[1][0], up_out.from_x[1], down_out.passed, *qkv_out[0].out
            )
            down_out.add(3)
            up_out.cross(up_out.from_x[1])
            qkv_out[0].cross(up_out.from_x[1])
        if rings:
            qkv_out.append(
                grads(
                    qkv_grad_kernel,
                    "qkv_grad",
                    where,
                    [normed] + d_mixed[j],
                    r,
                    n_seq // 2 * 3 * part,
                    [VMEM] + [ANY] * n_seq,
                    [pltpu.VMEM((seq_len, 3 * part), BF16), pltpu.SemaphoreType.DMA((n_seq,))],
                )
            )
        else:
            me = where[3]
            blocks = jnp.stack(d_mixed[j])
            order = jnp.stack([jnp.bitwise_xor(me, i) for i in range(n_seq)])
            blocks = jnp.take(blocks, order, axis=0)
            total_qkv.append(reduce_plain(normed, blocks.transpose(1, 0, 2).reshape(rows, -1)))
    if rings:
        d_mixed[1][0], up_out.passed, up_out.from_x[2], *qkv_out[1].out = together(
            d_mixed[1][0], up_out.passed, up_out.from_x[2], *qkv_out[1].out
        )
        up_out.add(1)
        up_out.ring()
        up_out.cross(up_out.from_x[2])
        qkv_out[0].cross(up_out.from_x[2])
    tokens_grad, small_grads = last(
        where, d_mixed, tokens, d_residual, vec, sums, fc1_sum, qkv_pieces
    )
    if rings:
        small_grads, up_out.from_x[3], qkv_out[0].from_x[0] = together(
            small_grads, up_out.from_x[3], qkv_out[0].from_x[0]
        )
    total_small = reduce_small(small_grads, fc1_sum, own)
    if rings:
        qkv_out[1].cross(up_out.from_x[3])
        qkv_out[1].cross(up_out.from_x[3])
        for step in range(2, nz):
            up_out.add(step)
            if step < nz - 1:
                up_out.ring()
        for step in range(nz):
            for flow in qkv_out:
                flow.add(step)
                if step < nz - 1:
                    flow.ring()
        low = down_out.finish()
        grad_fc2 = jnp.stack(low).reshape(2, r, groups, width // 2).transpose(2, 1, 0, 3)
        grad_fc2 = grad_fc2.reshape(groups * r, width).astype(F32)
        low = up_out.finish()
        at = width // 2
        grad_proj = jnp.concatenate([part_[:, :at] for part_ in low], axis=1).astype(F32)
        grad_fc1 = jnp.concatenate([part_[:, at:] for part_ in low], axis=1).astype(F32)
        total_qkv = [jnp.concatenate(f.finish(), axis=1).astype(F32) for f in qkv_out]
    qkv_grad = jnp.stack([t.reshape(-1, n_seq, 3, part) for t in total_qkv])
    qkv_grad = qkv_grad.transpose(1, 3, 2, 0, 4).reshape(-1, 3 * width)
    return (
        layer_out,
        tokens_grad,
        qkv_grad,
        total_small[0:2],
        grad_proj,
        grad_fc1,
        total_small[N_VEC:].reshape(-1),
        grad_fc2,
        total_small[2:4],
        total_small[4:8],
        total_small[8:12],
    )


CHUNKS = 2


def solution(mesh):
    n_dp, n_seq = mesh.devices.shape
    fine = Mesh(mesh.devices.reshape(n_dp // 2, 2, n_seq // 2, 2), DP_AXES + SEQ_AXES)
    tok = P(DP_AXES + SEQ_AXES, None)
    by_row = P(DP_AXES, None)
    by_col = P(None, DP_AXES)
    weights = (by_row, by_col, by_row, by_row, P(DP_AXES), by_row, by_col, by_col, by_col)
    return jax.shard_map(
        per_device,
        mesh=fine,
        in_specs=(tok, tok) + weights,
        out_specs=(tok, tok) + weights,
        check_vma=False,
    )
```

```python
import functools
import math

import jax
import jax.numpy as jnp
from jax.sharding import Mesh
from jax.sharding import PartitionSpec as P
from jax import lax
from jax.experimental import pallas as pl
from jax.experimental.pallas import tpu as pltpu
HD=64
RELAX=32.0
C2=RELAX*math.log2(math.e)
NEG=-1e30

def _nt(a,b):
    return lax.dot_general(a,b,(((1,),(1,)),((),())),preferred_element_type=jnp.float32)
def _nn(a,b):
    return lax.dot_general(a,b,(((1,),(0,)),((),())),preferred_element_type=jnp.float32)

def _tr(x):
    return jnp.transpose(x.astype(jnp.float32)).astype(jnp.bfloat16)

def by_source(where, refs, dst, sems):
    rows = refs[0].shape[0]
    copies = []
    for i, ref in enumerate(refs):
        at = pl.multiple_of(jnp.bitwise_xor(where[3], i) * rows, rows)
        copies.append(pltpu.make_async_copy(ref, dst.at[pl.ds(at, rows), :], sems.at[i]))
    return copies

def by_target(where, src, refs, sems):
    rows = refs[0].shape[0]
    copies = []
    for i, ref in enumerate(refs):
        at = pl.multiple_of(jnp.bitwise_xor(where[3], i) * rows, rows)
        copies.append(pltpu.make_async_copy(src.at[pl.ds(at, rows), :], ref, sems.at[i]))
    return copies

def run_copies(copies):
    for copy in copies:
        copy.start()
    for copy in copies:
        copy.wait()

def fwd_kernel(where,*refs,nh,blk,n):
    ins,outs=refs[:n],refs[n:2*n]
    ot_ref,lse_ref,vt_ref,qkv_ref,o_ref,sems=refs[2*n:]
    seq=qkv_ref.shape[0]; w=nh*HD
    nb=seq//blk
    run_copies(by_source(where,ins,qkv_ref,sems))
    q_ref,k_ref,v_ref=(qkv_ref.at[:,i*w:(i+1)*w] for i in range(3))
    for b in range(nb):
        vt_ref[:,b*blk:(b+1)*blk]=_tr(v_ref[b*blk:(b+1)*blk,:])
    lane=lax.broadcasted_iota(jnp.int32,(1,w),1)//HD
    tri=lax.broadcasted_iota(jnp.int32,(blk,blk),0)<=lax.broadcasted_iota(jnp.int32,(blk,blk),1)
    def qstep(qb,_):
        q0=pl.multiple_of(qb*blk,blk)
        q=q_ref[pl.ds(q0,blk),:]
        qm=[jnp.where(lane==h,q,jnp.zeros_like(q)) for h in range(nh)]
        def kv(kb,carry,diag):
            k0=pl.multiple_of(kb*blk,blk)
            k=k_ref[pl.ds(k0,blk),:]
            out=[]
            for h in range(nh):
                m,l,acc=carry[3*h:3*h+3]
                s=_nt(k,qm[h])*C2
                if diag: s=jnp.where(tri,s,NEG)
                mn=jnp.maximum(m,jnp.max(s,axis=0,keepdims=True))
                a=jnp.exp2(m-mn)
                p=jnp.exp2(s-mn)
                l=l*a+jnp.sum(p,axis=0,keepdims=True)
                acc=acc*a+_nn(vt_ref[h*HD:(h+1)*HD,pl.ds(k0,blk)],p.astype(jnp.bfloat16))
                out+= [mn,l,acc]
            return tuple(out)
        init=[]
        for h in range(nh):
            init+=[jnp.full((1,blk),NEG,jnp.float32),jnp.zeros((1,blk),jnp.float32),jnp.zeros((HD,blk),jnp.float32)]
        c=kv(qb,tuple(init),True)
        c=lax.fori_loop(0,qb,lambda kb,cc: kv(kb,cc,False),c)
        for h in range(nh):
            m,l,acc=c[3*h:3*h+3]
            ot_ref[h*HD:(h+1)*HD,pl.ds(q0,blk)]=acc/l
            lse_ref[h:h+1,pl.ds(q0,blk)]=m+jnp.log2(l)
        o_ref[pl.ds(q0,blk),:]=jnp.transpose(ot_ref[:,pl.ds(q0,blk)]).astype(jnp.bfloat16)
        return 0
    lax.fori_loop(0,nb,qstep,0)
    run_copies(by_target(where,o_ref,outs,sems))

def attn_fwd(where, qkv, nh, blk=512):
    n=len(qkv); rows=qkv[0].shape[0]
    seq=n*rows; w=nh*HD
    blk=min(blk,seq)
    vm=pl.BlockSpec(memory_space=pltpu.VMEM)
    an=pl.BlockSpec(memory_space=pl.ANY)
    outs=pl.pallas_call(functools.partial(fwd_kernel,nh=nh,blk=blk,n=n),
      grid_spec=pltpu.PrefetchScalarGridSpec(num_scalar_prefetch=1,
        in_specs=[an]*n,out_specs=[an]*n+[vm]*2,
        scratch_shapes=[pltpu.VMEM((w,seq),jnp.bfloat16),pltpu.VMEM((seq,3*w),jnp.bfloat16),pltpu.VMEM((seq,w),jnp.bfloat16),pltpu.SemaphoreType.DMA((n,))]),
      out_shape=[jax.ShapeDtypeStruct((rows,w),jnp.bfloat16)]*n+[jax.ShapeDtypeStruct((w,seq),jnp.float32),jax.ShapeDtypeStruct((8,seq),jnp.float32)],
      compiler_params=pltpu.CompilerParams(vmem_limit_bytes=48<<20),
      cost_estimate=pl.CostEstimate(flops=int(nh*4.5*1.1e9), transcendentals=0, bytes_accessed=1<<20),
      name="attn_fwd")(where,*qkv)
    return outs[:n],outs[n],outs[n+1]

def bwd_kernel(where,*refs,nh,blk,n):
    ins,dos,outs=refs[:n],refs[n:2*n],refs[2*n+2:3*n+2]
    ot_ref,lse_ref=refs[2*n:2*n+2]
    kt_ref,dl_ref,dqt_ref,qkv_ref,do_ref,d_ref,sems,do_sems=refs[3*n+2:]
    seq=qkv_ref.shape[0]; w=nh*HD
    nb=seq//blk
    run_copies(by_source(where,ins,qkv_ref,sems)+by_source(where,dos,do_ref,do_sems))
    q_ref,k_ref,v_ref=(qkv_ref.at[:,i*w:(i+1)*w] for i in range(3))
    for b in range(nb):
        sl=slice(b*blk,(b+1)*blk)
        kt_ref[:,sl]=_tr(k_ref[sl,:])
        dot_=jnp.transpose(do_ref[sl,:].astype(jnp.float32))
        pr=dot_*ot_ref[:,sl]
        for h in range(nh):
            dl_ref[h:h+1,sl]=jnp.sum(pr[h*HD:(h+1)*HD],axis=0,keepdims=True)
    dqt_ref[...]=jnp.zeros_like(dqt_ref)
    lane=lax.broadcasted_iota(jnp.int32,(1,w),1)//HD
    tri=lax.broadcasted_iota(jnp.int32,(blk,blk),0)<=lax.broadcasted_iota(jnp.int32,(blk,blk),1)
    def kstep(kb,_):
        k0=pl.multiple_of(kb*blk,blk)
        k=k_ref[pl.ds(k0,blk),:]
        v=v_ref[pl.ds(k0,blk),:]
        def qs(qb,carry,diag):
            dk,dv=carry
            q0=pl.multiple_of(qb*blk,blk)
            q=q_ref[pl.ds(q0,blk),:]
            do=do_ref[pl.ds(q0,blk),:]
            for h in range(nh):
                qm=jnp.where(lane==h,q,jnp.zeros_like(q))
                dom=jnp.where(lane==h,do,jnp.zeros_like(do))
                s=_nt(k,qm)
                dp=_nt(v,dom)
                p=jnp.exp2(s*C2-lse_ref[h:h+1,pl.ds(q0,blk)])
                if diag: p=jnp.where(tri,p,0.0)
                ds=(p*(dp-dl_ref[h:h+1,pl.ds(q0,blk)])).astype(jnp.bfloat16)
                dv=dv+_nn(p.astype(jnp.bfloat16),dom)
                dk=dk+_nn(ds,qm)
                dqt_ref[h*HD:(h+1)*HD,pl.ds(q0,blk)]+=_nn(kt_ref[h*HD:(h+1)*HD,pl.ds(k0,blk)],ds)
            return dk,dv
        z=jnp.zeros((blk,w),jnp.float32)
        c=qs(kb,(z,z),True)
        dk,dv=lax.fori_loop(kb+1,nb,lambda qb,cc: qs(qb,cc,False),c)
        d_ref[pl.ds(k0,blk),w:2*w]=(dk*RELAX).astype(jnp.bfloat16)
        d_ref[pl.ds(k0,blk),2*w:3*w]=dv.astype(jnp.bfloat16)
        return 0
    lax.fori_loop(0,nb,kstep,0)
    for b in range(nb):
        sl=slice(b*blk,(b+1)*blk)
        d_ref[sl,0:w]=(jnp.transpose(dqt_ref[:,sl])*(1.0/math.sqrt(HD))).astype(jnp.bfloat16)
    run_copies(by_target(where,d_ref,outs,sems))

def attn_bwd(where, qkv, do, ot, lse, nh, blk=512):
    n=len(qkv); rows=qkv[0].shape[0]
    seq=n*rows; w=nh*HD
    blk=min(blk,seq)
    vm=pl.BlockSpec(memory_space=pltpu.VMEM)
    an=pl.BlockSpec(memory_space=pl.ANY)
    return pl.pallas_call(functools.partial(bwd_kernel,nh=nh,blk=blk,n=n),
      grid_spec=pltpu.PrefetchScalarGridSpec(num_scalar_prefetch=1,
        in_specs=[an]*(2*n)+[vm]*2,out_specs=[an]*n,
        scratch_shapes=[pltpu.VMEM((w,seq),jnp.bfloat16),pltpu.VMEM((8,seq),jnp.float32),pltpu.VMEM((w,seq),jnp.float32),
          pltpu.VMEM((seq,3*w),jnp.bfloat16),pltpu.VMEM((seq,w),jnp.bfloat16),pltpu.VMEM((seq,3*w),jnp.bfloat16),
          pltpu.SemaphoreType.DMA((n,)),pltpu.SemaphoreType.DMA((n,))]),
      out_shape=[jax.ShapeDtypeStruct((rows,3*w),jnp.bfloat16)]*n,
      compiler_params=pltpu.CompilerParams(vmem_limit_bytes=56<<20),
      cost_estimate=pl.CostEstimate(flops=int(nh*9.5*1.1e9), transcendentals=0, bytes_accessed=1<<20),
      name="attn_bwd")(where,*qkv,*do,ot,lse)


NORM_EPS = 1e-05
F32 = jnp.float32
BF16 = jnp.bfloat16
SWAP = [(0, 1), (1, 0)]
SEQ_AXES = ("y", "c")
DP_AXES = ("z", "x")
ANY = pl.BlockSpec(memory_space=pl.ANY)
VMEM = pl.BlockSpec(memory_space=pltpu.VMEM)
GELU_K = math.sqrt(2.0 / math.pi)
GELU_A = 0.044715
N_VEC = 12
N_SEQ = 4


def add_low(*terms):
    return sum(t.astype(F32) for t in terms).astype(BF16)


def ring(n):
    return [(i, (i + 1) % n) for i in range(n)]


def uses_rings():
    return lax.axis_size("z") * lax.axis_size("x") <= 8


def here():
    seq = lax.axis_index("y") * lax.axis_size("c") + lax.axis_index("c")
    return jnp.stack([lax.axis_index(a) for a in ("z", "x", "c")] + [seq]).astype(jnp.int32)


def call(kernel, name, where, args, specs, outs, scratch=(), grid=(), out_specs=None, cost=None):
    if out_specs is None:
        out_specs = [VMEM] * len(outs)
    return list(pl.pallas_call(
        kernel,
        grid_spec=pltpu.PrefetchScalarGridSpec(
            num_scalar_prefetch=1,
            grid=grid,
            in_specs=specs,
            out_specs=out_specs,
            scratch_shapes=list(scratch),
        ),
        out_shape=[jax.ShapeDtypeStruct(s, d) for s, d in outs],
        compiler_params=pltpu.CompilerParams(vmem_limit_bytes=60 << 20),
        cost_estimate=cost,
        name=name,
    )(where, *args))


def cost_of(microseconds):
    return pl.CostEstimate(flops=int(microseconds * 1.1e9), transcendentals=0, bytes_accessed=1 << 20)


def tie(value, *others):
    return lax.optimization_barrier((value,) + others)[0]


def together(*values):
    return list(lax.optimization_barrier(tuple(values)))


class Box:
    def __init__(self, v):
        self.v = v


class Stages:
    def __init__(self):
        self.every = []

    def box(self, v):
        self.every.append(Box(v))
        return self.every[-1]

    def boxes(self, values):
        return [self.box(v) for v in values]

    def begin(self, *some):
        return [b.v for b in some]

    def sync(self):
        for box, v in zip(self.every, together(*[b.v for b in self.every])):
            box.v = v


class Gather:
    def __init__(self, stages, shards, core_halves=True):
        self.stages, self.shards, self.core_halves = stages, shards, core_halves
        cur = shards
        if core_halves:
            cur = lax.dynamic_index_in_dim(shards, lax.axis_index("c"), 0, False)
        self.box = stages.box
        self.blocks, self.others = [self.box(cur)], []
        self.swapped = {}

    def z(self):
        (block,) = self.stages.begin(self.blocks[-1])
        self.blocks.append(self.box(lax.ppermute(block, "z", ring(lax.axis_size("z")))))
        return self.blocks[-1]

    def x(self):
        (block,) = self.stages.begin(self.blocks[len(self.others)])
        self.others.append(self.box(lax.ppermute(block, "x", SWAP)))
        return self.others[-1]

    def c(self):
        new = [b for b in self.blocks[1:] + self.others if id(b) not in self.swapped]
        for box, v in zip(new, self.stages.begin(*new)):
            self.swapped[id(box)] = self.box(lax.ppermute(v, "c", SWAP))
        return [self.swapped[id(box)] for box in new]

    def pieces(self):
        mine = [self.others[0]]
        for block, other in zip(self.blocks[1:], self.others[1:]):
            mine += [block, other]
        if not self.core_halves:
            return [self.shards] + self.stages.begin(*mine)
        self.c()
        return [self.shards] + self.stages.begin(*mine, *[self.swapped[id(b)] for b in mine])


def in_halves(weight):
    rows, cols = weight.shape
    return weight.reshape(rows, 2, cols // 2).transpose(1, 0, 2)


def owner_of(index, nz, z, x):
    step, side = (index + 1) // 2, (index + 1) % 2
    return lax.rem(z + nz - step, nz) * 2 + (x if side == 0 else 1 - x)


class Loader:
    def __init__(self, where, pieces, dsts, sems, nz, col=0):
        self.copies = []
        self.sems = sems
        if len(pieces[0].shape) == 2:
            self.sides = (0, 1)
            for i, (piece, dst) in enumerate(zip(pieces, dsts)):
                half = dst.shape[2]
                for side in range(2):
                    at = side * (piece.shape[1] // 2) + col
                    self.add(i, side, piece.at[:, at : at + half], dst.at[side])
            return
        z, x, c = where[0], where[1], where[2]
        self.sides = (c, 1 - c)
        rows = pieces[0].shape[1]
        others = (len(pieces) - 1) // 2
        for i, dst in enumerate(dsts):
            half = dst.shape[2]
            groups = dst.shape[1] // (2 * nz * rows)
            for g in range(groups):
                cols = slice(col, col + half)
                col += half
                for k in range(2):
                    side = self.sides[k]
                    blocks = [(z * 2 + x, pieces[0].at[side, :, cols])]
                    for n in range(others):
                        blocks.append((owner_of(n, nz, z, x), pieces[1 + k * others + n].at[:, cols]))
                    for owner, block in blocks:
                        row = pl.multiple_of((owner * groups + g) * rows, rows)
                        self.add(i, k, block, dst.at[side, pl.ds(row, rows), :])

    def add(self, i, k, src, to):
        self.copies.append((i, k, pltpu.make_async_copy(src, to, self.sems.at[len(self.copies)])))

    def pick(self, dst, half):
        return [
            copy
            for i, k, copy in self.copies
            if (dst is None or i == dst) and (half is None or k == half)
        ]

    def start(self, dst=None, half=None):
        for copy in self.pick(dst, half):
            copy.start()

    def wait(self, dst=None, half=None):
        for copy in self.pick(dst, half):
            copy.wait()


class Writer:
    def __init__(self, sems):
        self.sems, self.copies = sems, []

    def put(self, src, to):
        copy = pltpu.make_async_copy(src, to, self.sems.at[len(self.copies)])
        copy.start()
        self.copies.append(copy)

    def wait(self):
        for copy in self.copies:
            copy.wait()


def n_copies(pieces, groups=1):
    return (len(pieces) + 1) * groups


def norm_parts(v):
    c = v - jnp.mean(v, axis=-1, keepdims=True)
    inv = lax.rsqrt(jnp.mean(c * c, axis=-1, keepdims=True) + NORM_EPS)
    return c * inv, inv


def norm_back(n, inv, gain, e):
    ge = g_e = gain * e
    return (g_e - jnp.mean(ge, axis=-1, keepdims=True) - n * jnp.mean(ge * n, axis=-1, keepdims=True)) * inv


def rowsum(v):
    return jnp.sum(v, axis=0, keepdims=True)


def vectors_kernel(where, *refs, nz, n_bias):
    pieces, vec, bias = refs[:-2], refs[-2], refs[-1]
    z, x = where[0], where[1]
    own = pieces[0].shape[0]
    order = [z * 2 + x] + [owner_of(i, nz, z, x) for i in range(2 * nz - 1)]
    got = [jnp.transpose(piece[...].astype(F32))[: N_VEC + n_bias] for piece in pieces]
    for o in range(2 * nz):
        acc = jnp.zeros(got[0].shape, F32)
        for at, piece in zip(order, got):
            acc = jnp.where(at == o, piece, acc)
        vec[0:N_VEC, o * own : (o + 1) * own] = acc[:N_VEC]
        for j in range(n_bias):
            lo = (o * n_bias + j) * own
            bias[0:1, lo : lo + own] = acc[N_VEC + j : N_VEC + j + 1]


def small_vectors(pieces, width, n_bias):
    nz = lax.axis_size("z")
    own = pieces[0].shape[-2]
    at = pieces[1].shape[1] // own - 1
    blocks = pieces[: 2 * nz]
    return call(
        functools.partial(vectors_kernel, nz=nz, n_bias=n_bias),
        "vectors",
        here(),
        blocks,
        [pl.BlockSpec((None, own, own), lambda i, w: (0, 0, at))]
        + [pl.BlockSpec((own, own), lambda i, w: (0, at))] * (len(blocks) - 1),
        [((16, width), F32), ((1, n_bias * 2 * nz * own), F32)],
        grid=(1,),
        out_specs=[
            pl.BlockSpec((16, width), lambda i, w: (0, 0)),
            pl.BlockSpec((1, n_bias * 2 * nz * own), lambda i, w: (0, 0)),
        ],
        cost=cost_of(2),
    )


def plain_vectors(small, width):
    placed = lax.all_gather(small, DP_AXES, axis=0, tiled=False).astype(F32)
    vec = placed[:, :N_VEC].transpose(1, 0, 2).reshape(N_VEC, width)
    return jnp.pad(vec, ((0, 4), (0, 0))), placed[:, N_VEC:].reshape(1, -1)


def first_norm(tok, vec, normed):
    rows = min(64, tok.shape[0])

    def body(i, carry):
        at = pl.ds(pl.multiple_of(i * rows, rows), rows)
        n, inv = norm_parts(tok[at, :].astype(F32))
        normed[at, :] = (n * vec[4:5, :] + vec[8:9, :]).astype(BF16)
        return carry

    lax.fori_loop(0, tok.shape[0] // rows, body, 0)


def qkv_kernel(where, first, vec, *refs, nz, chunk, chunks, n_pieces):
    pieces, refs = refs[:n_pieces], list(refs[n_pieces:])
    n_seq = N_SEQ
    outs = [refs.pop(0) for _ in range(n_seq)]
    normed = refs.pop(0) if chunk == 0 else first
    w, stage, sems, out_sems = refs
    rows, cols = outs[0].shape
    per_side = n_seq // 2
    load = Loader(where, pieces, [w], sems, nz, chunk * per_side * cols)
    load.start()
    if chunk == 0:
        first_norm(first, vec, normed)
    load.wait()
    wide = cols // 3
    grp = wide * chunks
    scale = 1.0 / (RELAX * math.sqrt(HD))
    for side in range(2):
        mixed = _nn(normed[...], w[side])
        for j in range(per_side):
            s = side * per_side + j
            lo = s * grp + chunk * wide
            block = mixed[:, j * cols : (j + 1) * cols]
            at = slice(s * rows, (s + 1) * rows)
            stage[at, 0:wide] = ((block[:, 0:wide] + vec[0:1, lo : lo + wide]) * scale).astype(BF16)
            stage[at, wide : 2 * wide] = block[:, wide : 2 * wide].astype(BF16)
            stage[at, 2 * wide :] = (block[:, 2 * wide :] + vec[1:2, lo : lo + wide]).astype(BF16)
    run_copies(by_target(where, stage, outs, out_sems))


def gelu_parts(h):
    return jnp.tanh(h * (GELU_K + (GELU_K * GELU_A) * (h * h)))


def up_kernel(where, *refs, nz, n_att, n_pieces):
    refs = list(refs)
    att_in = [[refs.pop(0) for _ in range(N_SEQ)] for _ in range(n_att)]
    tok, vec, fc1_b = [refs.pop(0) for _ in range(3)]
    pieces = [refs.pop(0) for _ in range(n_pieces)]
    out_att, out_branch, out_residual, out_normed, out_hidden, out_active = [refs.pop(0) for _ in range(6)]
    proj_w, fc1_w, attended, branch, residual, normed_two, hidden, active, in_sems, out_sems = refs
    load = Loader(where, pieces, (proj_w, fc1_w), in_sems, nz)
    load.start(0)
    load.start(1)
    out = Writer(out_sems)
    rows, width = tok.shape
    part = att_in[0][0].shape[1]
    for i in range(N_SEQ):
        s = jnp.bitwise_xor(where[3], i)
        for j in range(n_att):
            lo = pl.multiple_of((s * n_att + j) * part, part)
            attended[:, pl.ds(lo, part)] = att_in[j][i][...]
    out.put(attended, out_att)
    load.wait(0)
    half = width // 2
    for side in range(2):
        cols = slice(side * half, (side + 1) * half)
        branch[:, cols] = _nn(attended[...], proj_w[side]) + vec[2:3, cols]
    out.put(branch, out_branch)
    step = min(64, rows)

    def norms(i, carry):
        at = pl.ds(pl.multiple_of(i * step, step), step)
        n, inv = norm_parts(branch[at, :])
        r = tok[at, :].astype(F32) + (n * vec[5:6, :] + vec[9:10, :])
        residual[at, :] = r
        n, inv = norm_parts(r)
        normed_two[at, :] = (n * vec[6:7, :] + vec[10:11, :]).astype(BF16)
        return carry

    lax.fori_loop(0, rows // step, norms, 0)
    out.put(residual, out_residual)
    out.put(normed_two, out_normed)
    load.wait(1)
    ff = hidden.shape[1]
    blk = 512
    for i in range(ff // blk):
        at = slice(i * blk, (i + 1) * blk)
        side, col = divmod(i * blk, ff // 2)
        h = _nn(normed_two[...], fc1_w[side, :, col : col + blk]) + fc1_b[:, at]
        hidden[:, at] = h
        active[:, at] = (0.5 * h * (1.0 + gelu_parts(h))).astype(BF16)
        out.put(hidden.at[:, at], out_hidden.at[:, at])
        out.put(active.at[:, at], out_active.at[:, at])
    out.wait()


def mid_kernel(where, active_in, residual_in, hidden_in, out_grad, vec, *refs, nz, n_pieces):
    pieces, refs = refs[:n_pieces], list(refs[n_pieces:])
    layer_out, d_second, out_hidden, sums, fc1_sum = [refs.pop(0) for _ in range(5)]
    fc2_w, active, residual, wide, hidden, d_hidden, load_sems, in_sems, out_sems = refs
    rows, width = out_grad.shape
    ff = hidden.shape[1]
    blk = 512
    load = Loader(where, pieces, (fc2_w,), load_sems, nz)
    out = Writer(out_sems)
    blocks = [slice(i * blk, (i + 1) * blk) for i in range(ff // blk)]
    ins = [
        pltpu.make_async_copy(active_in, active, in_sems.at[0]),
        pltpu.make_async_copy(residual_in, residual, in_sems.at[1]),
    ] + [
        pltpu.make_async_copy(hidden_in.at[:, at], hidden.at[:, at], in_sems.at[2 + i])
        for i, at in enumerate(blocks)
    ]
    ins[0].start()
    load.start(0, 0)
    load.start(0, 1)
    for copy in ins[1:]:
        copy.start()
    half = width // 2
    ins[0].wait()
    for k in range(2):
        load.wait(0, k)
        side = load.sides[k]
        cols = pl.ds(pl.multiple_of(side * half, half), half)
        wide[:, cols] = _nn(active[...], fc2_w[side]) + vec[3:4, cols]
    ins[1].wait()
    step = min(64, rows)

    def top(i, carry):
        g_sum, s_sum, b_sum = carry
        at = pl.ds(pl.multiple_of(i * step, step), step)
        n, inv = norm_parts(wide[at, :])
        e = out_grad[at, :].astype(F32)
        layer_out[at, :] = (residual[at, :] + (n * vec[7:8, :] + vec[11:12, :])).astype(BF16)
        d = norm_back(n, inv, vec[7:8, :], e).astype(BF16)
        d_second[at, :] = d
        return g_sum + rowsum(e * n), s_sum + rowsum(e), b_sum + rowsum(d.astype(F32))

    zero = jnp.zeros((1, width), F32)
    g_sum, s_sum, b_sum = lax.fori_loop(0, rows // step, top, (zero, zero, zero))
    sums[...] = jnp.zeros_like(sums)
    sums[3:4, :] = b_sum
    sums[7:8, :] = g_sum
    sums[11:12, :] = s_sum
    for copy in ins[2:]:
        copy.wait()
    for i, at in enumerate(blocks):
        d = _nt(d_second[:, 0:half], fc2_w[0, at, :]) + _nt(d_second[:, half:], fc2_w[1, at, :])
        h = hidden[:, at]
        t = gelu_parts(h)
        square = h * h
        bend = h * (0.5 * GELU_K + (1.5 * GELU_K * GELU_A) * square)
        low = (d * ((0.5 + 0.5 * t) + (1.0 - t * t) * bend)).astype(BF16)
        d_hidden[:, at] = low
        fc1_sum[:, at] = rowsum(low.astype(F32))
        if i % 2 == 1:
            pair = slice((i - 1) * blk, (i + 1) * blk)
            out.put(d_hidden.at[:, pair], out_hidden.at[:, pair])
    out.wait()


def back_kernel(where, out_grad, vec, sums_in, d_hidden_in, residual_in, branch_in, *refs, nz, n_att, n_pieces):
    refs = list(refs)
    ups = [refs.pop(0) for _ in range(n_pieces)]
    out_residual, out_branch, sums = [refs.pop(0) for _ in range(3)]
    d_att = [[refs.pop(0) for _ in range(N_SEQ)] for _ in range(n_att)]
    proj_w, fc1_w, d_hidden, residual, branch, wide, d_residual, d_branch = [refs.pop(0) for _ in range(8)]
    stages = [refs.pop(0) for _ in range(n_att)]
    up_sems, in_sems, out_sems = refs
    rows, width = out_grad.shape
    ff = d_hidden.shape[1]
    load = Loader(where, ups, (proj_w, fc1_w), up_sems, nz)
    out = Writer(out_sems)
    ff_half = ff // 2
    ins = []
    for k in range(2):
        at = pl.ds(pl.multiple_of(load.sides[k] * ff_half, ff_half), ff_half)
        ins.append(pltpu.make_async_copy(d_hidden_in.at[:, at], d_hidden.at[:, at], in_sems.at[k]))
        ins[k].start()
        load.start(1, k)
    ins.append(pltpu.make_async_copy(residual_in, residual, in_sems.at[2]))
    ins.append(pltpu.make_async_copy(branch_in, branch, in_sems.at[3]))
    ins[2].start()
    ins[3].start()
    load.start(0)
    half = width // 2
    for k in range(2):
        ins[k].wait()
        load.wait(1, k)
        side = load.sides[k]
        at = pl.ds(pl.multiple_of(side * ff_half, ff_half), ff_half)
        for q in range(2):
            rows_at = slice(q * half, (q + 1) * half)
            part = _nt(d_hidden[:, at], fc1_w[side, rows_at, :])
            wide[:, rows_at] = part if k == 0 else wide[:, rows_at] + part
    ins[2].wait()
    ins[3].wait()
    step = min(64, rows)

    def mid(i, carry):
        g2, s2, g1, s1, b_sum = carry
        at = pl.ds(pl.multiple_of(i * step, step), step)
        e = wide[at, :]
        n, inv = norm_parts(residual[at, :])
        d = out_grad[at, :].astype(F32) + norm_back(n, inv, vec[6:7, :], e)
        d_residual[at, :] = d
        g2, s2 = g2 + rowsum(e * n), s2 + rowsum(e)
        n, inv = norm_parts(branch[at, :])
        low = norm_back(n, inv, vec[5:6, :], d).astype(BF16)
        d_branch[at, :] = low
        return g2, s2, g1 + rowsum(d * n), s1 + rowsum(d), b_sum + rowsum(low.astype(F32))

    zero = jnp.zeros((1, width), F32)
    g2, s2, g1, s1, b_sum = lax.fori_loop(0, rows // step, mid, (zero,) * 5)
    out.put(d_residual, out_residual)
    out.put(d_branch, out_branch)
    sums[...] = sums_in[...]
    for row, v in ((6, g2), (10, s2), (5, g1), (9, s1), (2, b_sum)):
        sums[row : row + 1, :] = v
    load.wait(0)
    part = stages[0].shape[1]
    for s in range(N_SEQ):
        at = slice(s * n_att * part, (s + 1) * n_att * part)
        low = (_nt(d_branch[:, 0:half], proj_w[0, at, :]) + _nt(d_branch[:, half:], proj_w[1, at, :])).astype(BF16)
        for j in range(n_att):
            stages[j][s * rows : (s + 1) * rows, :] = low[:, j * part : (j + 1) * part]
    for j in range(n_att):
        for i, ref in enumerate(d_att[j]):
            at = pl.multiple_of(jnp.bitwise_xor(where[3], i) * rows, rows)
            out.put(stages[j].at[pl.ds(at, rows), :], ref)
    out.wait()


def run_up(where, att, tokens, vec, fc1_b, ups):
    nz = lax.axis_size("z")
    rows, width = tokens.shape
    ff = fc1_b.shape[1]
    flat = [block for blocks in att for block in blocks]
    big = (rows, width)
    outs = [(big, BF16), (big, F32), (big, F32), (big, BF16), ((rows, ff), F32), ((rows, ff), BF16)]
    return call(
        functools.partial(up_kernel, nz=nz, n_att=len(att), n_pieces=len(ups)),
        "up",
        where,
        flat + [tokens, vec, fc1_b] + ups,
        [VMEM] * (len(flat) + 3) + [ANY] * len(ups),
        outs,
        [
            pltpu.VMEM((2, width, width // 2), BF16),
            pltpu.VMEM((2, width, ff // 2), BF16),
        ]
        + [pltpu.VMEM(shape, dtype) for shape, dtype in outs]
        + [pltpu.SemaphoreType.DMA((n_copies(ups, 2),)), pltpu.SemaphoreType.DMA((4 + 2 * (ff // 512),))],
        out_specs=[ANY] * len(outs),
        cost=cost_of(20),
    )


def run_mid(where, active, residual, hidden, out_grad, vec, downs):
    nz = lax.axis_size("z")
    rows, width = out_grad.shape
    ff = active.shape[1]
    big = (rows, width)
    return call(
        functools.partial(mid_kernel, nz=nz, n_pieces=len(downs)),
        "mid",
        where,
        [active, residual, hidden, out_grad, vec] + downs,
        [ANY] * 3 + [VMEM] * 2 + [ANY] * len(downs),
        [(big, BF16), (big, BF16), ((rows, ff), BF16), ((16, width), F32), ((1, ff), F32)],
        [
            pltpu.VMEM((2, ff, width // 2), BF16),
            pltpu.VMEM((rows, ff), BF16),
            pltpu.VMEM(big, F32),
            pltpu.VMEM(big, F32),
            pltpu.VMEM((rows, ff), F32),
            pltpu.VMEM((rows, ff), BF16),
            pltpu.SemaphoreType.DMA((n_copies(downs, ff // width),)),
            pltpu.SemaphoreType.DMA((2 + ff // 512,)),
            pltpu.SemaphoreType.DMA((ff // 512,)),
        ],
        out_specs=[VMEM] * 2 + [ANY] + [VMEM] * 2,
        cost=cost_of(28),
    )


def run_back(where, out_grad, vec, sums, d_hidden, residual, branch, ups, n_att):
    nz = lax.axis_size("z")
    rows, width = out_grad.shape
    ff = d_hidden.shape[1]
    big = (rows, width)
    part = width // N_SEQ // n_att
    outs = [(big, F32), (big, BF16), ((16, width), F32)]
    outs += [((rows, part), BF16)] * (n_att * N_SEQ)
    return call(
        functools.partial(back_kernel, nz=nz, n_att=n_att, n_pieces=len(ups)),
        "back",
        where,
        [out_grad, vec, sums, d_hidden, residual, branch] + ups,
        [VMEM] * 3 + [ANY] * (3 + len(ups)),
        outs,
        [
            pltpu.VMEM((2, width, width // 2), BF16),
            pltpu.VMEM((2, width, ff // 2), BF16),
            pltpu.VMEM((rows, ff), BF16),
            pltpu.VMEM(big, F32),
            pltpu.VMEM(big, F32),
            pltpu.VMEM(big, F32),
            pltpu.VMEM(big, F32),
            pltpu.VMEM(big, BF16),
        ]
        + [pltpu.VMEM((N_SEQ * rows, part), BF16)] * n_att
        + [
            pltpu.SemaphoreType.DMA((n_copies(ups, 2),)),
            pltpu.SemaphoreType.DMA((4,)),
            pltpu.SemaphoreType.DMA((2 + n_att * N_SEQ,)),
        ],
        out_specs=[ANY] * 2 + [VMEM] + [ANY] * (n_att * N_SEQ),
        cost=cost_of(20),
    )


def slot_owner(i, nz, where):
    z, x = where[0], where[1]
    return lax.rem(z + 2 * nz - 1 - i % nz, nz) * 2 + (1 - x if i < nz else x)


def contract_rows(left, right):
    return lax.dot_general(left, right, (((0,), (0,)), ((), ())), preferred_element_type=F32)


def halves_of(ref, c):
    half = ref.shape[1] // 2
    return [ref[:, pl.ds(pl.multiple_of(h * half, half), half)] for h in (1 - c, c)]


def columns_of(ref, owner, count):
    return ref[:, pl.ds(pl.multiple_of(owner * count, count), count)]


def row_grad_kernel(where, lhs, rhs, *outs, nz):
    c = where[2]
    rows = outs[0].shape[1]
    half = rhs.shape[1] // 2
    blk = min(1024, half)
    for side in range(2):
        owners = [slot_owner(side * nz + i, nz, where) for i in range(nz)]
        left = jnp.concatenate([columns_of(lhs, o, rows) for o in owners], axis=1)
        for h in range(2):
            out = outs[2 * side + h]
            base = (1 - c if h == 0 else c) * half
            for n in range(half // blk):
                right = rhs[:, pl.ds(pl.multiple_of(base + n * blk, blk), blk)]
                low = contract_rows(left, right).astype(BF16)
                for i in range(nz):
                    out[i, :, n * blk : (n + 1) * blk] = low[i * rows : (i + 1) * rows]


def wide_grad_kernel(where, *refs, nz, side):
    ins, outs = refs[:4], refs[4:6]
    normed_two, d_hidden, active, d_second = refs[6:10]
    stages, in_sems, out_sems = refs[10:12], refs[12], refs[13]
    c = where[2]
    rows = outs[0].shape[1]
    owners = [slot_owner(side * nz + i, nz, where) for i in range(nz)]
    half = d_hidden.shape[1] // 2
    blk = min(1024, half)
    loads = [pltpu.make_async_copy(ins[0], normed_two, in_sems.at[0])]
    for k, h in enumerate((1 - c, c)):
        at = pl.ds(pl.multiple_of(h * half, half), half)
        loads.append(pltpu.make_async_copy(ins[1].at[:, at], d_hidden.at[:, at], in_sems.at[1 + k]))
    loads.append(pltpu.make_async_copy(ins[3], d_second, in_sems.at[3]))
    wide = active.shape[1] // (2 * nz)
    for i in range(nz):
        at = pl.ds(pl.multiple_of(owners[i] * wide, wide), wide)
        loads.append(pltpu.make_async_copy(ins[2].at[:, at], active.at[:, at], in_sems.at[4 + i]))
    for load in loads:
        load.start()
    write = Writer(out_sems)
    loads[0].wait()
    left = jnp.concatenate([columns_of(normed_two, o, rows) for o in owners], axis=1)
    for h, out in enumerate(stages):
        loads[1 + h].wait()
        base = (1 - c if h == 0 else c) * half
        for n in range(half // blk):
            right = d_hidden[:, pl.ds(pl.multiple_of(base + n * blk, blk), blk)]
            low = contract_rows(left, right).astype(BF16)
            for i in range(nz):
                out[i, :, n * blk : (n + 1) * blk] = low[i * rows : (i + 1) * rows]
    loads[3].wait()
    rights = halves_of(d_second, c)
    cols = d_second.shape[1] // 2
    for i in range(nz):
        loads[4 + i].wait()
        left = columns_of(active, owners[i], wide)
        for stage, out, right in zip(stages, outs, rights):
            low = contract_rows(left, right).astype(BF16)
            for g in range(wide // rows):
                lo = half + g * cols
                stage[i, :, lo : lo + cols] = low[g * rows : (g + 1) * rows]
            write.put(stage.at[i], out.at[i])
    write.wait()


def run_wide_grad(where, normed_two, d_hidden, active, d_second, rows, side):
    nz = lax.axis_size("z")
    tok, width = normed_two.shape
    ff = active.shape[1]
    out = ((nz, rows, ff // 2 + ff // width * width // 2), BF16)
    return call(
        functools.partial(wide_grad_kernel, nz=nz, side=side),
        "wide_grad",
        where,
        (normed_two, d_hidden, active, d_second),
        [ANY] * 4,
        [out] * 2,
        [
            pltpu.VMEM((tok, width), BF16),
            pltpu.VMEM((tok, ff), BF16),
            pltpu.VMEM((tok, ff), BF16),
            pltpu.VMEM((tok, width), BF16),
            pltpu.VMEM(*out),
            pltpu.VMEM(*out),
            pltpu.SemaphoreType.DMA((4 + nz,)),
            pltpu.SemaphoreType.DMA((2 * nz,)),
        ],
        out_specs=[ANY] * 2,
        cost=cost_of(9),
    )


def grads(kernel, name, where, args, rows, half, specs=None, scratch=(), count=4, **more):
    nz = lax.axis_size("z")
    return call(
        functools.partial(kernel, nz=nz, **more),
        name,
        where,
        args,
        specs or [VMEM] * len(args),
        [((nz, rows, half), BF16)] * count,
        scratch,
        cost=cost_of(2.5 * count),
    )


def qkv_grad_kernel(where, normed, *refs, nz):
    blocks, outs, (stage, sems) = refs[:N_SEQ], refs[N_SEQ:-2], refs[-2:]
    c = where[2]
    rows = outs[0].shape[1]
    tok = normed.shape[0]
    per_side = N_SEQ // 2
    run_copies(by_source(where, blocks, stage, sems))
    for h in range(2):
        base = (1 - c if h == 0 else c) * per_side
        right = jnp.concatenate(
            [stage[pl.ds(pl.multiple_of((base + j) * tok, tok), tok), :] for j in range(per_side)], axis=1
        )
        for side in range(2):
            owners = [slot_owner(side * nz + i, nz, where) for i in range(nz)]
            left = jnp.concatenate([columns_of(normed, o, rows) for o in owners], axis=1)
            low = contract_rows(left, right).astype(BF16)
            for i in range(nz):
                outs[2 * side + h][i] = low[i * rows : (i + 1) * rows]


class Reduce:
    def __init__(self, stages, parts):
        self.stages, self.parts_x = stages, parts
        self.box = stages.box
        self.from_x, self.out = [], []
        self.steps = 0

    def set_first(self, outs):
        self.first = self.stages.boxes(outs)

    def set_second(self, outs):
        self.second = self.stages.boxes(outs)

    def c_first(self):
        self.got = self.box(lax.ppermute(self.first[0].v, "c", SWAP))

    def c_second(self):
        self.own_got = self.box(lax.ppermute(self.second[0].v, "c", SWAP))

    def c(self):
        self.c_first()
        self.c_second()

    def sum(self, count=1):
        got, kept = self.got.v, self.first[1].v
        self.size = got.shape[0] // self.parts_x
        for unused in range(count):
            at = len(self.out) * self.size
            self.out.append(self.box(add_low(kept[at : at + self.size], got[at : at + self.size])))

    def x(self):
        if len(self.out) == len(self.from_x):
            self.sum()
        self.from_x.append(self.box(lax.ppermute(self.out[len(self.from_x)].v, "x", SWAP)))

    def add(self):
        step = self.steps
        ready = [self.from_x[step // self.size]] + ([self.passed] if step > 0 else [])
        ready = self.stages.begin(*ready)
        terms = [self.second[1].v[step], self.own_got.v[step], ready[0][step % self.size]] + ready[1:]
        self.cur = self.box(add_low(*terms))
        self.steps += 1

    def z(self):
        self.add()
        self.passed = self.box(lax.ppermute(self.cur.v, "z", ring(lax.axis_size("z"))))
        return self.passed

    def direct(self):
        nz = lax.axis_size("z")
        (crossed,) = self.stages.begin(self.from_x[0])
        blocks = [add_low(self.second[1].v[i], self.own_got.v[i], crossed[i]) for i in range(nz)]
        self.kept = blocks[-1]
        self.parts = [
            self.box(lax.ppermute(blocks[i], "z", [(s, (s - 1 - i) % nz) for s in range(nz)]))
            for i in range(nz - 1)
        ]
        return self.parts

    def gather_parts(self):
        self.cur = self.box(add_low(self.kept, *self.stages.begin(*self.parts)))

    def y(self):
        if hasattr(self, "parts"):
            self.gather_parts()
        else:
            self.add()
        self.from_y = self.box(lax.ppermute(self.cur.v, "y", SWAP))
        return self.from_y

    def last_c(self):
        (got,) = self.stages.begin(self.from_y)
        self.low = add_low(self.cur.v, got)
        self.other = self.box(lax.ppermute(self.low, "c", SWAP))
        return self.other

    def finish(self):
        c = lax.axis_index("c")
        low, (other,) = self.low, self.stages.begin(self.other)
        return jnp.where(c == 0, low, other), jnp.where(c == 0, other, low)


class SmallReduce:
    def __init__(self, stages, grads):
        self.stages, self.box = stages, stages.box
        self.cur = self.box(grads.astype(BF16))

    def seq(self):
        (cur,) = self.stages.begin(self.cur)
        both = [(i, i ^ 3) for i in range(4)]
        self.parts = [
            self.box(lax.ppermute(cur, "c", SWAP)),
            self.box(lax.ppermute(cur, "y", SWAP)),
            self.box(lax.ppermute(cur, SEQ_AXES, both)),
        ]
        return self.parts

    def x(self):
        nz = lax.axis_size("z")
        cur = add_low(self.cur.v, *self.stages.begin(*self.parts))
        self.keep = cur[nz:]
        self.got = self.box(lax.ppermute(cur[:nz], "x", SWAP))
        return [self.got]

    def z(self):
        nz = lax.axis_size("z")
        (got,) = self.stages.begin(self.got)
        cur = add_low(self.keep, got)
        self.keep = cur[nz - 1]
        self.parts = [
            self.box(lax.ppermute(cur[i], "z", [(s, (s - 1 - i) % nz) for s in range(nz)]))
            for i in range(nz - 1)
        ]
        return self.parts

    def finish(self):
        return add_low(self.keep, *self.stages.begin(*self.parts)).astype(F32)


def reduce_plain(lhs, rhs):
    grad = lax.dot_general(
        lhs, rhs, (((0,), (0,)), ((), ())), preferred_element_type=F32
    ).astype(BF16)
    part = lax.psum_scatter(grad, DP_AXES, scatter_dimension=0, tiled=True)
    return lax.psum(part, SEQ_AXES).astype(F32)


def last_kernel(where, *refs, nz, chunks, n_pieces, rings):
    refs = list(refs)
    blocks = [[refs.pop(0) for _ in range(N_SEQ)] for _ in range(chunks)]
    tok, d_residual, vec, sums, fc1_sum = [refs.pop(0) for _ in range(5)]
    pieces = [refs.pop(0) for _ in range(n_pieces)]
    tokens_grad, small = refs.pop(0), refs.pop(0)
    ws = [refs.pop(0) for _ in range(chunks)]
    stages = [refs.pop(0) for _ in range(chunks)]
    wide, total, in_sems = refs.pop(0), refs.pop(0), refs.pop(0)
    loads = [
        Loader(where, pieces, [w], sem, nz, j * w.shape[2]) for j, (w, sem) in enumerate(zip(ws, refs))
    ]
    for load in loads:
        load.start()
    rows, width = tok.shape
    n_seq, cols = N_SEQ, stages[0].shape[1]
    run_copies(
        [copy for j in range(chunks) for copy in by_source(where, blocks[j], stages[j], in_sems.at[j])]
    )
    d_mixed = [stage.reshape(n_seq, rows, cols) for stage in stages]
    part = cols // 3
    zero = jnp.zeros((1, width), F32)
    total[...] = sums[...]
    for j in range(chunks):
        for s in range(n_seq):
            lo = (s * chunks + j) * part
            total[0:1, lo : lo + part] = rowsum(d_mixed[j][s, :, 0:part].astype(F32))
            total[1:2, lo : lo + part] = rowsum(d_mixed[j][s, :, 2 * part :].astype(F32))
    for load in loads:
        load.wait()
    quarter = width // 4
    per_side = n_seq // 2
    for q in range(4):
        at = slice(q * quarter, (q + 1) * quarter)
        acc = None
        for j in range(chunks):
            for side in range(2):
                left = jnp.concatenate([d_mixed[j][side * per_side + i] for i in range(per_side)], axis=1)
                term = _nt(left, ws[j][side, at, :])
                acc = term if acc is None else acc + term
        wide[:, at] = acc
    step = min(64, rows)

    def norms(i, carry):
        g, s = carry
        at = pl.ds(pl.multiple_of(i * step, step), step)
        e = wide[at, :]
        n, inv = norm_parts(tok[at, :].astype(F32))
        tokens_grad[at, :] = (d_residual[at, :] + norm_back(n, inv, vec[4:5, :], e)).astype(BF16)
        return g + rowsum(e * n), s + rowsum(e)

    g, s = lax.fori_loop(0, rows // step, norms, (zero, zero))
    total[4:5, :] = g
    total[8:9, :] = s
    if not rings:
        small[...] = total[...]
        return
    z, x = where[0], where[1]
    own = width // (2 * nz)
    n_bias = fc1_sum.shape[1] // width
    for o in range(2 * nz):
        slot = lax.rem(z + 2 * nz - 1 - o // 2, nz) + jnp.where(x == o % 2, nz, 0)
        small[slot, 0:N_VEC, :] = total[0:N_VEC, o * own : (o + 1) * own]
        for j in range(n_bias):
            lo = (o * n_bias + j) * own
            small[slot, N_VEC + j : N_VEC + j + 1, :] = fc1_sum[:, lo : lo + own]


def last(where, d_mixed, tokens, d_residual, vec, sums, fc1_sum, pieces):
    nz = lax.axis_size("z")
    rings = uses_rings()
    rows, width = tokens.shape
    chunks = len(d_mixed)
    small = ((2 * nz, N_VEC + fc1_sum.shape[1] // width, width // (2 * nz)), F32) if rings else ((16, width), F32)
    return call(
        functools.partial(last_kernel, nz=nz, chunks=chunks, n_pieces=len(pieces), rings=rings),
        "last",
        where,
        [b for blocks in d_mixed for b in blocks] + [tokens, d_residual, vec, sums, fc1_sum] + list(pieces),
        [ANY] * (chunks * N_SEQ) + [VMEM] * 5 + [ANY] * len(pieces),
        [((rows, width), BF16), small],
        [pltpu.VMEM((2, width, 3 * width // chunks // 2), BF16)] * chunks
        + [pltpu.VMEM((N_SEQ * rows, 3 * width // chunks // N_SEQ), BF16)] * chunks
        + [pltpu.VMEM((rows, width), F32), pltpu.VMEM((16, width), F32), pltpu.SemaphoreType.DMA((chunks, N_SEQ))]
        + [pltpu.SemaphoreType.DMA((n_copies(pieces),))] * chunks,
        cost=cost_of(12),
    )


def reduce_small(small, fc1_sum, own):
    n_dp = lax.axis_size("z") * lax.axis_size("x")
    low = jnp.concatenate(
        (small[:N_VEC].reshape(N_VEC, n_dp, own).transpose(1, 0, 2), fc1_sum.reshape(n_dp, -1, own)),
        axis=1,
    )
    part = lax.psum_scatter(low, DP_AXES, scatter_dimension=0, tiled=False)
    return lax.psum(part.astype(BF16), SEQ_AXES).astype(F32)


def exchange(blocks):
    both = [(i, i ^ 3) for i in range(4)]
    return [
        blocks[0],
        lax.ppermute(blocks[1], "c", SWAP),
        lax.ppermute(blocks[2], "y", SWAP),
        lax.ppermute(blocks[3], SEQ_AXES, both),
    ]


def per_device(
    tokens,
    out_grad,
    qkv_weight,
    qv_bias,
    proj_weight,
    fc1_weight,
    fc1_bias,
    fc2_weight,
    out_bias,
    norm_gains,
    norm_shifts,
):
    n_seq = lax.axis_size("y") * lax.axis_size("c")
    rows, width = tokens.shape
    own = qv_bias.shape[1]
    chunks = CHUNKS
    grp = width // n_seq
    part = grp // chunks
    heads = part // HD
    seq_len = n_seq * rows
    nz = lax.axis_size("z")
    where = here()
    qkv_shards = qkv_weight.reshape(-1, 3, n_seq, chunks, part).transpose(3, 0, 2, 1, 4)
    qkv_shards = qkv_shards.reshape(chunks, -1, 3 * width // chunks)
    small = jnp.concatenate(
        (qv_bias, out_bias, norm_gains, norm_shifts, fc1_bias.reshape(-1, own)), axis=0
    )
    rings = uses_rings()
    st = Stages()
    ff = fc1_weight.shape[1]
    r = proj_weight.shape[0]
    qkv_cat = jnp.concatenate([in_halves(w) for w in qkv_shards], axis=2)
    groups = fc2_weight.shape[0] // r
    if rings:
        fc2_groups = fc2_weight.reshape(groups, -1, 2, width // 2).transpose(2, 1, 0, 3)
        n_bias = small.shape[0] - N_VEC
        columns = jnp.pad(small.T, ((0, 0), (0, own - small.shape[0])))
        qkv_in = Gather(st, jnp.concatenate((qkv_cat, jnp.stack((columns, columns))), axis=2))
        up_in = Gather(st, jnp.concatenate((in_halves(proj_weight), in_halves(fc1_weight)), axis=2))
        down_in = Gather(st, fc2_groups.reshape(2, -1, groups * width // 2))
        for step in range(nz):
            if step > 0:
                st.sync()
                qkv_in.c()
            qkv_in.x()
            if step < nz - 1:
                qkv_in.z()
            else:
                up_in.z()
        st.sync()
        qkv_pieces = qkv_in.pieces()
        vec, fc1_b = small_vectors(qkv_pieces, width, n_bias)
    else:
        vec, fc1_b = plain_vectors(small, width)
        whole = lax.all_gather(qkv_cat, DP_AXES, axis=1, tiled=True)
        qkv_pieces = [jnp.concatenate((whole[0], whole[1]), axis=1)]
        ups, downs = [
            [lax.all_gather(w, DP_AXES, axis=0, tiled=True) for w in ws]
            for ws in ((proj_weight, fc1_weight), (fc2_weight,))
        ]

    def project(j, first, vec):
        outs = [((rows, 3 * part), BF16)] * n_seq
        if j == 0:
            outs.append(((rows, width), BF16))
        return call(
            functools.partial(qkv_kernel, nz=nz, chunk=j, chunks=chunks, n_pieces=len(qkv_pieces)),
            "qkv",
            where,
            [first, vec] + qkv_pieces,
            [VMEM] * 2 + [ANY] * len(qkv_pieces),
            outs,
            [
                pltpu.VMEM((2, width, 3 * width // chunks // 2), BF16),
                pltpu.VMEM((seq_len, 3 * part), BF16),
                pltpu.SemaphoreType.DMA((n_copies(qkv_pieces),)),
                pltpu.SemaphoreType.DMA((n_seq,)),
            ],
            out_specs=[ANY] * n_seq + [VMEM] * (j == 0),
            cost=cost_of(7),
        )

    def swap(blocks):
        return st.boxes(exchange(st.begin(*blocks)))

    def hops(*some):
        for hop in some if rings else []:
            hop()

    vec_box = st.box(vec)
    st.sync()
    vec = vec_box.v
    if not rings:
        up_in = down_in = Gather(st, qkv_cat)
    got = st.boxes(project(0, tokens, vec_box.v))
    sent_a, normed_box = got[:n_seq], got[n_seq]
    hops(up_in.x, up_in.z)
    st.sync()
    normed = normed_box.v
    heads_a = swap(sent_a)
    sent_b = st.boxes(project(1, normed, vec))
    hops(up_in.x, up_in.z)
    st.sync()
    heads_b = swap(sent_b)
    by_a = st.begin(*heads_a)
    out_a, cols_a, lse_a = attn_fwd(where, by_a, heads, 1024)
    out_a = st.boxes(out_a)
    hops(up_in.x, down_in.z)
    st.sync()
    att_a = swap(out_a)
    by_b = st.begin(*heads_b)
    out_b, cols_b, lse_b = attn_fwd(where, by_b, heads, 1024)
    out_b = st.boxes(out_b)
    hops(up_in.x, down_in.z)
    st.sync()
    att_b = swap(out_b)
    hops(down_in.x, down_in.x, down_in.z)
    st.sync()
    if rings:
        ups = up_in.pieces()
    hops(down_in.c, down_in.x, down_in.x)
    arrived = st.begin(*att_a, *att_b)
    kept = run_up(where, [arrived[:n_seq], arrived[n_seq:]], tokens, vec, fc1_b, ups)
    attended, branch, residual, normed_two, hidden, active = kept
    active_box = st.box(active)
    st.sync()
    if rings:
        downs = down_in.pieces()
    active = active_box.v
    layer_out, d_second, d_hidden, sums, fc1_sum = run_mid(
        where, active, residual, hidden, out_grad, vec, downs
    )

    hidden_box = st.box(d_hidden)

    def reduction(outs, parts):
        flow = Reduce(st, parts)
        flow.set_first(outs[:2])
        flow.set_second(outs[2:])
        return flow

    if rings:
        wide = Reduce(st, nz)

        def wide_grads(side):
            return run_wide_grad(where, normed_two, hidden_box.v, active, d_second, r, side)

        wide.set_first(wide_grads(0))
        st.sync()
        wide.c_first()
        wide.set_second(wide_grads(1))
        st.sync()
        wide.sum()
        st.sync()
        hops(wide.x, wide.c_second)
    else:
        grad_fc2 = reduce_plain(active, d_second)
        grad_fc1 = reduce_plain(normed_two, d_hidden)
    outs = run_back(where, out_grad, vec, sums, hidden_box.v, residual, branch, ups, chunks)
    d_residual, d_branch, sums = outs[:3]
    branch_box = st.box(d_branch)
    d_out = st.boxes(outs[3:])
    st.sync()
    d_heads_a = swap(d_out[:n_seq])
    d_branch = branch_box.v
    if rings:
        wide.sum(nz - 1)
        proj = reduction(
            grads(row_grad_kernel, "proj_grad", where, (attended, d_branch), r, width // 2), 1
        )
    else:
        grad_proj = reduce_plain(attended, d_branch)
    st.sync()
    hops(*([wide.x, wide.z] if rings else []))
    d_heads_b = swap(d_out[n_seq:])
    d_by_a = st.boxes(attn_bwd(where, by_a, st.begin(*d_heads_a), cols_a, lse_a, heads, 512))
    st.sync()
    d_mixed_a = swap(d_by_a)
    hops(*([wide.x, wide.z] if rings else []))
    d_by_b = st.boxes(attn_bwd(where, by_b, st.begin(*d_heads_b), cols_b, lse_b, heads, 512))
    st.sync()
    d_mixed_b = swap(d_by_b)
    hops(*([wide.x, wide.z] if rings else []))

    def qkv_grads(d_mixed):
        outs = grads(
            qkv_grad_kernel,
            "qkv_grad",
            where,
            [normed] + st.begin(*d_mixed),
            r,
            n_seq // 2 * 3 * part,
            [VMEM] + [ANY] * n_seq,
            [pltpu.VMEM((seq_len, 3 * part), BF16), pltpu.SemaphoreType.DMA((n_seq,))],
        )
        return reduction(outs, 1)

    if rings:
        qkv_a = qkv_grads(d_mixed_a)
        st.sync()
        hops(qkv_a.c)
        st.sync()
        hops(qkv_a.x, wide.y)
        qkv_b = qkv_grads(d_mixed_b)
        st.sync()
        hops(qkv_b.c, proj.c)
        st.sync()
        hops(qkv_b.x, qkv_a.direct, proj.x)
    both = st.begin(*d_mixed_a, *d_mixed_b)
    d_mixed_a, d_mixed_b = both[:n_seq], both[n_seq:]
    tokens_grad, small_grads = last(
        where, [d_mixed_a, d_mixed_b], tokens, d_residual, vec, sums, fc1_sum, qkv_pieces
    )
    if rings:
        vecs = SmallReduce(st, small_grads)
        st.sync()
        hops(qkv_b.direct, qkv_a.y, wide.last_c)
        st.sync()
        hops(vecs.seq, qkv_b.y, qkv_a.last_c, proj.direct)
        st.sync()
        hops(qkv_b.last_c, vecs.x, proj.y)
        st.sync()
        hops(vecs.z, proj.last_c)
        total_small = vecs.finish()
    else:
        total_small = reduce_small(small_grads, fc1_sum, own)
    if rings:
        low = wide.finish()
        at = ff // 2
        grad_fc1 = jnp.concatenate([half[:, :at] for half in low], axis=1).astype(F32)
        grad_fc2 = jnp.stack([half[:, at:] for half in low]).reshape(2, r, groups, width // 2)
        grad_fc2 = grad_fc2.transpose(2, 1, 0, 3).reshape(groups * r, width).astype(F32)
        grad_proj = jnp.concatenate(proj.finish(), axis=1).astype(F32)
        total_qkv = [jnp.concatenate(f.finish(), axis=1).astype(F32) for f in (qkv_a, qkv_b)]
    else:
        total_qkv = []
        order = jnp.stack([jnp.bitwise_xor(where[3], i) for i in range(n_seq)])
        for d_mixed in (d_mixed_a, d_mixed_b):
            blocks = jnp.take(jnp.stack(d_mixed), order, axis=0)
            total_qkv.append(reduce_plain(normed, blocks.transpose(1, 0, 2).reshape(rows, -1)))
    qkv_grad = jnp.stack([t.reshape(-1, n_seq, 3, part) for t in total_qkv])
    qkv_grad = qkv_grad.transpose(1, 3, 2, 0, 4).reshape(-1, 3 * width)
    return (
        layer_out,
        tokens_grad,
        qkv_grad,
        total_small[0:2],
        grad_proj,
        grad_fc1,
        total_small[N_VEC:].reshape(-1),
        grad_fc2,
        total_small[2:4],
        total_small[4:8],
        total_small[8:12],
    )


CHUNKS = 2


def solution(mesh):
    n_dp, n_seq = mesh.devices.shape
    fine = Mesh(mesh.devices.reshape(n_dp // 2, 2, n_seq // 2, 2), DP_AXES + SEQ_AXES)
    tok = P(DP_AXES + SEQ_AXES, None)
    by_row = P(DP_AXES, None)
    by_col = P(None, DP_AXES)
    weights = (by_row, by_col, by_row, by_row, P(DP_AXES), by_row, by_col, by_col, by_col)
    return jax.shard_map(
        per_device,
        mesh=fine,
        in_specs=(tok, tok) + weights,
        out_specs=(tok, tok) + weights,
        check_vma=False,
    )
```

```python
import functools
import math

import jax
import jax.numpy as jnp
from jax.sharding import Mesh
from jax.sharding import PartitionSpec as P
from jax import lax
from jax.experimental import pallas as pl
from jax.experimental.pallas import tpu as pltpu
HD=64
RELAX=32.0
C2=RELAX*math.log2(math.e)
NEG=-1e30

def _nt(a,b):
    return lax.dot_general(a,b,(((1,),(1,)),((),())),preferred_element_type=jnp.float32)
def _nn(a,b):
    return lax.dot_general(a,b,(((1,),(0,)),((),())),preferred_element_type=jnp.float32)

def _tr(x):
    return jnp.transpose(x.astype(jnp.float32)).astype(jnp.bfloat16)

def by_source(where, refs, dst, sems):
    rows = refs[0].shape[0]
    copies = []
    for i, ref in enumerate(refs):
        at = pl.multiple_of(jnp.bitwise_xor(where[3], i) * rows, rows)
        copies.append(pltpu.make_async_copy(ref, dst.at[pl.ds(at, rows), :], sems.at[i]))
    return copies

def by_target(where, src, refs, sems):
    rows = refs[0].shape[0]
    copies = []
    for i, ref in enumerate(refs):
        at = pl.multiple_of(jnp.bitwise_xor(where[3], i) * rows, rows)
        copies.append(pltpu.make_async_copy(src.at[pl.ds(at, rows), :], ref, sems.at[i]))
    return copies

def run_copies(copies):
    for copy in copies:
        copy.start()
    for copy in copies:
        copy.wait()

def fwd_kernel(where,*refs,nh,blk,n):
    ins,outs=refs[:n],refs[n:2*n]
    ot_ref,lse_ref,vt_ref,qkv_ref,o_ref,sems=refs[2*n:]
    seq=qkv_ref.shape[0]; w=nh*HD
    nb=seq//blk
    run_copies(by_source(where,ins,qkv_ref,sems))
    q_ref,k_ref,v_ref=(qkv_ref.at[:,i*w:(i+1)*w] for i in range(3))
    for b in range(nb):
        vt_ref[:,b*blk:(b+1)*blk]=_tr(v_ref[b*blk:(b+1)*blk,:])
    lane=lax.broadcasted_iota(jnp.int32,(1,w),1)//HD
    tri=lax.broadcasted_iota(jnp.int32,(blk,blk),0)<=lax.broadcasted_iota(jnp.int32,(blk,blk),1)
    def qstep(qb,_):
        q0=pl.multiple_of(qb*blk,blk)
        q=q_ref[pl.ds(q0,blk),:]
        qm=[jnp.where(lane==h,q,jnp.zeros_like(q)) for h in range(nh)]
        def kv(kb,carry,diag):
            k0=pl.multiple_of(kb*blk,blk)
            k=k_ref[pl.ds(k0,blk),:]
            out=[]
            for h in range(nh):
                m,l,acc=carry[3*h:3*h+3]
                s=_nt(k,qm[h])*C2
                if diag: s=jnp.where(tri,s,NEG)
                mn=jnp.maximum(m,jnp.max(s,axis=0,keepdims=True))
                a=jnp.exp2(m-mn)
                p=jnp.exp2(s-mn)
                l=l*a+jnp.sum(p,axis=0,keepdims=True)
                acc=acc*a+_nn(vt_ref[h*HD:(h+1)*HD,pl.ds(k0,blk)],p.astype(jnp.bfloat16))
                out+= [mn,l,acc]
            return tuple(out)
        init=[]
        for h in range(nh):
            init+=[jnp.full((1,blk),NEG,jnp.float32),jnp.zeros((1,blk),jnp.float32),jnp.zeros((HD,blk),jnp.float32)]
        c=kv(qb,tuple(init),True)
        c=lax.fori_loop(0,qb,lambda kb,cc: kv(kb,cc,False),c)
        for h in range(nh):
            m,l,acc=c[3*h:3*h+3]
            ot_ref[h*HD:(h+1)*HD,pl.ds(q0,blk)]=acc/l
            lse_ref[h:h+1,pl.ds(q0,blk)]=m+jnp.log2(l)
        o_ref[pl.ds(q0,blk),:]=jnp.transpose(ot_ref[:,pl.ds(q0,blk)]).astype(jnp.bfloat16)
        return 0
    lax.fori_loop(0,nb,qstep,0)
    run_copies(by_target(where,o_ref,outs,sems))

def attn_fwd(where, qkv, nh, blk=512):
    n=len(qkv); rows=qkv[0].shape[0]
    seq=n*rows; w=nh*HD
    blk=min(blk,seq)
    vm=pl.BlockSpec(memory_space=pltpu.VMEM)
    an=pl.BlockSpec(memory_space=pl.ANY)
    outs=pl.pallas_call(functools.partial(fwd_kernel,nh=nh,blk=blk,n=n),
      grid_spec=pltpu.PrefetchScalarGridSpec(num_scalar_prefetch=1,
        in_specs=[an]*n,out_specs=[an]*n+[vm]*2,
        scratch_shapes=[pltpu.VMEM((w,seq),jnp.bfloat16),pltpu.VMEM((seq,3*w),jnp.bfloat16),pltpu.VMEM((seq,w),jnp.bfloat16),pltpu.SemaphoreType.DMA((n,))]),
      out_shape=[jax.ShapeDtypeStruct((rows,w),jnp.bfloat16)]*n+[jax.ShapeDtypeStruct((w,seq),jnp.float32),jax.ShapeDtypeStruct((8,seq),jnp.float32)],
      compiler_params=pltpu.CompilerParams(vmem_limit_bytes=48<<20),
      cost_estimate=pl.CostEstimate(flops=int(nh*4.5*1.1e9), transcendentals=0, bytes_accessed=1<<20),
      name="attn_fwd")(where,*qkv)
    return outs[:n],outs[n],outs[n+1]

def bwd_kernel(where,*refs,nh,blk,n):
    ins,dos,outs=refs[:n],refs[n:2*n],refs[2*n+2:3*n+2]
    ot_ref,lse_ref=refs[2*n:2*n+2]
    kt_ref,dl_ref,dqt_ref,qkv_ref,do_ref,d_ref,sems,do_sems=refs[3*n+2:]
    seq=qkv_ref.shape[0]; w=nh*HD
    nb=seq//blk
    run_copies(by_source(where,ins,qkv_ref,sems)+by_source(where,dos,do_ref,do_sems))
    q_ref,k_ref,v_ref=(qkv_ref.at[:,i*w:(i+1)*w] for i in range(3))
    for b in range(nb):
        sl=slice(b*blk,(b+1)*blk)
        kt_ref[:,sl]=_tr(k_ref[sl,:])
        dot_=jnp.transpose(do_ref[sl,:].astype(jnp.float32))
        pr=dot_*ot_ref[:,sl]
        for h in range(nh):
            dl_ref[h:h+1,sl]=jnp.sum(pr[h*HD:(h+1)*HD],axis=0,keepdims=True)
    dqt_ref[...]=jnp.zeros_like(dqt_ref)
    lane=lax.broadcasted_iota(jnp.int32,(1,w),1)//HD
    tri=lax.broadcasted_iota(jnp.int32,(blk,blk),0)<=lax.broadcasted_iota(jnp.int32,(blk,blk),1)
    def kstep(kb,_):
        k0=pl.multiple_of(kb*blk,blk)
        k=k_ref[pl.ds(k0,blk),:]
        v=v_ref[pl.ds(k0,blk),:]
        def qs(qb,carry,diag):
            dk,dv=carry
            q0=pl.multiple_of(qb*blk,blk)
            q=q_ref[pl.ds(q0,blk),:]
            do=do_ref[pl.ds(q0,blk),:]
            for h in range(nh):
                qm=jnp.where(lane==h,q,jnp.zeros_like(q))
                dom=jnp.where(lane==h,do,jnp.zeros_like(do))
                s=_nt(k,qm)
                dp=_nt(v,dom)
                p=jnp.exp2(s*C2-lse_ref[h:h+1,pl.ds(q0,blk)])
                if diag: p=jnp.where(tri,p,0.0)
                ds=(p*(dp-dl_ref[h:h+1,pl.ds(q0,blk)])).astype(jnp.bfloat16)
                dv=dv+_nn(p.astype(jnp.bfloat16),dom)
                dk=dk+_nn(ds,qm)
                dqt_ref[h*HD:(h+1)*HD,pl.ds(q0,blk)]+=_nn(kt_ref[h*HD:(h+1)*HD,pl.ds(k0,blk)],ds)
            return dk,dv
        z=jnp.zeros((blk,w),jnp.float32)
        c=qs(kb,(z,z),True)
        dk,dv=lax.fori_loop(kb+1,nb,lambda qb,cc: qs(qb,cc,False),c)
        d_ref[pl.ds(k0,blk),w:2*w]=(dk*RELAX).astype(jnp.bfloat16)
        d_ref[pl.ds(k0,blk),2*w:3*w]=dv.astype(jnp.bfloat16)
        return 0
    lax.fori_loop(0,nb,kstep,0)
    for b in range(nb):
        sl=slice(b*blk,(b+1)*blk)
        d_ref[sl,0:w]=(jnp.transpose(dqt_ref[:,sl])*(1.0/math.sqrt(HD))).astype(jnp.bfloat16)
    run_copies(by_target(where,d_ref,outs,sems))

def attn_bwd(where, qkv, do, ot, lse, nh, blk=512):
    n=len(qkv); rows=qkv[0].shape[0]
    seq=n*rows; w=nh*HD
    blk=min(blk,seq)
    vm=pl.BlockSpec(memory_space=pltpu.VMEM)
    an=pl.BlockSpec(memory_space=pl.ANY)
    return pl.pallas_call(functools.partial(bwd_kernel,nh=nh,blk=blk,n=n),
      grid_spec=pltpu.PrefetchScalarGridSpec(num_scalar_prefetch=1,
        in_specs=[an]*(2*n)+[vm]*2,out_specs=[an]*n,
        scratch_shapes=[pltpu.VMEM((w,seq),jnp.bfloat16),pltpu.VMEM((8,seq),jnp.float32),pltpu.VMEM((w,seq),jnp.float32),
          pltpu.VMEM((seq,3*w),jnp.bfloat16),pltpu.VMEM((seq,w),jnp.bfloat16),pltpu.VMEM((seq,3*w),jnp.bfloat16),
          pltpu.SemaphoreType.DMA((n,)),pltpu.SemaphoreType.DMA((n,))]),
      out_shape=[jax.ShapeDtypeStruct((rows,3*w),jnp.bfloat16)]*n,
      compiler_params=pltpu.CompilerParams(vmem_limit_bytes=56<<20),
      cost_estimate=pl.CostEstimate(flops=int(nh*9.5*1.1e9), transcendentals=0, bytes_accessed=1<<20),
      name="attn_bwd")(where,*qkv,*do,ot,lse)


NORM_EPS = 1e-05
F32 = jnp.float32
BF16 = jnp.bfloat16
SWAP = [(0, 1), (1, 0)]
SEQ_AXES = ("y", "c")
DP_AXES = ("z", "x")
ANY = pl.BlockSpec(memory_space=pl.ANY)
VMEM = pl.BlockSpec(memory_space=pltpu.VMEM)
GELU_K = math.sqrt(2.0 / math.pi)
GELU_A = 0.044715
N_VEC = 12
N_SEQ = 4


def add_low(*terms):
    return sum(t.astype(F32) for t in terms).astype(BF16)


def ring(n):
    return [(i, (i + 1) % n) for i in range(n)]


def uses_rings():
    return lax.axis_size("z") * lax.axis_size("x") <= 8


def here():
    seq = lax.axis_index("y") * lax.axis_size("c") + lax.axis_index("c")
    return jnp.stack([lax.axis_index(a) for a in ("z", "x", "c")] + [seq]).astype(jnp.int32)


def call(kernel, name, where, args, specs, outs, scratch=(), grid=(), out_specs=None, cost=None):
    if out_specs is None:
        out_specs = [VMEM] * len(outs)
    return list(pl.pallas_call(
        kernel,
        grid_spec=pltpu.PrefetchScalarGridSpec(
            num_scalar_prefetch=1,
            grid=grid,
            in_specs=specs,
            out_specs=out_specs,
            scratch_shapes=list(scratch),
        ),
        out_shape=[jax.ShapeDtypeStruct(s, d) for s, d in outs],
        compiler_params=pltpu.CompilerParams(vmem_limit_bytes=60 << 20),
        cost_estimate=cost,
        name=name,
    )(where, *args))


def cost_of(microseconds):
    return pl.CostEstimate(flops=int(microseconds * 1.1e9), transcendentals=0, bytes_accessed=1 << 20)


def tie(value, *others):
    return lax.optimization_barrier((value,) + others)[0]


def together(*values):
    return list(lax.optimization_barrier(tuple(values)))


class Box:
    def __init__(self, v):
        self.v = v


class Stages:
    def __init__(self):
        self.every = []

    def box(self, v):
        self.every.append(Box(v))
        return self.every[-1]

    def boxes(self, values):
        return [self.box(v) for v in values]

    def begin(self, *some):
        return [b.v for b in some]

    def sync(self):
        for box, v in zip(self.every, together(*[b.v for b in self.every])):
            box.v = v


class Gather:
    def __init__(self, stages, shards, core_halves=True):
        self.stages, self.shards, self.core_halves = stages, shards, core_halves
        cur = shards
        if core_halves:
            cur = lax.dynamic_index_in_dim(shards, lax.axis_index("c"), 0, False)
        self.box = stages.box
        self.blocks, self.others = [self.box(cur)], []
        self.swapped = {}

    def z(self):
        (block,) = self.stages.begin(self.blocks[-1])
        self.blocks.append(self.box(lax.ppermute(block, "z", ring(lax.axis_size("z")))))
        return self.blocks[-1]

    def x(self):
        (block,) = self.stages.begin(self.blocks[len(self.others)])
        self.others.append(self.box(lax.ppermute(block, "x", SWAP)))
        return self.others[-1]

    def x_pair(self):
        block = jnp.where(lax.axis_index("y") == 0, self.blocks[0].v, self.blocks[1].v)
        self.others.append(self.box(lax.ppermute(block, "x", SWAP)))

    def y_pair(self):
        self.others.append(self.box(lax.ppermute(self.others[0].v, "y", SWAP)))

    def c(self):
        new = [b for b in self.blocks[1:] + self.others if id(b) not in self.swapped]
        for box, v in zip(new, self.stages.begin(*new)):
            self.swapped[id(box)] = self.box(lax.ppermute(v, "c", SWAP))
        return [self.swapped[id(box)] for box in new]

    def pieces(self):
        mine = [self.others[0]]
        for block, other in zip(self.blocks[1:], self.others[1:]):
            mine += [block, other]
        if not self.core_halves:
            return [self.shards] + self.stages.begin(*mine)
        self.c()
        return [self.shards] + self.stages.begin(*mine, *[self.swapped[id(b)] for b in mine])


def in_halves(weight):
    rows, cols = weight.shape
    return weight.reshape(rows, 2, cols // 2).transpose(1, 0, 2)


def owner_of(index, nz, z, x):
    step, side = (index + 1) // 2, (index + 1) % 2
    return lax.rem(z + nz - step, nz) * 2 + (x if side == 0 else 1 - x)


def paired_owner(index, nz, where):
    y = where[3] // 2
    step = y if index == 0 else 1 - y
    return lax.rem(where[0] + nz - step, nz) * 2 + 1 - where[1]


class Loader:
    def __init__(self, where, pieces, dsts, sems, nz, col=0, paired=False):
        self.copies = []
        self.sems = sems
        if len(pieces[0].shape) == 2:
            self.sides = (0, 1)
            for i, (piece, dst) in enumerate(zip(pieces, dsts)):
                half = dst.shape[2]
                for side in range(2):
                    at = side * (piece.shape[1] // 2) + col
                    self.add(i, side, piece.at[:, at : at + half], dst.at[side])
            return
        z, x, c = where[0], where[1], where[2]
        self.sides = (c, 1 - c)
        rows = pieces[0].shape[1]
        others = (len(pieces) - 1) // 2
        for i, dst in enumerate(dsts):
            half = dst.shape[2]
            groups = dst.shape[1] // (2 * nz * rows)
            for g in range(groups):
                cols = slice(col, col + half)
                col += half
                for k in range(2):
                    side = self.sides[k]
                    blocks = [(z * 2 + x, pieces[0].at[side, :, cols])]
                    for n in range(others):
                        owner = owner_of(n, nz, z, x)
                        if paired and n in (0, 2):
                            owner = paired_owner(n, nz, where)
                        blocks.append((owner, pieces[1 + k * others + n].at[:, cols]))
                    for owner, block in blocks:
                        row = pl.multiple_of((owner * groups + g) * rows, rows)
                        self.add(i, k, block, dst.at[side, pl.ds(row, rows), :])

    def add(self, i, k, src, to):
        self.copies.append((i, k, pltpu.make_async_copy(src, to, self.sems.at[len(self.copies)])))

    def pick(self, dst, half):
        return [
            copy
            for i, k, copy in self.copies
            if (dst is None or i == dst) and (half is None or k == half)
        ]

    def start(self, dst=None, half=None):
        for copy in self.pick(dst, half):
            copy.start()

    def wait(self, dst=None, half=None):
        for copy in self.pick(dst, half):
            copy.wait()


class Writer:
    def __init__(self, sems):
        self.sems, self.copies = sems, []

    def put(self, src, to):
        copy = pltpu.make_async_copy(src, to, self.sems.at[len(self.copies)])
        copy.start()
        self.copies.append(copy)

    def wait(self):
        for copy in self.copies:
            copy.wait()


def n_copies(pieces, groups=1):
    return (len(pieces) + 1) * groups


def norm_parts(v):
    c = v - jnp.mean(v, axis=-1, keepdims=True)
    inv = lax.rsqrt(jnp.mean(c * c, axis=-1, keepdims=True) + NORM_EPS)
    return c * inv, inv


def norm_back(n, inv, gain, e):
    ge = g_e = gain * e
    return (g_e - jnp.mean(ge, axis=-1, keepdims=True) - n * jnp.mean(ge * n, axis=-1, keepdims=True)) * inv


def rowsum(v):
    return jnp.sum(v, axis=0, keepdims=True)


def vectors_kernel(where, *refs, nz, n_bias):
    pieces, vec, bias = refs[:-2], refs[-2], refs[-1]
    z, x = where[0], where[1]
    own = pieces[0].shape[0]
    order = [z * 2 + x] + [owner_of(i, nz, z, x) for i in range(2 * nz - 1)]
    got = [jnp.transpose(piece[...].astype(F32))[: N_VEC + n_bias] for piece in pieces]
    for o in range(2 * nz):
        acc = jnp.zeros(got[0].shape, F32)
        for at, piece in zip(order, got):
            acc = jnp.where(at == o, piece, acc)
        vec[0:N_VEC, o * own : (o + 1) * own] = acc[:N_VEC]
        for j in range(n_bias):
            lo = (o * n_bias + j) * own
            bias[0:1, lo : lo + own] = acc[N_VEC + j : N_VEC + j + 1]


def small_vectors(pieces, width, n_bias):
    nz = lax.axis_size("z")
    own = pieces[0].shape[-2]
    at = pieces[1].shape[1] // own - 1
    blocks = pieces[: 2 * nz]
    return call(
        functools.partial(vectors_kernel, nz=nz, n_bias=n_bias),
        "vectors",
        here(),
        blocks,
        [pl.BlockSpec((None, own, own), lambda i, w: (0, 0, at))]
        + [pl.BlockSpec((own, own), lambda i, w: (0, at))] * (len(blocks) - 1),
        [((16, width), F32), ((1, n_bias * 2 * nz * own), F32)],
        grid=(1,),
        out_specs=[
            pl.BlockSpec((16, width), lambda i, w: (0, 0)),
            pl.BlockSpec((1, n_bias * 2 * nz * own), lambda i, w: (0, 0)),
        ],
        cost=cost_of(2),
    )


def plain_vectors(small, width):
    placed = lax.all_gather(small, DP_AXES, axis=0, tiled=False).astype(F32)
    vec = placed[:, :N_VEC].transpose(1, 0, 2).reshape(N_VEC, width)
    return jnp.pad(vec, ((0, 4), (0, 0))), placed[:, N_VEC:].reshape(1, -1)


def first_norm(tok, vec, normed):
    rows = min(64, tok.shape[0])

    def body(i, carry):
        at = pl.ds(pl.multiple_of(i * rows, rows), rows)
        n, inv = norm_parts(tok[at, :].astype(F32))
        normed[at, :] = (n * vec[4:5, :] + vec[8:9, :]).astype(BF16)
        return carry

    lax.fori_loop(0, tok.shape[0] // rows, body, 0)


def qkv_kernel(where, first, vec, *refs, nz, chunk, chunks, n_pieces):
    pieces, refs = refs[:n_pieces], list(refs[n_pieces:])
    n_seq = N_SEQ
    outs = [refs.pop(0) for _ in range(n_seq)]
    normed = refs.pop(0) if chunk == 0 else first
    w, stage, sems, out_sems = refs
    rows, cols = outs[0].shape
    per_side = n_seq // 2
    load = Loader(where, pieces, [w], sems, nz, chunk * per_side * cols)
    load.start()
    if chunk == 0:
        first_norm(first, vec, normed)
    load.wait()
    wide = cols // 3
    grp = wide * chunks
    scale = 1.0 / (RELAX * math.sqrt(HD))
    for side in range(2):
        mixed = _nn(normed[...], w[side])
        for j in range(per_side):
            s = side * per_side + j
            lo = s * grp + chunk * wide
            block = mixed[:, j * cols : (j + 1) * cols]
            at = slice(s * rows, (s + 1) * rows)
            stage[at, 0:wide] = ((block[:, 0:wide] + vec[0:1, lo : lo + wide]) * scale).astype(BF16)
            stage[at, wide : 2 * wide] = block[:, wide : 2 * wide].astype(BF16)
            stage[at, 2 * wide :] = (block[:, 2 * wide :] + vec[1:2, lo : lo + wide]).astype(BF16)
    run_copies(by_target(where, stage, outs, out_sems))


def gelu_parts(h):
    return jnp.tanh(h * (GELU_K + (GELU_K * GELU_A) * (h * h)))


def up_kernel(where, *refs, nz, n_att, n_pieces):
    refs = list(refs)
    att_in = [[refs.pop(0) for _ in range(N_SEQ)] for _ in range(n_att)]
    tok, vec, fc1_b = [refs.pop(0) for _ in range(3)]
    pieces = [refs.pop(0) for _ in range(n_pieces)]
    out_att, out_branch, out_residual, out_normed, out_hidden, out_active = [refs.pop(0) for _ in range(6)]
    proj_w, fc1_w, attended, branch, residual, normed_two, hidden, active, in_sems, out_sems = refs
    load = Loader(where, pieces, (proj_w, fc1_w), in_sems, nz)
    load.start(0)
    load.start(1)
    out = Writer(out_sems)
    rows, width = tok.shape
    part = att_in[0][0].shape[1]
    for i in range(N_SEQ):
        s = jnp.bitwise_xor(where[3], i)
        for j in range(n_att):
            lo = pl.multiple_of((s * n_att + j) * part, part)
            attended[:, pl.ds(lo, part)] = att_in[j][i][...]
    out.put(attended, out_att)
    load.wait(0)
    half = width // 2
    for side in range(2):
        cols = slice(side * half, (side + 1) * half)
        branch[:, cols] = _nn(attended[...], proj_w[side]) + vec[2:3, cols]
    out.put(branch, out_branch)
    step = min(64, rows)

    def norms(i, carry):
        at = pl.ds(pl.multiple_of(i * step, step), step)
        n, inv = norm_parts(branch[at, :])
        r = tok[at, :].astype(F32) + (n * vec[5:6, :] + vec[9:10, :])
        residual[at, :] = r
        n, inv = norm_parts(r)
        normed_two[at, :] = (n * vec[6:7, :] + vec[10:11, :]).astype(BF16)
        return carry

    lax.fori_loop(0, rows // step, norms, 0)
    out.put(residual, out_residual)
    out.put(normed_two, out_normed)
    load.wait(1)
    ff = hidden.shape[1]
    blk = 512
    for i in range(ff // blk):
        at = slice(i * blk, (i + 1) * blk)
        side, col = divmod(i * blk, ff // 2)
        h = _nn(normed_two[...], fc1_w[side, :, col : col + blk]) + fc1_b[:, at]
        hidden[:, at] = h
        active[:, at] = (0.5 * h * (1.0 + gelu_parts(h))).astype(BF16)
        out.put(hidden.at[:, at], out_hidden.at[:, at])
        out.put(active.at[:, at], out_active.at[:, at])
    out.wait()


def mid_kernel(where, active_in, residual_in, hidden_in, out_grad, vec, *refs, nz, n_pieces):
    pieces, refs = refs[:n_pieces], list(refs[n_pieces:])
    layer_out, d_second, out_hidden, sums, fc1_sum = [refs.pop(0) for _ in range(5)]
    fc2_w, active, residual, wide, hidden, d_hidden, load_sems, in_sems, out_sems = refs
    rows, width = out_grad.shape
    ff = hidden.shape[1]
    blk = 512
    load = Loader(where, pieces, (fc2_w,), load_sems, nz, 0, True)
    out = Writer(out_sems)
    blocks = [slice(i * blk, (i + 1) * blk) for i in range(ff // blk)]
    ins = [
        pltpu.make_async_copy(active_in, active, in_sems.at[0]),
        pltpu.make_async_copy(residual_in, residual, in_sems.at[1]),
    ] + [
        pltpu.make_async_copy(hidden_in.at[:, at], hidden.at[:, at], in_sems.at[2 + i])
        for i, at in enumerate(blocks)
    ]
    ins[0].start()
    load.start(0, 0)
    load.start(0, 1)
    for copy in ins[1:]:
        copy.start()
    half = width // 2
    ins[0].wait()
    for k in range(2):
        load.wait(0, k)
        side = load.sides[k]
        cols = pl.ds(pl.multiple_of(side * half, half), half)
        wide[:, cols] = _nn(active[...], fc2_w[side]) + vec[3:4, cols]
    ins[1].wait()
    step = min(64, rows)

    def top(i, carry):
        g_sum, s_sum, b_sum = carry
        at = pl.ds(pl.multiple_of(i * step, step), step)
        n, inv = norm_parts(wide[at, :])
        e = out_grad[at, :].astype(F32)
        layer_out[at, :] = (residual[at, :] + (n * vec[7:8, :] + vec[11:12, :])).astype(BF16)
        d = norm_back(n, inv, vec[7:8, :], e).astype(BF16)
        d_second[at, :] = d
        return g_sum + rowsum(e * n), s_sum + rowsum(e), b_sum + rowsum(d.astype(F32))

    zero = jnp.zeros((1, width), F32)
    g_sum, s_sum, b_sum = lax.fori_loop(0, rows // step, top, (zero, zero, zero))
    sums[...] = jnp.zeros_like(sums)
    sums[3:4, :] = b_sum
    sums[7:8, :] = g_sum
    sums[11:12, :] = s_sum
    for copy in ins[2:]:
        copy.wait()
    for i, at in enumerate(blocks):
        d = _nt(d_second[:, 0:half], fc2_w[0, at, :]) + _nt(d_second[:, half:], fc2_w[1, at, :])
        h = hidden[:, at]
        t = gelu_parts(h)
        square = h * h
        bend = h * (0.5 * GELU_K + (1.5 * GELU_K * GELU_A) * square)
        low = (d * ((0.5 + 0.5 * t) + (1.0 - t * t) * bend)).astype(BF16)
        d_hidden[:, at] = low
        fc1_sum[:, at] = rowsum(low.astype(F32))
        if i % 2 == 1:
            pair = slice((i - 1) * blk, (i + 1) * blk)
            out.put(d_hidden.at[:, pair], out_hidden.at[:, pair])
    out.wait()


def back_kernel(where, out_grad, vec, sums_in, d_hidden_in, residual_in, branch_in, *refs, nz, n_att, n_pieces):
    refs = list(refs)
    ups = [refs.pop(0) for _ in range(n_pieces)]
    out_residual, out_branch, sums = [refs.pop(0) for _ in range(3)]
    d_att = [[refs.pop(0) for _ in range(N_SEQ)] for _ in range(n_att)]
    proj_w, fc1_w, d_hidden, residual, branch, wide, d_residual, d_branch = [refs.pop(0) for _ in range(8)]
    stages = [refs.pop(0) for _ in range(n_att)]
    up_sems, in_sems, out_sems = refs
    rows, width = out_grad.shape
    ff = d_hidden.shape[1]
    load = Loader(where, ups, (proj_w, fc1_w), up_sems, nz)
    out = Writer(out_sems)
    ff_half = ff // 2
    ins = []
    for k in range(2):
        at = pl.ds(pl.multiple_of(load.sides[k] * ff_half, ff_half), ff_half)
        ins.append(pltpu.make_async_copy(d_hidden_in.at[:, at], d_hidden.at[:, at], in_sems.at[k]))
        ins[k].start()
        load.start(1, k)
    ins.append(pltpu.make_async_copy(residual_in, residual, in_sems.at[2]))
    ins.append(pltpu.make_async_copy(branch_in, branch, in_sems.at[3]))
    ins[2].start()
    ins[3].start()
    load.start(0)
    half = width // 2
    for k in range(2):
        ins[k].wait()
        load.wait(1, k)
        side = load.sides[k]
        at = pl.ds(pl.multiple_of(side * ff_half, ff_half), ff_half)
        for q in range(2):
            rows_at = slice(q * half, (q + 1) * half)
            part = _nt(d_hidden[:, at], fc1_w[side, rows_at, :])
            wide[:, rows_at] = part if k == 0 else wide[:, rows_at] + part
    ins[2].wait()
    ins[3].wait()
    step = min(64, rows)

    def mid(i, carry):
        g2, s2, g1, s1, b_sum = carry
        at = pl.ds(pl.multiple_of(i * step, step), step)
        e = wide[at, :]
        n, inv = norm_parts(residual[at, :])
        d = out_grad[at, :].astype(F32) + norm_back(n, inv, vec[6:7, :], e)
        d_residual[at, :] = d
        g2, s2 = g2 + rowsum(e * n), s2 + rowsum(e)
        n, inv = norm_parts(branch[at, :])
        low = norm_back(n, inv, vec[5:6, :], d).astype(BF16)
        d_branch[at, :] = low
        return g2, s2, g1 + rowsum(d * n), s1 + rowsum(d), b_sum + rowsum(low.astype(F32))

    zero = jnp.zeros((1, width), F32)
    g2, s2, g1, s1, b_sum = lax.fori_loop(0, rows // step, mid, (zero,) * 5)
    out.put(d_residual, out_residual)
    out.put(d_branch, out_branch)
    sums[...] = sums_in[...]
    for row, v in ((6, g2), (10, s2), (5, g1), (9, s1), (2, b_sum)):
        sums[row : row + 1, :] = v
    load.wait(0)
    part = stages[0].shape[1]
    for s in range(N_SEQ):
        at = slice(s * n_att * part, (s + 1) * n_att * part)
        low = (_nt(d_branch[:, 0:half], proj_w[0, at, :]) + _nt(d_branch[:, half:], proj_w[1, at, :])).astype(BF16)
        for j in range(n_att):
            stages[j][s * rows : (s + 1) * rows, :] = low[:, j * part : (j + 1) * part]
    for j in range(n_att):
        for i, ref in enumerate(d_att[j]):
            at = pl.multiple_of(jnp.bitwise_xor(where[3], i) * rows, rows)
            out.put(stages[j].at[pl.ds(at, rows), :], ref)
    out.wait()


def run_up(where, att, tokens, vec, fc1_b, ups):
    nz = lax.axis_size("z")
    rows, width = tokens.shape
    ff = fc1_b.shape[1]
    flat = [block for blocks in att for block in blocks]
    big = (rows, width)
    outs = [(big, BF16), (big, F32), (big, F32), (big, BF16), ((rows, ff), F32), ((rows, ff), BF16)]
    return call(
        functools.partial(up_kernel, nz=nz, n_att=len(att), n_pieces=len(ups)),
        "up",
        where,
        flat + [tokens, vec, fc1_b] + ups,
        [VMEM] * (len(flat) + 3) + [ANY] * len(ups),
        outs,
        [
            pltpu.VMEM((2, width, width // 2), BF16),
            pltpu.VMEM((2, width, ff // 2), BF16),
        ]
        + [pltpu.VMEM(shape, dtype) for shape, dtype in outs]
        + [pltpu.SemaphoreType.DMA((n_copies(ups, 2),)), pltpu.SemaphoreType.DMA((4 + 2 * (ff // 512),))],
        out_specs=[ANY] * len(outs),
        cost=cost_of(20),
    )


def run_mid(where, active, residual, hidden, out_grad, vec, downs):
    nz = lax.axis_size("z")
    rows, width = out_grad.shape
    ff = active.shape[1]
    big = (rows, width)
    return call(
        functools.partial(mid_kernel, nz=nz, n_pieces=len(downs)),
        "mid",
        where,
        [active, residual, hidden, out_grad, vec] + downs,
        [ANY] * 3 + [VMEM] * 2 + [ANY] * len(downs),
        [(big, BF16), (big, BF16), ((rows, ff), BF16), ((16, width), F32), ((1, ff), F32)],
        [
            pltpu.VMEM((2, ff, width // 2), BF16),
            pltpu.VMEM((rows, ff), BF16),
            pltpu.VMEM(big, F32),
            pltpu.VMEM(big, F32),
            pltpu.VMEM((rows, ff), F32),
            pltpu.VMEM((rows, ff), BF16),
            pltpu.SemaphoreType.DMA((n_copies(downs, ff // width),)),
            pltpu.SemaphoreType.DMA((2 + ff // 512,)),
            pltpu.SemaphoreType.DMA((ff // 512,)),
        ],
        out_specs=[VMEM] * 2 + [ANY] + [VMEM] * 2,
        cost=cost_of(28),
    )


def run_back(where, out_grad, vec, sums, d_hidden, residual, branch, ups, n_att):
    nz = lax.axis_size("z")
    rows, width = out_grad.shape
    ff = d_hidden.shape[1]
    big = (rows, width)
    part = width // N_SEQ // n_att
    outs = [(big, F32), (big, BF16), ((16, width), F32)]
    outs += [((rows, part), BF16)] * (n_att * N_SEQ)
    return call(
        functools.partial(back_kernel, nz=nz, n_att=n_att, n_pieces=len(ups)),
        "back",
        where,
        [out_grad, vec, sums, d_hidden, residual, branch] + ups,
        [VMEM] * 3 + [ANY] * (3 + len(ups)),
        outs,
        [
            pltpu.VMEM((2, width, width // 2), BF16),
            pltpu.VMEM((2, width, ff // 2), BF16),
            pltpu.VMEM((rows, ff), BF16),
            pltpu.VMEM(big, F32),
            pltpu.VMEM(big, F32),
            pltpu.VMEM(big, F32),
            pltpu.VMEM(big, F32),
            pltpu.VMEM(big, BF16),
        ]
        + [pltpu.VMEM((N_SEQ * rows, part), BF16)] * n_att
        + [
            pltpu.SemaphoreType.DMA((n_copies(ups, 2),)),
            pltpu.SemaphoreType.DMA((4,)),
            pltpu.SemaphoreType.DMA((2 + n_att * N_SEQ,)),
        ],
        out_specs=[ANY] * 2 + [VMEM] + [ANY] * (n_att * N_SEQ),
        cost=cost_of(20),
    )


def slot_owner(i, nz, where):
    z, x = where[0], where[1]
    return lax.rem(z + 2 * nz - 1 - i % nz, nz) * 2 + (1 - x if i < nz else x)


def contract_rows(left, right):
    return lax.dot_general(left, right, (((0,), (0,)), ((), ())), preferred_element_type=F32)


def halves_of(ref, c):
    half = ref.shape[1] // 2
    return [ref[:, pl.ds(pl.multiple_of(h * half, half), half)] for h in (1 - c, c)]


def columns_of(ref, owner, count):
    return ref[:, pl.ds(pl.multiple_of(owner * count, count), count)]


def row_grad_kernel(where, lhs, rhs, *outs, nz):
    c = where[2]
    rows = outs[0].shape[1]
    half = rhs.shape[1] // 2
    blk = min(1024, half)
    for side in range(2):
        owners = [slot_owner(side * nz + i, nz, where) for i in range(nz)]
        left = jnp.concatenate([columns_of(lhs, o, rows) for o in owners], axis=1)
        for h in range(2):
            out = outs[2 * side + h]
            base = (1 - c if h == 0 else c) * half
            for n in range(half // blk):
                right = rhs[:, pl.ds(pl.multiple_of(base + n * blk, blk), blk)]
                low = contract_rows(left, right).astype(BF16)
                for i in range(nz):
                    out[i, :, n * blk : (n + 1) * blk] = low[i * rows : (i + 1) * rows]


def wide_grad_kernel(where, *refs, nz, side):
    ins, outs = refs[:4], refs[4:6]
    normed_two, d_hidden, active, d_second = refs[6:10]
    stages, in_sems, out_sems = refs[10:12], refs[12], refs[13]
    c = where[2]
    rows = outs[0].shape[1]
    owners = [slot_owner(side * nz + i, nz, where) for i in range(nz)]
    half = d_hidden.shape[1] // 2
    blk = min(1024, half)
    loads = [pltpu.make_async_copy(ins[0], normed_two, in_sems.at[0])]
    for k, h in enumerate((1 - c, c)):
        at = pl.ds(pl.multiple_of(h * half, half), half)
        loads.append(pltpu.make_async_copy(ins[1].at[:, at], d_hidden.at[:, at], in_sems.at[1 + k]))
    loads.append(pltpu.make_async_copy(ins[3], d_second, in_sems.at[3]))
    wide = active.shape[1] // (2 * nz)
    for i in range(nz):
        at = pl.ds(pl.multiple_of(owners[i] * wide, wide), wide)
        loads.append(pltpu.make_async_copy(ins[2].at[:, at], active.at[:, at], in_sems.at[4 + i]))
    for load in loads:
        load.start()
    write = Writer(out_sems)
    loads[0].wait()
    left = jnp.concatenate([columns_of(normed_two, o, rows) for o in owners], axis=1)
    for h, out in enumerate(stages):
        loads[1 + h].wait()
        base = (1 - c if h == 0 else c) * half
        for n in range(half // blk):
            right = d_hidden[:, pl.ds(pl.multiple_of(base + n * blk, blk), blk)]
            low = contract_rows(left, right).astype(BF16)
            for i in range(nz):
                out[i, :, n * blk : (n + 1) * blk] = low[i * rows : (i + 1) * rows]
    loads[3].wait()
    rights = halves_of(d_second, c)
    cols = d_second.shape[1] // 2
    for i in range(nz):
        loads[4 + i].wait()
        left = columns_of(active, owners[i], wide)
        for stage, out, right in zip(stages, outs, rights):
            low = contract_rows(left, right).astype(BF16)
            for g in range(wide // rows):
                lo = half + g * cols
                stage[i, :, lo : lo + cols] = low[g * rows : (g + 1) * rows]
            write.put(stage.at[i], out.at[i])
    write.wait()


def run_wide_grad(where, normed_two, d_hidden, active, d_second, rows, side):
    nz = lax.axis_size("z")
    tok, width = normed_two.shape
    ff = active.shape[1]
    out = ((nz, rows, ff // 2 + ff // width * width // 2), BF16)
    return call(
        functools.partial(wide_grad_kernel, nz=nz, side=side),
        "wide_grad",
        where,
        (normed_two, d_hidden, active, d_second),
        [ANY] * 4,
        [out] * 2,
        [
            pltpu.VMEM((tok, width), BF16),
            pltpu.VMEM((tok, ff), BF16),
            pltpu.VMEM((tok, ff), BF16),
            pltpu.VMEM((tok, width), BF16),
            pltpu.VMEM(*out),
            pltpu.VMEM(*out),
            pltpu.SemaphoreType.DMA((4 + nz,)),
            pltpu.SemaphoreType.DMA((2 * nz,)),
        ],
        out_specs=[ANY] * 2,
        cost=cost_of(9),
    )


def grads(kernel, name, where, args, rows, half, specs=None, scratch=(), count=4, **more):
    nz = lax.axis_size("z")
    return call(
        functools.partial(kernel, nz=nz, **more),
        name,
        where,
        args,
        specs or [VMEM] * len(args),
        [((nz, rows, half), BF16)] * count,
        scratch,
        cost=cost_of(2.5 * count),
    )


def qkv_grad_kernel(where, normed, *refs, nz):
    blocks, outs, (stage, sems) = refs[:N_SEQ], refs[N_SEQ:-2], refs[-2:]
    c = where[2]
    rows = outs[0].shape[1]
    tok = normed.shape[0]
    per_side = N_SEQ // 2
    run_copies(by_source(where, blocks, stage, sems))
    for h in range(2):
        base = (1 - c if h == 0 else c) * per_side
        right = jnp.concatenate(
            [stage[pl.ds(pl.multiple_of((base + j) * tok, tok), tok), :] for j in range(per_side)], axis=1
        )
        for side in range(2):
            owners = [slot_owner(side * nz + i, nz, where) for i in range(nz)]
            left = jnp.concatenate([columns_of(normed, o, rows) for o in owners], axis=1)
            low = contract_rows(left, right).astype(BF16)
            for i in range(nz):
                outs[2 * side + h][i] = low[i * rows : (i + 1) * rows]


class Reduce:
    def __init__(self, stages, parts):
        self.stages, self.parts_x = stages, parts
        self.box = stages.box
        self.from_x, self.out = [], []
        self.steps, self.ready, self.blocks_out = 0, False, []

    def set_first(self, outs):
        self.first = self.stages.boxes(outs)

    def set_second(self, outs):
        self.second = self.stages.boxes(outs)

    def c_first(self):
        self.got = self.box(lax.ppermute(self.first[0].v, "c", SWAP))

    def c_second(self):
        self.own_got = self.box(lax.ppermute(self.second[0].v, "c", SWAP))

    def c(self):
        self.c_first()
        self.c_second()

    def sum(self, count=1):
        got, kept = self.got.v, self.first[1].v
        self.size = got.shape[0] // self.parts_x
        for unused in range(count):
            at = len(self.out) * self.size
            self.out.append(self.box(add_low(kept[at : at + self.size], got[at : at + self.size])))

    def x(self):
        if len(self.out) == len(self.from_x):
            self.sum()
        self.from_x.append(self.box(lax.ppermute(self.out[len(self.from_x)].v, "x", SWAP)))

    def add(self):
        step = self.steps
        ready = [self.from_x[step // self.size]] + ([self.passed] if step > 0 else [])
        ready = self.stages.begin(*ready)
        terms = [self.second[1].v[step], self.own_got.v[step], ready[0][step % self.size]] + ready[1:]
        self.cur = self.box(add_low(*terms))
        self.steps += 1

    def z(self):
        if not self.ready:
            self.add()
        self.ready = False
        self.passed = self.box(lax.ppermute(self.cur.v, "z", ring(lax.axis_size("z"))))
        return self.passed

    def blocks(self):
        crossed = self.from_x[0].v
        return [
            add_low(self.second[1].v[i], self.own_got.v[i], crossed[i])
            for i in range(lax.axis_size("z"))
        ]

    def prepare(self, *others):
        blocks = self.blocks()
        if others:
            blocks = [jnp.concatenate(b, axis=1) for b in zip(blocks, *[o.blocks() for o in others])]
        self.blocks_out = self.stages.boxes(blocks)

    def direct(self):
        nz = lax.axis_size("z")
        if not self.blocks_out:
            self.prepare()
        blocks = [b.v for b in self.blocks_out]
        self.kept = blocks[-1]
        self.parts = [
            self.box(lax.ppermute(blocks[i], "z", [(s, (s - 1 - i) % nz) for s in range(nz)]))
            for i in range(nz - 1)
        ]
        return self.parts

    def gather_parts(self):
        self.cur = self.box(add_low(self.kept, *self.stages.begin(*self.parts)))

    def y(self):
        if hasattr(self, "parts"):
            self.gather_parts()
        elif not self.ready:
            self.add()
        self.from_y = self.box(lax.ppermute(self.cur.v, "y", SWAP))
        return self.from_y

    def last_c(self):
        (got,) = self.stages.begin(self.from_y)
        self.low = add_low(self.cur.v, got)
        self.other = self.box(lax.ppermute(self.low, "c", SWAP))
        return self.other

    def finish(self):
        c = lax.axis_index("c")
        low, (other,) = self.low, self.stages.begin(self.other)
        return jnp.where(c == 0, low, other), jnp.where(c == 0, other, low)


class SmallReduce:
    def __init__(self, stages, grads):
        self.stages, self.box = stages, stages.box
        self.cur = self.box(grads.astype(BF16))

    def seq(self):
        (cur,) = self.stages.begin(self.cur)
        both = [(i, i ^ 3) for i in range(4)]
        self.parts = [
            self.box(lax.ppermute(cur, "c", SWAP)),
            self.box(lax.ppermute(cur, "y", SWAP)),
            self.box(lax.ppermute(cur, SEQ_AXES, both)),
        ]
        return self.parts

    def x(self):
        nz = lax.axis_size("z")
        cur = add_low(self.cur.v, *self.stages.begin(*self.parts))
        self.keep = cur[nz:]
        self.got = self.box(lax.ppermute(cur[:nz], "x", SWAP))
        return [self.got]

    def z(self):
        nz = lax.axis_size("z")
        (got,) = self.stages.begin(self.got)
        cur = add_low(self.keep, got)
        self.keep = cur[nz - 1]
        self.parts = [
            self.box(lax.ppermute(cur[i], "z", [(s, (s - 1 - i) % nz) for s in range(nz)]))
            for i in range(nz - 1)
        ]
        return self.parts

    def finish(self):
        return add_low(self.keep, *self.stages.begin(*self.parts)).astype(F32)


def reduce_plain(lhs, rhs):
    grad = lax.dot_general(
        lhs, rhs, (((0,), (0,)), ((), ())), preferred_element_type=F32
    ).astype(BF16)
    part = lax.psum_scatter(grad, DP_AXES, scatter_dimension=0, tiled=True)
    return lax.psum(part, SEQ_AXES).astype(F32)


def last_kernel(where, *refs, nz, chunks, n_pieces, rings):
    refs = list(refs)
    blocks = [[refs.pop(0) for _ in range(N_SEQ)] for _ in range(chunks)]
    tok, d_residual, vec, sums, fc1_sum = [refs.pop(0) for _ in range(5)]
    pieces = [refs.pop(0) for _ in range(n_pieces)]
    tokens_grad, small = refs.pop(0), refs.pop(0)
    ws = [refs.pop(0) for _ in range(chunks)]
    stages = [refs.pop(0) for _ in range(chunks)]
    wide, total, in_sems = refs.pop(0), refs.pop(0), refs.pop(0)
    loads = [
        Loader(where, pieces, [w], sem, nz, j * w.shape[2]) for j, (w, sem) in enumerate(zip(ws, refs))
    ]
    for load in loads:
        load.start()
    rows, width = tok.shape
    n_seq, cols = N_SEQ, stages[0].shape[1]
    run_copies(
        [copy for j in range(chunks) for copy in by_source(where, blocks[j], stages[j], in_sems.at[j])]
    )
    d_mixed = [stage.reshape(n_seq, rows, cols) for stage in stages]
    part = cols // 3
    zero = jnp.zeros((1, width), F32)
    total[...] = sums[...]
    for j in range(chunks):
        for s in range(n_seq):
            lo = (s * chunks + j) * part
            total[0:1, lo : lo + part] = rowsum(d_mixed[j][s, :, 0:part].astype(F32))
            total[1:2, lo : lo + part] = rowsum(d_mixed[j][s, :, 2 * part :].astype(F32))
    for load in loads:
        load.wait()
    quarter = width // 4
    per_side = n_seq // 2
    for q in range(4):
        at = slice(q * quarter, (q + 1) * quarter)
        acc = None
        for j in range(chunks):
            for side in range(2):
                left = jnp.concatenate([d_mixed[j][side * per_side + i] for i in range(per_side)], axis=1)
                term = _nt(left, ws[j][side, at, :])
                acc = term if acc is None else acc + term
        wide[:, at] = acc
    step = min(64, rows)

    def norms(i, carry):
        g, s = carry
        at = pl.ds(pl.multiple_of(i * step, step), step)
        e = wide[at, :]
        n, inv = norm_parts(tok[at, :].astype(F32))
        tokens_grad[at, :] = (d_residual[at, :] + norm_back(n, inv, vec[4:5, :], e)).astype(BF16)
        return g + rowsum(e * n), s + rowsum(e)

    g, s = lax.fori_loop(0, rows // step, norms, (zero, zero))
    total[4:5, :] = g
    total[8:9, :] = s
    if not rings:
        small[...] = total[...]
        return
    z, x = where[0], where[1]
    own = width // (2 * nz)
    n_bias = fc1_sum.shape[1] // width
    for o in range(2 * nz):
        slot = lax.rem(z + 2 * nz - 1 - o // 2, nz) + jnp.where(x == o % 2, nz, 0)
        small[slot, 0:N_VEC, :] = total[0:N_VEC, o * own : (o + 1) * own]
        for j in range(n_bias):
            lo = (o * n_bias + j) * own
            small[slot, N_VEC + j : N_VEC + j + 1, :] = fc1_sum[:, lo : lo + own]


def last(where, d_mixed, tokens, d_residual, vec, sums, fc1_sum, pieces):
    nz = lax.axis_size("z")
    rings = uses_rings()
    rows, width = tokens.shape
    chunks = len(d_mixed)
    small = ((2 * nz, N_VEC + fc1_sum.shape[1] // width, width // (2 * nz)), F32) if rings else ((16, width), F32)
    return call(
        functools.partial(last_kernel, nz=nz, chunks=chunks, n_pieces=len(pieces), rings=rings),
        "last",
        where,
        [b for blocks in d_mixed for b in blocks] + [tokens, d_residual, vec, sums, fc1_sum] + list(pieces),
        [ANY] * (chunks * N_SEQ) + [VMEM] * 5 + [ANY] * len(pieces),
        [((rows, width), BF16), small],
        [pltpu.VMEM((2, width, 3 * width // chunks // 2), BF16)] * chunks
        + [pltpu.VMEM((N_SEQ * rows, 3 * width // chunks // N_SEQ), BF16)] * chunks
        + [pltpu.VMEM((rows, width), F32), pltpu.VMEM((16, width), F32), pltpu.SemaphoreType.DMA((chunks, N_SEQ))]
        + [pltpu.SemaphoreType.DMA((n_copies(pieces),))] * chunks,
        cost=cost_of(12),
    )


def reduce_small(small, fc1_sum, own):
    n_dp = lax.axis_size("z") * lax.axis_size("x")
    low = jnp.concatenate(
        (small[:N_VEC].reshape(N_VEC, n_dp, own).transpose(1, 0, 2), fc1_sum.reshape(n_dp, -1, own)),
        axis=1,
    )
    part = lax.psum_scatter(low, DP_AXES, scatter_dimension=0, tiled=False)
    return lax.psum(part.astype(BF16), SEQ_AXES).astype(F32)


def exchange(blocks):
    both = [(i, i ^ 3) for i in range(4)]
    return [
        blocks[0],
        lax.ppermute(blocks[1], "c", SWAP),
        lax.ppermute(blocks[2], "y", SWAP),
        lax.ppermute(blocks[3], SEQ_AXES, both),
    ]


def per_device(
    tokens,
    out_grad,
    qkv_weight,
    qv_bias,
    proj_weight,
    fc1_weight,
    fc1_bias,
    fc2_weight,
    out_bias,
    norm_gains,
    norm_shifts,
):
    n_seq = lax.axis_size("y") * lax.axis_size("c")
    rows, width = tokens.shape
    own = qv_bias.shape[1]
    chunks = CHUNKS
    grp = width // n_seq
    part = grp // chunks
    heads = part // HD
    seq_len = n_seq * rows
    nz = lax.axis_size("z")
    where = here()
    qkv_shards = qkv_weight.reshape(-1, 3, n_seq, chunks, part).transpose(3, 0, 2, 1, 4)
    qkv_shards = qkv_shards.reshape(chunks, -1, 3 * width // chunks)
    small = jnp.concatenate(
        (qv_bias, out_bias, norm_gains, norm_shifts, fc1_bias.reshape(-1, own)), axis=0
    )
    rings = uses_rings()
    st = Stages()
    ff = fc1_weight.shape[1]
    r = proj_weight.shape[0]
    qkv_cat = jnp.concatenate([in_halves(w) for w in qkv_shards], axis=2)
    groups = fc2_weight.shape[0] // r
    if rings:
        fc2_groups = fc2_weight.reshape(groups, -1, 2, width // 2).transpose(2, 1, 0, 3)
        n_bias = small.shape[0] - N_VEC
        columns = jnp.pad(small.T, ((0, 0), (0, own - small.shape[0])))
        qkv_in = Gather(st, jnp.concatenate((qkv_cat, jnp.stack((columns, columns))), axis=2))
        up_in = Gather(st, jnp.concatenate((in_halves(proj_weight), in_halves(fc1_weight)), axis=2))
        down_in = Gather(st, fc2_groups.reshape(2, -1, groups * width // 2))
        for step in range(nz):
            if step > 0:
                st.sync()
                qkv_in.c()
            qkv_in.x()
            if step < nz - 1:
                qkv_in.z()
            else:
                up_in.z()
                up_in.x()
        qkv_pieces = qkv_in.pieces()
        vec, fc1_b = small_vectors(qkv_pieces, width, n_bias)
    else:
        vec, fc1_b = plain_vectors(small, width)
        whole = lax.all_gather(qkv_cat, DP_AXES, axis=1, tiled=True)
        qkv_pieces = [jnp.concatenate((whole[0], whole[1]), axis=1)]
        ups, downs = [
            [lax.all_gather(w, DP_AXES, axis=0, tiled=True) for w in ws]
            for ws in ((proj_weight, fc1_weight), (fc2_weight,))
        ]

    def project(j, first, vec):
        outs = [((rows, 3 * part), BF16)] * n_seq
        if j == 0:
            outs.append(((rows, width), BF16))
        return call(
            functools.partial(qkv_kernel, nz=nz, chunk=j, chunks=chunks, n_pieces=len(qkv_pieces)),
            "qkv",
            where,
            [first, vec] + qkv_pieces,
            [VMEM] * 2 + [ANY] * len(qkv_pieces),
            outs,
            [
                pltpu.VMEM((2, width, 3 * width // chunks // 2), BF16),
                pltpu.VMEM((seq_len, 3 * part), BF16),
                pltpu.SemaphoreType.DMA((n_copies(qkv_pieces),)),
                pltpu.SemaphoreType.DMA((n_seq,)),
            ],
            out_specs=[ANY] * n_seq + [VMEM] * (j == 0),
            cost=cost_of(7),
        )

    def swap(blocks):
        return st.boxes(exchange(st.begin(*blocks)))

    def hops(*some):
        for hop in some if rings else []:
            hop()

    if not rings:
        up_in = down_in = Gather(st, qkv_cat)
    got = st.boxes(project(0, tokens, vec))
    sent_a, normed_box = got[:n_seq], got[n_seq]
    st.sync()
    normed = normed_box.v
    heads_a = swap(sent_a)
    sent_b = st.boxes(project(1, normed, vec))
    hops(up_in.x, up_in.z)
    st.sync()
    heads_b = swap(sent_b)
    by_a = st.begin(*heads_a)
    out_a, cols_a, lse_a = attn_fwd(where, by_a, heads, 512)
    out_a = st.boxes(out_a)
    hops(up_in.x, up_in.z)
    st.sync()
    att_a = swap(out_a)
    by_b = st.begin(*heads_b)
    out_b, cols_b, lse_b = attn_fwd(where, by_b, heads, 512)
    out_b = st.boxes(out_b)
    hops(up_in.x, down_in.z)
    st.sync()
    att_b = swap(out_b)
    hops(*([down_in.x_pair, down_in.z] if rings else []))
    st.sync()
    if rings:
        ups = up_in.pieces()
    hops(*([down_in.c, down_in.y_pair, down_in.x, down_in.z] if rings else []))
    arrived = st.begin(*att_a, *att_b)
    kept = run_up(where, [arrived[:n_seq], arrived[n_seq:]], tokens, vec, fc1_b, ups)
    attended, branch, residual, normed_two, hidden, active = kept
    active_box = st.box(active)
    st.sync()
    hops(down_in.x)
    st.sync()
    if rings:
        downs = down_in.pieces()
    active = active_box.v
    layer_out, d_second, d_hidden, sums, fc1_sum = run_mid(
        where, active, residual, hidden, out_grad, vec, downs
    )

    hidden_box = st.box(d_hidden)

    def proj_grads():
        outs = grads(row_grad_kernel, "proj_grad", where, (attended, d_branch), r, width // 2)
        return reduction(outs, 1)

    def reduction(outs, parts):
        flow = Reduce(st, parts)
        flow.set_first(outs[:2])
        flow.set_second(outs[2:])
        return flow

    if rings:
        wide = Reduce(st, nz)

        def wide_grads(side):
            return run_wide_grad(where, normed_two, hidden_box.v, active, d_second, r, side)

        wide.set_first(wide_grads(0))
        st.sync()
        wide.c_first()
        wide.set_second(wide_grads(1))
        st.sync()
        wide.sum()
        st.sync()
        hops(wide.x, wide.c_second)
    else:
        grad_fc2 = reduce_plain(active, d_second)
        grad_fc1 = reduce_plain(normed_two, d_hidden)
    outs = run_back(where, out_grad, vec, sums, hidden_box.v, residual, branch, ups, chunks)
    d_residual, d_branch, sums = outs[:3]
    branch_box = st.box(d_branch)
    d_out = st.boxes(outs[3:])
    st.sync()
    d_heads_a = swap(d_out[:n_seq])
    d_branch = branch_box.v
    if rings:
        wide.sum(nz - 1)
        wide.add()
        wide.ready = True
    else:
        grad_proj = reduce_plain(attended, d_branch)
    st.sync()
    hops(*([wide.x, wide.z] if rings else []))
    d_heads_b = swap(d_out[n_seq:])
    d_by_a = st.boxes(attn_bwd(where, by_a, st.begin(*d_heads_a), cols_a, lse_a, heads, 512))
    st.sync()
    d_mixed_a = swap(d_by_a)
    hops(*([wide.x, wide.z] if rings else []))
    d_by_b = st.boxes(attn_bwd(where, by_b, st.begin(*d_heads_b), cols_b, lse_b, heads, 512))
    st.sync()
    d_mixed_b = swap(d_by_b)
    hops(*([wide.x, wide.z] if rings else []))

    def qkv_grads(d_mixed):
        outs = grads(
            qkv_grad_kernel,
            "qkv_grad",
            where,
            [normed] + st.begin(*d_mixed),
            r,
            n_seq // 2 * 3 * part,
            [VMEM] + [ANY] * n_seq,
            [pltpu.VMEM((seq_len, 3 * part), BF16), pltpu.SemaphoreType.DMA((n_seq,))],
        )
        return reduction(outs, 1)

    if rings:
        qkv_a = qkv_grads(d_mixed_a)
        proj = proj_grads()
        st.sync()
        hops(qkv_a.c, proj.c)
        st.sync()
        hops(qkv_a.x)
        qkv_b = qkv_grads(d_mixed_b)
        st.sync()
        hops(qkv_b.c)
        qkv_a.prepare()
        wide.add()
        wide.ready = True
        st.sync()
        hops(qkv_b.x, wide.y, qkv_a.direct)
    both = st.begin(*d_mixed_a, *d_mixed_b)
    d_mixed_a, d_mixed_b = both[:n_seq], both[n_seq:]
    tokens_grad, small_grads = last(
        where, [d_mixed_a, d_mixed_b], tokens, d_residual, vec, sums, fc1_sum, qkv_pieces
    )
    if rings:
        vecs = SmallReduce(st, small_grads)
        st.sync()
        hops(wide.last_c, qkv_b.direct, qkv_a.y, proj.x)
        st.sync()
        hops(vecs.seq, qkv_b.y, qkv_a.last_c, proj.direct)
        low = wide.finish()
        at = ff // 2
        grad_fc1 = jnp.concatenate([half[:, :at] for half in low], axis=1).astype(F32)
        grad_fc2 = jnp.stack([half[:, at:] for half in low]).reshape(2, r, groups, width // 2)
        grad_fc2 = grad_fc2.transpose(2, 1, 0, 3).reshape(groups * r, width).astype(F32)
        ffs = st.boxes((grad_fc1, grad_fc2))
        st.sync()
        grad_fc1, grad_fc2 = [b.v for b in ffs]
        hops(vecs.x, qkv_b.last_c, proj.y)
        st.sync()
        hops(vecs.z, proj.last_c)
        total_small = vecs.finish()
    else:
        total_small = reduce_small(small_grads, fc1_sum, own)
    if rings:
        grad_proj = jnp.concatenate(proj.finish(), axis=1).astype(F32)
        total_qkv = [jnp.concatenate(f.finish(), axis=1).astype(F32) for f in (qkv_a, qkv_b)]
    else:
        total_qkv = []
        order = jnp.stack([jnp.bitwise_xor(where[3], i) for i in range(n_seq)])
        for d_mixed in (d_mixed_a, d_mixed_b):
            blocks = jnp.take(jnp.stack(d_mixed), order, axis=0)
            total_qkv.append(reduce_plain(normed, blocks.transpose(1, 0, 2).reshape(rows, -1)))
    qkv_grad = jnp.stack([t.reshape(-1, n_seq, 3, part) for t in total_qkv])
    qkv_grad = qkv_grad.transpose(1, 3, 2, 0, 4).reshape(-1, 3 * width)
    return (
        layer_out,
        tokens_grad,
        qkv_grad,
        total_small[0:2],
        grad_proj,
        grad_fc1,
        total_small[N_VEC:].reshape(-1),
        grad_fc2,
        total_small[2:4],
        total_small[4:8],
        total_small[8:12],
    )


CHUNKS = 2


def solution(mesh):
    n_dp, n_seq = mesh.devices.shape
    fine = Mesh(mesh.devices.reshape(n_dp // 2, 2, n_seq // 2, 2), DP_AXES + SEQ_AXES)
    tok = P(DP_AXES + SEQ_AXES, None)
    by_row = P(DP_AXES, None)
    by_col = P(None, DP_AXES)
    weights = (by_row, by_col, by_row, by_row, P(DP_AXES), by_row, by_col, by_col, by_col)
    return jax.shard_map(
        per_device,
        mesh=fine,
        in_specs=(tok, tok) + weights,
        out_specs=(tok, tok) + weights,
        check_vma=False,
    )
```

```python
import functools
import math

import jax
import jax.numpy as jnp
from jax.sharding import Mesh
from jax.sharding import PartitionSpec as P
from jax import lax
from jax.experimental import pallas as pl
from jax.experimental.pallas import tpu as pltpu
HD=64
RELAX=32.0
C2=RELAX*math.log2(math.e)
NEG=-1e30

def _nt(a,b):
    return lax.dot_general(a,b,(((1,),(1,)),((),())),preferred_element_type=jnp.float32)
def _nn(a,b):
    return lax.dot_general(a,b,(((1,),(0,)),((),())),preferred_element_type=jnp.float32)

def _tr(x):
    return jnp.transpose(x.astype(jnp.float32)).astype(jnp.bfloat16)

def by_source(where, refs, dst, sems):
    rows = refs[0].shape[0]
    copies = []
    for i, ref in enumerate(refs):
        at = pl.multiple_of(jnp.bitwise_xor(where[3], i) * rows, rows)
        copies.append(pltpu.make_async_copy(ref, dst.at[pl.ds(at, rows), :], sems.at[i]))
    return copies

def by_target(where, src, refs, sems):
    rows = refs[0].shape[0]
    copies = []
    for i, ref in enumerate(refs):
        at = pl.multiple_of(jnp.bitwise_xor(where[3], i) * rows, rows)
        copies.append(pltpu.make_async_copy(src.at[pl.ds(at, rows), :], ref, sems.at[i]))
    return copies

def run_copies(copies):
    for copy in copies:
        copy.start()
    for copy in copies:
        copy.wait()

def fwd_kernel(where,*refs,nh,blk,n):
    ins,outs=refs[:n],refs[n:2*n]
    ot_ref,lse_ref,vt_ref,qkv_ref,o_ref,sems=refs[2*n:]
    seq=qkv_ref.shape[0]; w=nh*HD
    nb=seq//blk
    run_copies(by_source(where,ins,qkv_ref,sems))
    q_ref,k_ref,v_ref=(qkv_ref.at[:,i*w:(i+1)*w] for i in range(3))
    for b in range(nb):
        vt_ref[:,b*blk:(b+1)*blk]=_tr(v_ref[b*blk:(b+1)*blk,:])
    lane=lax.broadcasted_iota(jnp.int32,(1,w),1)//HD
    tri=lax.broadcasted_iota(jnp.int32,(blk,blk),0)<=lax.broadcasted_iota(jnp.int32,(blk,blk),1)
    def qstep(qb,_):
        q0=pl.multiple_of(qb*blk,blk)
        q=q_ref[pl.ds(q0,blk),:]
        qm=[jnp.where(lane==h,q,jnp.zeros_like(q)) for h in range(nh)]
        def kv(kb,carry,diag):
            k0=pl.multiple_of(kb*blk,blk)
            k=k_ref[pl.ds(k0,blk),:]
            out=[]
            for h in range(nh):
                m,l,acc=carry[3*h:3*h+3]
                s=_nt(k,qm[h])*C2
                if diag: s=jnp.where(tri,s,NEG)
                mn=jnp.maximum(m,jnp.max(s,axis=0,keepdims=True))
                a=jnp.exp2(m-mn)
                p=jnp.exp2(s-mn)
                l=l*a+jnp.sum(p,axis=0,keepdims=True)
                acc=acc*a+_nn(vt_ref[h*HD:(h+1)*HD,pl.ds(k0,blk)],p.astype(jnp.bfloat16))
                out+= [mn,l,acc]
            return tuple(out)
        init=[]
        for h in range(nh):
            init+=[jnp.full((1,blk),NEG,jnp.float32),jnp.zeros((1,blk),jnp.float32),jnp.zeros((HD,blk),jnp.float32)]
        c=kv(qb,tuple(init),True)
        c=lax.fori_loop(0,qb,lambda kb,cc: kv(kb,cc,False),c)
        for h in range(nh):
            m,l,acc=c[3*h:3*h+3]
            ot_ref[h*HD:(h+1)*HD,pl.ds(q0,blk)]=acc/l
            lse_ref[h:h+1,pl.ds(q0,blk)]=m+jnp.log2(l)
        o_ref[pl.ds(q0,blk),:]=jnp.transpose(ot_ref[:,pl.ds(q0,blk)]).astype(jnp.bfloat16)
        return 0
    lax.fori_loop(0,nb,qstep,0)
    run_copies(by_target(where,o_ref,outs,sems))

def attn_fwd(where, qkv, nh, blk=512):
    n=len(qkv); rows=qkv[0].shape[0]
    seq=n*rows; w=nh*HD
    blk=min(blk,seq)
    vm=pl.BlockSpec(memory_space=pltpu.VMEM)
    an=pl.BlockSpec(memory_space=pl.ANY)
    outs=pl.pallas_call(functools.partial(fwd_kernel,nh=nh,blk=blk,n=n),
      grid_spec=pltpu.PrefetchScalarGridSpec(num_scalar_prefetch=1,
        in_specs=[an]*n,out_specs=[an]*n+[vm]*2,
        scratch_shapes=[pltpu.VMEM((w,seq),jnp.bfloat16),pltpu.VMEM((seq,3*w),jnp.bfloat16),pltpu.VMEM((seq,w),jnp.bfloat16),pltpu.SemaphoreType.DMA((n,))]),
      out_shape=[jax.ShapeDtypeStruct((rows,w),jnp.bfloat16)]*n+[jax.ShapeDtypeStruct((w,seq),jnp.float32),jax.ShapeDtypeStruct((8,seq),jnp.float32)],
      compiler_params=pltpu.CompilerParams(vmem_limit_bytes=48<<20),
      cost_estimate=pl.CostEstimate(flops=int(nh*4.5*1.1e9), transcendentals=0, bytes_accessed=1<<20),
      name="attn_fwd")(where,*qkv)
    return outs[:n],outs[n],outs[n+1]

def bwd_kernel(where,*refs,nh,blk,n):
    ins,dos,outs=refs[:n],refs[n:2*n],refs[2*n+2:3*n+2]
    ot_ref,lse_ref=refs[2*n:2*n+2]
    kt_ref,dl_ref,dqt_ref,qkv_ref,do_ref,d_ref,sems,do_sems=refs[3*n+2:]
    seq=qkv_ref.shape[0]; w=nh*HD
    nb=seq//blk
    run_copies(by_source(where,ins,qkv_ref,sems)+by_source(where,dos,do_ref,do_sems))
    q_ref,k_ref,v_ref=(qkv_ref.at[:,i*w:(i+1)*w] for i in range(3))
    for b in range(nb):
        sl=slice(b*blk,(b+1)*blk)
        kt_ref[:,sl]=_tr(k_ref[sl,:])
        dot_=jnp.transpose(do_ref[sl,:].astype(jnp.float32))
        pr=dot_*ot_ref[:,sl]
        for h in range(nh):
            dl_ref[h:h+1,sl]=jnp.sum(pr[h*HD:(h+1)*HD],axis=0,keepdims=True)
    dqt_ref[...]=jnp.zeros_like(dqt_ref)
    lane=lax.broadcasted_iota(jnp.int32,(1,w),1)//HD
    tri=lax.broadcasted_iota(jnp.int32,(blk,blk),0)<=lax.broadcasted_iota(jnp.int32,(blk,blk),1)
    def kstep(kb,_):
        k0=pl.multiple_of(kb*blk,blk)
        k=k_ref[pl.ds(k0,blk),:]
        v=v_ref[pl.ds(k0,blk),:]
        def qs(qb,carry,diag):
            dk,dv=carry
            q0=pl.multiple_of(qb*blk,blk)
            q=q_ref[pl.ds(q0,blk),:]
            do=do_ref[pl.ds(q0,blk),:]
            for h in range(nh):
                qm=jnp.where(lane==h,q,jnp.zeros_like(q))
                dom=jnp.where(lane==h,do,jnp.zeros_like(do))
                s=_nt(k,qm)
                dp=_nt(v,dom)
                p=jnp.exp2(s*C2-lse_ref[h:h+1,pl.ds(q0,blk)])
                if diag: p=jnp.where(tri,p,0.0)
                ds=(p*(dp-dl_ref[h:h+1,pl.ds(q0,blk)])).astype(jnp.bfloat16)
                dv=dv+_nn(p.astype(jnp.bfloat16),dom)
                dk=dk+_nn(ds,qm)
                dqt_ref[h*HD:(h+1)*HD,pl.ds(q0,blk)]+=_nn(kt_ref[h*HD:(h+1)*HD,pl.ds(k0,blk)],ds)
            return dk,dv
        z=jnp.zeros((blk,w),jnp.float32)
        c=qs(kb,(z,z),True)
        dk,dv=lax.fori_loop(kb+1,nb,lambda qb,cc: qs(qb,cc,False),c)
        d_ref[pl.ds(k0,blk),w:2*w]=(dk*RELAX).astype(jnp.bfloat16)
        d_ref[pl.ds(k0,blk),2*w:3*w]=dv.astype(jnp.bfloat16)
        return 0
    lax.fori_loop(0,nb,kstep,0)
    for b in range(nb):
        sl=slice(b*blk,(b+1)*blk)
        d_ref[sl,0:w]=(jnp.transpose(dqt_ref[:,sl])*(1.0/math.sqrt(HD))).astype(jnp.bfloat16)
    run_copies(by_target(where,d_ref,outs,sems))

def attn_bwd(where, qkv, do, ot, lse, nh, blk=512):
    n=len(qkv); rows=qkv[0].shape[0]
    seq=n*rows; w=nh*HD
    blk=min(blk,seq)
    vm=pl.BlockSpec(memory_space=pltpu.VMEM)
    an=pl.BlockSpec(memory_space=pl.ANY)
    return pl.pallas_call(functools.partial(bwd_kernel,nh=nh,blk=blk,n=n),
      grid_spec=pltpu.PrefetchScalarGridSpec(num_scalar_prefetch=1,
        in_specs=[an]*(2*n)+[vm]*2,out_specs=[an]*n,
        scratch_shapes=[pltpu.VMEM((w,seq),jnp.bfloat16),pltpu.VMEM((8,seq),jnp.float32),pltpu.VMEM((w,seq),jnp.float32),
          pltpu.VMEM((seq,3*w),jnp.bfloat16),pltpu.VMEM((seq,w),jnp.bfloat16),pltpu.VMEM((seq,3*w),jnp.bfloat16),
          pltpu.SemaphoreType.DMA((n,)),pltpu.SemaphoreType.DMA((n,))]),
      out_shape=[jax.ShapeDtypeStruct((rows,3*w),jnp.bfloat16)]*n,
      compiler_params=pltpu.CompilerParams(vmem_limit_bytes=56<<20),
      cost_estimate=pl.CostEstimate(flops=int(nh*9.5*1.1e9), transcendentals=0, bytes_accessed=1<<20),
      name="attn_bwd")(where,*qkv,*do,ot,lse)


NORM_EPS = 1e-05
F32 = jnp.float32
BF16 = jnp.bfloat16
SWAP = [(0, 1), (1, 0)]
SEQ_AXES = ("y", "c")
DP_AXES = ("z", "x")
ANY = pl.BlockSpec(memory_space=pl.ANY)
VMEM = pl.BlockSpec(memory_space=pltpu.VMEM)
GELU_K = math.sqrt(2.0 / math.pi)
GELU_A = 0.044715
N_VEC = 12
N_SEQ = 4


def add_low(*terms):
    return sum(t.astype(F32) for t in terms).astype(BF16)


def ring(n):
    return [(i, (i + 1) % n) for i in range(n)]


def uses_rings():
    return lax.axis_size("z") * lax.axis_size("x") <= 8


def here():
    seq = lax.axis_index("y") * lax.axis_size("c") + lax.axis_index("c")
    return jnp.stack([lax.axis_index(a) for a in ("z", "x", "c")] + [seq]).astype(jnp.int32)


def call(kernel, name, where, args, specs, outs, scratch=(), grid=(), out_specs=None, cost=None):
    if out_specs is None:
        out_specs = [VMEM] * len(outs)
    return list(pl.pallas_call(
        kernel,
        grid_spec=pltpu.PrefetchScalarGridSpec(
            num_scalar_prefetch=1,
            grid=grid,
            in_specs=specs,
            out_specs=out_specs,
            scratch_shapes=list(scratch),
        ),
        out_shape=[jax.ShapeDtypeStruct(s, d) for s, d in outs],
        compiler_params=pltpu.CompilerParams(vmem_limit_bytes=60 << 20),
        cost_estimate=cost,
        name=name,
    )(where, *args))


def cost_of(microseconds):
    return pl.CostEstimate(flops=int(microseconds * 1.1e9), transcendentals=0, bytes_accessed=1 << 20)


def tie(value, *others):
    return lax.optimization_barrier((value,) + others)[0]


def together(*values):
    return list(lax.optimization_barrier(tuple(values)))


class Box:
    def __init__(self, v):
        self.v = v


class Stages:
    def __init__(self):
        self.every = []

    def box(self, v):
        self.every.append(Box(v))
        return self.every[-1]

    def boxes(self, values):
        return [self.box(v) for v in values]

    def begin(self, *some):
        return [b.v for b in some]

    def sync(self):
        for box, v in zip(self.every, together(*[b.v for b in self.every])):
            box.v = v


class Gather:
    def __init__(self, stages, shards, core_halves=True):
        self.stages, self.shards, self.core_halves = stages, shards, core_halves
        cur = shards
        if core_halves:
            cur = lax.dynamic_index_in_dim(shards, lax.axis_index("c"), 0, False)
        self.box = stages.box
        self.blocks, self.others = [self.box(cur)], []
        self.swapped = {}

    def z(self):
        (block,) = self.stages.begin(self.blocks[-1])
        self.blocks.append(self.box(lax.ppermute(block, "z", ring(lax.axis_size("z")))))
        return self.blocks[-1]

    def x(self):
        (block,) = self.stages.begin(self.blocks[len(self.others)])
        self.others.append(self.box(lax.ppermute(block, "x", SWAP)))
        return self.others[-1]

    def x_pair(self):
        block = jnp.where(lax.axis_index("y") == 0, self.blocks[0].v, self.blocks[1].v)
        self.others.append(self.box(lax.ppermute(block, "x", SWAP)))

    def y_pair(self):
        self.others.append(self.box(lax.ppermute(self.others[0].v, "y", SWAP)))

    def c(self):
        new = [b for b in self.blocks[1:] + self.others if id(b) not in self.swapped]
        for box, v in zip(new, self.stages.begin(*new)):
            self.swapped[id(box)] = self.box(lax.ppermute(v, "c", SWAP))
        return [self.swapped[id(box)] for box in new]

    def pieces(self):
        mine = [self.others[0]]
        for block, other in zip(self.blocks[1:], self.others[1:]):
            mine += [block, other]
        if not self.core_halves:
            return [self.shards] + self.stages.begin(*mine)
        self.c()
        return [self.shards] + self.stages.begin(*mine, *[self.swapped[id(b)] for b in mine])


def in_halves(weight):
    rows, cols = weight.shape
    return weight.reshape(rows, 2, cols // 2).transpose(1, 0, 2)


def owner_of(index, nz, z, x):
    step, side = (index + 1) // 2, (index + 1) % 2
    return lax.rem(z + nz - step, nz) * 2 + (x if side == 0 else 1 - x)


def paired_owner(index, nz, where):
    y = where[3] // 2
    step = y if index == 0 else 1 - y
    return lax.rem(where[0] + nz - step, nz) * 2 + 1 - where[1]


class Loader:
    def __init__(self, where, pieces, dsts, sems, nz, col=0, paired=False):
        self.copies = []
        self.sems = sems
        if len(pieces[0].shape) == 2:
            self.sides = (0, 1)
            for i, (piece, dst) in enumerate(zip(pieces, dsts)):
                half = dst.shape[2]
                for side in range(2):
                    at = side * (piece.shape[1] // 2) + col
                    self.add(i, side, piece.at[:, at : at + half], dst.at[side])
            return
        z, x, c = where[0], where[1], where[2]
        self.sides = (c, 1 - c)
        rows = pieces[0].shape[1]
        others = (len(pieces) - 1) // 2
        for i, dst in enumerate(dsts):
            half = dst.shape[2]
            groups = dst.shape[1] // (2 * nz * rows)
            for g in range(groups):
                cols = slice(col, col + half)
                col += half
                for k in range(2):
                    side = self.sides[k]
                    blocks = [(z * 2 + x, pieces[0].at[side, :, cols])]
                    for n in range(others):
                        owner = owner_of(n, nz, z, x)
                        if paired and n in (0, 2):
                            owner = paired_owner(n, nz, where)
                        blocks.append((owner, pieces[1 + k * others + n].at[:, cols]))
                    for owner, block in blocks:
                        row = pl.multiple_of((owner * groups + g) * rows, rows)
                        self.add(i, k, block, dst.at[side, pl.ds(row, rows), :])

    def add(self, i, k, src, to):
        self.copies.append((i, k, pltpu.make_async_copy(src, to, self.sems.at[len(self.copies)])))

    def pick(self, dst, half):
        return [
            copy
            for i, k, copy in self.copies
            if (dst is None or i == dst) and (half is None or k == half)
        ]

    def start(self, dst=None, half=None):
        for copy in self.pick(dst, half):
            copy.start()

    def wait(self, dst=None, half=None):
        for copy in self.pick(dst, half):
            copy.wait()


class Writer:
    def __init__(self, sems):
        self.sems, self.copies = sems, []

    def put(self, src, to):
        copy = pltpu.make_async_copy(src, to, self.sems.at[len(self.copies)])
        copy.start()
        self.copies.append(copy)

    def wait(self):
        for copy in self.copies:
            copy.wait()


def n_copies(pieces, groups=1):
    return (len(pieces) + 1) * groups


def norm_parts(v):
    c = v - jnp.mean(v, axis=-1, keepdims=True)
    inv = lax.rsqrt(jnp.mean(c * c, axis=-1, keepdims=True) + NORM_EPS)
    return c * inv, inv


def norm_back(n, inv, gain, e):
    ge = g_e = gain * e
    return (g_e - jnp.mean(ge, axis=-1, keepdims=True) - n * jnp.mean(ge * n, axis=-1, keepdims=True)) * inv


def rowsum(v):
    return jnp.sum(v, axis=0, keepdims=True)


def vectors_kernel(where, *refs, nz, n_bias):
    pieces, vec, bias = refs[:-2], refs[-2], refs[-1]
    z, x = where[0], where[1]
    own = pieces[0].shape[0]
    order = [z * 2 + x] + [owner_of(i, nz, z, x) for i in range(2 * nz - 1)]
    got = [jnp.transpose(piece[...].astype(F32))[: N_VEC + n_bias] for piece in pieces]
    for o in range(2 * nz):
        acc = jnp.zeros(got[0].shape, F32)
        for at, piece in zip(order, got):
            acc = jnp.where(at == o, piece, acc)
        vec[0:N_VEC, o * own : (o + 1) * own] = acc[:N_VEC]
        for j in range(n_bias):
            lo = (o * n_bias + j) * own
            bias[0:1, lo : lo + own] = acc[N_VEC + j : N_VEC + j + 1]


def small_vectors(pieces, width, n_bias):
    nz = lax.axis_size("z")
    own = pieces[0].shape[-2]
    at = pieces[1].shape[1] // own - 1
    blocks = pieces[: 2 * nz]
    return call(
        functools.partial(vectors_kernel, nz=nz, n_bias=n_bias),
        "vectors",
        here(),
        blocks,
        [pl.BlockSpec((None, own, own), lambda i, w: (0, 0, at))]
        + [pl.BlockSpec((own, own), lambda i, w: (0, at))] * (len(blocks) - 1),
        [((16, width), F32), ((1, n_bias * 2 * nz * own), F32)],
        grid=(1,),
        out_specs=[
            pl.BlockSpec((16, width), lambda i, w: (0, 0)),
            pl.BlockSpec((1, n_bias * 2 * nz * own), lambda i, w: (0, 0)),
        ],
        cost=cost_of(2),
    )


def plain_vectors(small, width):
    placed = lax.all_gather(small, DP_AXES, axis=0, tiled=False).astype(F32)
    vec = placed[:, :N_VEC].transpose(1, 0, 2).reshape(N_VEC, width)
    return jnp.pad(vec, ((0, 4), (0, 0))), placed[:, N_VEC:].reshape(1, -1)


def first_norm(tok, vec, normed):
    rows = min(64, tok.shape[0])

    def body(i, carry):
        at = pl.ds(pl.multiple_of(i * rows, rows), rows)
        n, inv = norm_parts(tok[at, :].astype(F32))
        normed[at, :] = (n * vec[4:5, :] + vec[8:9, :]).astype(BF16)
        return carry

    lax.fori_loop(0, tok.shape[0] // rows, body, 0)


def qkv_kernel(where, first, vec, *refs, nz, chunk, chunks, n_pieces):
    pieces, refs = refs[:n_pieces], list(refs[n_pieces:])
    n_seq = N_SEQ
    outs = [refs.pop(0) for _ in range(n_seq)]
    normed = refs.pop(0) if chunk == 0 else first
    w, stage, sems, out_sems = refs
    rows, cols = outs[0].shape
    per_side = n_seq // 2
    load = Loader(where, pieces, [w], sems, nz, chunk * per_side * cols)
    load.start()
    if chunk == 0:
        first_norm(first, vec, normed)
    load.wait()
    wide = cols // 3
    grp = wide * chunks
    scale = 1.0 / (RELAX * math.sqrt(HD))
    for side in range(2):
        mixed = _nn(normed[...], w[side])
        for j in range(per_side):
            s = side * per_side + j
            lo = s * grp + chunk * wide
            block = mixed[:, j * cols : (j + 1) * cols]
            at = slice(s * rows, (s + 1) * rows)
            stage[at, 0:wide] = ((block[:, 0:wide] + vec[0:1, lo : lo + wide]) * scale).astype(BF16)
            stage[at, wide : 2 * wide] = block[:, wide : 2 * wide].astype(BF16)
            stage[at, 2 * wide :] = (block[:, 2 * wide :] + vec[1:2, lo : lo + wide]).astype(BF16)
    run_copies(by_target(where, stage, outs, out_sems))


def gelu_parts(h):
    return jnp.tanh(h * (GELU_K + (GELU_K * GELU_A) * (h * h)))


def up_kernel(where, *refs, nz, n_att, n_pieces):
    refs = list(refs)
    att_in = [[refs.pop(0) for _ in range(N_SEQ)] for _ in range(n_att)]
    tok, vec, fc1_b = [refs.pop(0) for _ in range(3)]
    pieces = [refs.pop(0) for _ in range(n_pieces)]
    out_att, out_branch, out_residual, out_normed, out_hidden, out_active = [refs.pop(0) for _ in range(6)]
    proj_w, fc1_w, attended, branch, residual, normed_two, hidden, active, in_sems, out_sems = refs
    load = Loader(where, pieces, (proj_w, fc1_w), in_sems, nz)
    load.start(0)
    load.start(1)
    out = Writer(out_sems)
    rows, width = tok.shape
    part = att_in[0][0].shape[1]
    for i in range(N_SEQ):
        s = jnp.bitwise_xor(where[3], i)
        for j in range(n_att):
            lo = pl.multiple_of((s * n_att + j) * part, part)
            attended[:, pl.ds(lo, part)] = att_in[j][i][...]
    out.put(attended, out_att)
    load.wait(0)
    half = width // 2
    for side in range(2):
        cols = slice(side * half, (side + 1) * half)
        branch[:, cols] = _nn(attended[...], proj_w[side]) + vec[2:3, cols]
    out.put(branch, out_branch)
    step = min(64, rows)

    def norms(i, carry):
        at = pl.ds(pl.multiple_of(i * step, step), step)
        n, inv = norm_parts(branch[at, :])
        r = tok[at, :].astype(F32) + (n * vec[5:6, :] + vec[9:10, :])
        residual[at, :] = r
        n, inv = norm_parts(r)
        normed_two[at, :] = (n * vec[6:7, :] + vec[10:11, :]).astype(BF16)
        return carry

    lax.fori_loop(0, rows // step, norms, 0)
    out.put(residual, out_residual)
    out.put(normed_two, out_normed)
    load.wait(1)
    ff = hidden.shape[1]
    blk = 512
    for i in range(ff // blk):
        at = slice(i * blk, (i + 1) * blk)
        side, col = divmod(i * blk, ff // 2)
        h = _nn(normed_two[...], fc1_w[side, :, col : col + blk]) + fc1_b[:, at]
        hidden[:, at] = h
        active[:, at] = (0.5 * h * (1.0 + gelu_parts(h))).astype(BF16)
        out.put(hidden.at[:, at], out_hidden.at[:, at])
        out.put(active.at[:, at], out_active.at[:, at])
    out.wait()


def mid_kernel(where, active_in, residual_in, hidden_in, out_grad, vec, *refs, nz, n_pieces):
    pieces, refs = refs[:n_pieces], list(refs[n_pieces:])
    layer_out, d_second, out_hidden, sums, fc1_sum = [refs.pop(0) for _ in range(5)]
    fc2_w, active, residual, wide, hidden, d_hidden, load_sems, in_sems, out_sems = refs
    rows, width = out_grad.shape
    ff = hidden.shape[1]
    blk = 512
    load = Loader(where, pieces, (fc2_w,), load_sems, nz, 0, True)
    out = Writer(out_sems)
    blocks = [slice(i * blk, (i + 1) * blk) for i in range(ff // blk)]
    ins = [
        pltpu.make_async_copy(active_in, active, in_sems.at[0]),
        pltpu.make_async_copy(residual_in, residual, in_sems.at[1]),
    ] + [
        pltpu.make_async_copy(hidden_in.at[:, at], hidden.at[:, at], in_sems.at[2 + i])
        for i, at in enumerate(blocks)
    ]
    ins[0].start()
    load.start(0, 0)
    load.start(0, 1)
    for copy in ins[1:]:
        copy.start()
    half = width // 2
    ins[0].wait()
    for k in range(2):
        load.wait(0, k)
        side = load.sides[k]
        cols = pl.ds(pl.multiple_of(side * half, half), half)
        wide[:, cols] = _nn(active[...], fc2_w[side]) + vec[3:4, cols]
    ins[1].wait()
    step = min(64, rows)

    def top(i, carry):
        g_sum, s_sum, b_sum = carry
        at = pl.ds(pl.multiple_of(i * step, step), step)
        n, inv = norm_parts(wide[at, :])
        e = out_grad[at, :].astype(F32)
        layer_out[at, :] = (residual[at, :] + (n * vec[7:8, :] + vec[11:12, :])).astype(BF16)
        d = norm_back(n, inv, vec[7:8, :], e).astype(BF16)
        d_second[at, :] = d
        return g_sum + rowsum(e * n), s_sum + rowsum(e), b_sum + rowsum(d.astype(F32))

    zero = jnp.zeros((1, width), F32)
    g_sum, s_sum, b_sum = lax.fori_loop(0, rows // step, top, (zero, zero, zero))
    sums[...] = jnp.zeros_like(sums)
    sums[3:4, :] = b_sum
    sums[7:8, :] = g_sum
    sums[11:12, :] = s_sum
    for copy in ins[2:]:
        copy.wait()
    for i, at in enumerate(blocks):
        d = _nt(d_second[:, 0:half], fc2_w[0, at, :]) + _nt(d_second[:, half:], fc2_w[1, at, :])
        h = hidden[:, at]
        t = gelu_parts(h)
        square = h * h
        bend = h * (0.5 * GELU_K + (1.5 * GELU_K * GELU_A) * square)
        low = (d * ((0.5 + 0.5 * t) + (1.0 - t * t) * bend)).astype(BF16)
        d_hidden[:, at] = low
        fc1_sum[:, at] = rowsum(low.astype(F32))
        if i % 2 == 1:
            pair = slice((i - 1) * blk, (i + 1) * blk)
            out.put(d_hidden.at[:, pair], out_hidden.at[:, pair])
    out.wait()


def back_kernel(where, out_grad, vec, sums_in, d_hidden_in, residual_in, branch_in, *refs, nz, n_att, n_pieces):
    refs = list(refs)
    ups = [refs.pop(0) for _ in range(n_pieces)]
    out_residual, out_branch, sums = [refs.pop(0) for _ in range(3)]
    d_att = [[refs.pop(0) for _ in range(N_SEQ)] for _ in range(n_att)]
    proj_w, fc1_w, d_hidden, residual, branch, wide, d_residual, d_branch = [refs.pop(0) for _ in range(8)]
    stages = [refs.pop(0) for _ in range(n_att)]
    up_sems, in_sems, out_sems = refs
    rows, width = out_grad.shape
    ff = d_hidden.shape[1]
    load = Loader(where, ups, (proj_w, fc1_w), up_sems, nz)
    out = Writer(out_sems)
    ff_half = ff // 2
    ins = []
    for k in range(2):
        at = pl.ds(pl.multiple_of(load.sides[k] * ff_half, ff_half), ff_half)
        ins.append(pltpu.make_async_copy(d_hidden_in.at[:, at], d_hidden.at[:, at], in_sems.at[k]))
        ins[k].start()
        load.start(1, k)
    ins.append(pltpu.make_async_copy(residual_in, residual, in_sems.at[2]))
    ins.append(pltpu.make_async_copy(branch_in, branch, in_sems.at[3]))
    ins[2].start()
    ins[3].start()
    load.start(0)
    half = width // 2
    for k in range(2):
        ins[k].wait()
        load.wait(1, k)
        side = load.sides[k]
        at = pl.ds(pl.multiple_of(side * ff_half, ff_half), ff_half)
        for q in range(2):
            rows_at = slice(q * half, (q + 1) * half)
            part = _nt(d_hidden[:, at], fc1_w[side, rows_at, :])
            wide[:, rows_at] = part if k == 0 else wide[:, rows_at] + part
    ins[2].wait()
    ins[3].wait()
    step = min(64, rows)

    def mid(i, carry):
        g2, s2, g1, s1, b_sum = carry
        at = pl.ds(pl.multiple_of(i * step, step), step)
        e = wide[at, :]
        n, inv = norm_parts(residual[at, :])
        d = out_grad[at, :].astype(F32) + norm_back(n, inv, vec[6:7, :], e)
        d_residual[at, :] = d
        g2, s2 = g2 + rowsum(e * n), s2 + rowsum(e)
        n, inv = norm_parts(branch[at, :])
        low = norm_back(n, inv, vec[5:6, :], d).astype(BF16)
        d_branch[at, :] = low
        return g2, s2, g1 + rowsum(d * n), s1 + rowsum(d), b_sum + rowsum(low.astype(F32))

    zero = jnp.zeros((1, width), F32)
    g2, s2, g1, s1, b_sum = lax.fori_loop(0, rows // step, mid, (zero,) * 5)
    out.put(d_residual, out_residual)
    out.put(d_branch, out_branch)
    sums[...] = sums_in[...]
    for row, v in ((6, g2), (10, s2), (5, g1), (9, s1), (2, b_sum)):
        sums[row : row + 1, :] = v
    load.wait(0)
    part = stages[0].shape[1]
    for s in range(N_SEQ):
        at = slice(s * n_att * part, (s + 1) * n_att * part)
        low = (_nt(d_branch[:, 0:half], proj_w[0, at, :]) + _nt(d_branch[:, half:], proj_w[1, at, :])).astype(BF16)
        for j in range(n_att):
            stages[j][s * rows : (s + 1) * rows, :] = low[:, j * part : (j + 1) * part]
    for j in range(n_att):
        for i, ref in enumerate(d_att[j]):
            at = pl.multiple_of(jnp.bitwise_xor(where[3], i) * rows, rows)
            out.put(stages[j].at[pl.ds(at, rows), :], ref)
    out.wait()


def run_up(where, att, tokens, vec, fc1_b, ups):
    nz = lax.axis_size("z")
    rows, width = tokens.shape
    ff = fc1_b.shape[1]
    flat = [block for blocks in att for block in blocks]
    big = (rows, width)
    outs = [(big, BF16), (big, F32), (big, F32), (big, BF16), ((rows, ff), F32), ((rows, ff), BF16)]
    return call(
        functools.partial(up_kernel, nz=nz, n_att=len(att), n_pieces=len(ups)),
        "up",
        where,
        flat + [tokens, vec, fc1_b] + ups,
        [VMEM] * (len(flat) + 3) + [ANY] * len(ups),
        outs,
        [
            pltpu.VMEM((2, width, width // 2), BF16),
            pltpu.VMEM((2, width, ff // 2), BF16),
        ]
        + [pltpu.VMEM(shape, dtype) for shape, dtype in outs]
        + [pltpu.SemaphoreType.DMA((n_copies(ups, 2),)), pltpu.SemaphoreType.DMA((4 + 2 * (ff // 512),))],
        out_specs=[ANY] * len(outs),
        cost=cost_of(20),
    )


def run_mid(where, active, residual, hidden, out_grad, vec, downs):
    nz = lax.axis_size("z")
    rows, width = out_grad.shape
    ff = active.shape[1]
    big = (rows, width)
    return call(
        functools.partial(mid_kernel, nz=nz, n_pieces=len(downs)),
        "mid",
        where,
        [active, residual, hidden, out_grad, vec] + downs,
        [ANY] * 3 + [VMEM] * 2 + [ANY] * len(downs),
        [(big, BF16), (big, BF16), ((rows, ff), BF16), ((16, width), F32), ((1, ff), F32)],
        [
            pltpu.VMEM((2, ff, width // 2), BF16),
            pltpu.VMEM((rows, ff), BF16),
            pltpu.VMEM(big, F32),
            pltpu.VMEM(big, F32),
            pltpu.VMEM((rows, ff), F32),
            pltpu.VMEM((rows, ff), BF16),
            pltpu.SemaphoreType.DMA((n_copies(downs, ff // width),)),
            pltpu.SemaphoreType.DMA((2 + ff // 512,)),
            pltpu.SemaphoreType.DMA((ff // 512,)),
        ],
        out_specs=[VMEM] * 2 + [ANY] + [VMEM] * 2,
        cost=cost_of(28),
    )


def run_back(where, out_grad, vec, sums, d_hidden, residual, branch, ups, n_att):
    nz = lax.axis_size("z")
    rows, width = out_grad.shape
    ff = d_hidden.shape[1]
    big = (rows, width)
    part = width // N_SEQ // n_att
    outs = [(big, F32), (big, BF16), ((16, width), F32)]
    outs += [((rows, part), BF16)] * (n_att * N_SEQ)
    return call(
        functools.partial(back_kernel, nz=nz, n_att=n_att, n_pieces=len(ups)),
        "back",
        where,
        [out_grad, vec, sums, d_hidden, residual, branch] + ups,
        [VMEM] * 3 + [ANY] * (3 + len(ups)),
        outs,
        [
            pltpu.VMEM((2, width, width // 2), BF16),
            pltpu.VMEM((2, width, ff // 2), BF16),
            pltpu.VMEM((rows, ff), BF16),
            pltpu.VMEM(big, F32),
            pltpu.VMEM(big, F32),
            pltpu.VMEM(big, F32),
            pltpu.VMEM(big, F32),
            pltpu.VMEM(big, BF16),
        ]
        + [pltpu.VMEM((N_SEQ * rows, part), BF16)] * n_att
        + [
            pltpu.SemaphoreType.DMA((n_copies(ups, 2),)),
            pltpu.SemaphoreType.DMA((4,)),
            pltpu.SemaphoreType.DMA((2 + n_att * N_SEQ,)),
        ],
        out_specs=[ANY] * 2 + [VMEM] + [ANY] * (n_att * N_SEQ),
        cost=cost_of(20),
    )


def slot_owner(i, nz, where):
    z, x = where[0], where[1]
    return lax.rem(z + 2 * nz - 1 - i % nz, nz) * 2 + (1 - x if i < nz else x)


def contract_rows(left, right):
    return lax.dot_general(left, right, (((0,), (0,)), ((), ())), preferred_element_type=F32)


def halves_of(ref, c):
    half = ref.shape[1] // 2
    return [ref[:, pl.ds(pl.multiple_of(h * half, half), half)] for h in (1 - c, c)]


def columns_of(ref, owner, count):
    return ref[:, pl.ds(pl.multiple_of(owner * count, count), count)]


def row_grad_kernel(where, lhs, rhs, *outs, nz):
    c = where[2]
    rows = outs[0].shape[1]
    half = rhs.shape[1] // 2
    blk = min(1024, half)
    for side in range(2):
        owners = [slot_owner(side * nz + i, nz, where) for i in range(nz)]
        left = jnp.concatenate([columns_of(lhs, o, rows) for o in owners], axis=1)
        for h in range(2):
            out = outs[2 * side + h]
            base = (1 - c if h == 0 else c) * half
            for n in range(half // blk):
                right = rhs[:, pl.ds(pl.multiple_of(base + n * blk, blk), blk)]
                low = contract_rows(left, right).astype(BF16)
                for i in range(nz):
                    out[i, :, n * blk : (n + 1) * blk] = low[i * rows : (i + 1) * rows]


def wide_grad_kernel(where, *refs, nz, side):
    ins, outs = refs[:4], refs[4:6]
    normed_two, d_hidden, active, d_second = refs[6:10]
    stages, in_sems, out_sems = refs[10:12], refs[12], refs[13]
    c = where[2]
    rows = outs[0].shape[1]
    owners = [slot_owner(side * nz + i, nz, where) for i in range(nz)]
    half = d_hidden.shape[1] // 2
    blk = min(1024, half)
    loads = [pltpu.make_async_copy(ins[0], normed_two, in_sems.at[0])]
    for k, h in enumerate((1 - c, c)):
        at = pl.ds(pl.multiple_of(h * half, half), half)
        loads.append(pltpu.make_async_copy(ins[1].at[:, at], d_hidden.at[:, at], in_sems.at[1 + k]))
    loads.append(pltpu.make_async_copy(ins[3], d_second, in_sems.at[3]))
    wide = active.shape[1] // (2 * nz)
    for i in range(nz):
        at = pl.ds(pl.multiple_of(owners[i] * wide, wide), wide)
        loads.append(pltpu.make_async_copy(ins[2].at[:, at], active.at[:, at], in_sems.at[4 + i]))
    for load in loads:
        load.start()
    write = Writer(out_sems)
    loads[0].wait()
    left = jnp.concatenate([columns_of(normed_two, o, rows) for o in owners], axis=1)
    for h, out in enumerate(stages):
        loads[1 + h].wait()
        base = (1 - c if h == 0 else c) * half
        for n in range(half // blk):
            right = d_hidden[:, pl.ds(pl.multiple_of(base + n * blk, blk), blk)]
            low = contract_rows(left, right).astype(BF16)
            for i in range(nz):
                out[i, :, n * blk : (n + 1) * blk] = low[i * rows : (i + 1) * rows]
    loads[3].wait()
    rights = halves_of(d_second, c)
    cols = d_second.shape[1] // 2
    for i in range(nz):
        loads[4 + i].wait()
        left = columns_of(active, owners[i], wide)
        for stage, out, right in zip(stages, outs, rights):
            low = contract_rows(left, right).astype(BF16)
            for g in range(wide // rows):
                lo = half + g * cols
                stage[i, :, lo : lo + cols] = low[g * rows : (g + 1) * rows]
            write.put(stage.at[i], out.at[i])
    write.wait()


def run_wide_grad(where, normed_two, d_hidden, active, d_second, rows, side):
    nz = lax.axis_size("z")
    tok, width = normed_two.shape
    ff = active.shape[1]
    out = ((nz, rows, ff // 2 + ff // width * width // 2), BF16)
    return call(
        functools.partial(wide_grad_kernel, nz=nz, side=side),
        "wide_grad",
        where,
        (normed_two, d_hidden, active, d_second),
        [ANY] * 4,
        [out] * 2,
        [
            pltpu.VMEM((tok, width), BF16),
            pltpu.VMEM((tok, ff), BF16),
            pltpu.VMEM((tok, ff), BF16),
            pltpu.VMEM((tok, width), BF16),
            pltpu.VMEM(*out),
            pltpu.VMEM(*out),
            pltpu.SemaphoreType.DMA((4 + nz,)),
            pltpu.SemaphoreType.DMA((2 * nz,)),
        ],
        out_specs=[ANY] * 2,
        cost=cost_of(9),
    )


def grads(kernel, name, where, args, rows, half, specs=None, scratch=(), count=4, **more):
    nz = lax.axis_size("z")
    return call(
        functools.partial(kernel, nz=nz, **more),
        name,
        where,
        args,
        specs or [VMEM] * len(args),
        [((nz, rows, half), BF16)] * count,
        scratch,
        cost=cost_of(2.5 * count),
    )


def qkv_grad_kernel(where, normed, *refs, nz):
    blocks, outs, (stage, sems) = refs[:N_SEQ], refs[N_SEQ:-2], refs[-2:]
    c = where[2]
    rows = outs[0].shape[1]
    tok = normed.shape[0]
    per_side = N_SEQ // 2
    run_copies(by_source(where, blocks, stage, sems))
    for h in range(2):
        base = (1 - c if h == 0 else c) * per_side
        right = jnp.concatenate(
            [stage[pl.ds(pl.multiple_of((base + j) * tok, tok), tok), :] for j in range(per_side)], axis=1
        )
        for side in range(2):
            owners = [slot_owner(side * nz + i, nz, where) for i in range(nz)]
            left = jnp.concatenate([columns_of(normed, o, rows) for o in owners], axis=1)
            low = contract_rows(left, right).astype(BF16)
            for i in range(nz):
                outs[2 * side + h][i] = low[i * rows : (i + 1) * rows]


class Reduce:
    def __init__(self, stages, parts):
        self.stages, self.parts_x = stages, parts
        self.box = stages.box
        self.from_x, self.out = [], []
        self.steps, self.ready, self.blocks_out = 0, False, []

    def set_first(self, outs):
        self.first = self.stages.boxes(outs)

    def set_second(self, outs):
        self.second = self.stages.boxes(outs)

    def c_first(self):
        self.got = self.box(lax.ppermute(self.first[0].v, "c", SWAP))

    def c_second(self):
        self.own_got = self.box(lax.ppermute(self.second[0].v, "c", SWAP))

    def c(self):
        self.c_first()
        self.c_second()

    def sum(self, count=1):
        got, kept = self.got.v, self.first[1].v
        self.size = got.shape[0] // self.parts_x
        for unused in range(count):
            at = len(self.out) * self.size
            self.out.append(self.box(add_low(kept[at : at + self.size], got[at : at + self.size])))

    def x(self):
        if len(self.out) == len(self.from_x):
            self.sum()
        self.from_x.append(self.box(lax.ppermute(self.out[len(self.from_x)].v, "x", SWAP)))

    def add(self):
        step = self.steps
        ready = [self.from_x[step // self.size]] + ([self.passed] if step > 0 else [])
        ready = self.stages.begin(*ready)
        terms = [self.second[1].v[step], self.own_got.v[step], ready[0][step % self.size]] + ready[1:]
        self.cur = self.box(add_low(*terms))
        self.steps += 1

    def z(self):
        if not self.ready:
            self.add()
        self.ready = False
        self.passed = self.box(lax.ppermute(self.cur.v, "z", ring(lax.axis_size("z"))))
        return self.passed

    def blocks(self):
        crossed = self.from_x[0].v
        return [
            add_low(self.second[1].v[i], self.own_got.v[i], crossed[i])
            for i in range(lax.axis_size("z"))
        ]

    def prepare(self, *others):
        blocks = self.blocks()
        if others:
            blocks = [jnp.concatenate(b, axis=1) for b in zip(blocks, *[o.blocks() for o in others])]
        self.blocks_out = self.stages.boxes(blocks)

    def direct(self):
        nz = lax.axis_size("z")
        if not self.blocks_out:
            self.prepare()
        blocks = [b.v for b in self.blocks_out]
        self.kept = blocks[-1]
        self.parts = [
            self.box(lax.ppermute(blocks[i], "z", [(s, (s - 1 - i) % nz) for s in range(nz)]))
            for i in range(nz - 1)
        ]
        return self.parts

    def gather_parts(self):
        self.cur = self.box(add_low(self.kept, *self.stages.begin(*self.parts)))

    def y(self):
        if hasattr(self, "parts"):
            self.gather_parts()
        elif not self.ready:
            self.add()
        self.from_y = self.box(lax.ppermute(self.cur.v, "y", SWAP))
        return self.from_y

    def last_c(self):
        (got,) = self.stages.begin(self.from_y)
        self.low = add_low(self.cur.v, got)
        self.other = self.box(lax.ppermute(self.low, "c", SWAP))
        return self.other

    def finish(self):
        c = lax.axis_index("c")
        low, (other,) = self.low, self.stages.begin(self.other)
        return jnp.where(c == 0, low, other), jnp.where(c == 0, other, low)


class SmallReduce:
    def __init__(self, stages, grads):
        self.stages, self.box = stages, stages.box
        self.cur = self.box(grads.astype(BF16))

    def seq(self):
        (cur,) = self.stages.begin(self.cur)
        both = [(i, i ^ 3) for i in range(4)]
        self.parts = [
            self.box(lax.ppermute(cur, "c", SWAP)),
            self.box(lax.ppermute(cur, "y", SWAP)),
            self.box(lax.ppermute(cur, SEQ_AXES, both)),
        ]
        return self.parts

    def x(self):
        nz = lax.axis_size("z")
        cur = add_low(self.cur.v, *self.stages.begin(*self.parts))
        self.keep = cur[nz:]
        self.got = self.box(lax.ppermute(cur[:nz], "x", SWAP))
        return [self.got]

    def z(self):
        nz = lax.axis_size("z")
        (got,) = self.stages.begin(self.got)
        cur = add_low(self.keep, got)
        self.keep = cur[nz - 1]
        self.parts = [
            self.box(lax.ppermute(cur[i], "z", [(s, (s - 1 - i) % nz) for s in range(nz)]))
            for i in range(nz - 1)
        ]
        return self.parts

    def finish(self):
        return add_low(self.keep, *self.stages.begin(*self.parts)).astype(F32)


def reduce_plain(lhs, rhs):
    grad = lax.dot_general(
        lhs, rhs, (((0,), (0,)), ((), ())), preferred_element_type=F32
    ).astype(BF16)
    part = lax.psum_scatter(grad, DP_AXES, scatter_dimension=0, tiled=True)
    return lax.psum(part, SEQ_AXES).astype(F32)


def last_kernel(where, *refs, nz, chunks, n_pieces, rings):
    refs = list(refs)
    blocks = [[refs.pop(0) for _ in range(N_SEQ)] for _ in range(chunks)]
    tok, d_residual, vec, sums, fc1_sum = [refs.pop(0) for _ in range(5)]
    pieces = [refs.pop(0) for _ in range(n_pieces)]
    tokens_grad, small = refs.pop(0), refs.pop(0)
    ws = [refs.pop(0) for _ in range(chunks)]
    stages = [refs.pop(0) for _ in range(chunks)]
    wide, total, in_sems = refs.pop(0), refs.pop(0), refs.pop(0)
    loads = [
        Loader(where, pieces, [w], sem, nz, j * w.shape[2]) for j, (w, sem) in enumerate(zip(ws, refs))
    ]
    for load in loads:
        load.start()
    rows, width = tok.shape
    n_seq, cols = N_SEQ, stages[0].shape[1]
    run_copies(
        [copy for j in range(chunks) for copy in by_source(where, blocks[j], stages[j], in_sems.at[j])]
    )
    d_mixed = [stage.reshape(n_seq, rows, cols) for stage in stages]
    part = cols // 3
    zero = jnp.zeros((1, width), F32)
    total[...] = sums[...]
    for j in range(chunks):
        for s in range(n_seq):
            lo = (s * chunks + j) * part
            total[0:1, lo : lo + part] = rowsum(d_mixed[j][s, :, 0:part].astype(F32))
            total[1:2, lo : lo + part] = rowsum(d_mixed[j][s, :, 2 * part :].astype(F32))
    for load in loads:
        load.wait()
    quarter = width // 4
    per_side = n_seq // 2
    for q in range(4):
        at = slice(q * quarter, (q + 1) * quarter)
        acc = None
        for j in range(chunks):
            for side in range(2):
                left = jnp.concatenate([d_mixed[j][side * per_side + i] for i in range(per_side)], axis=1)
                term = _nt(left, ws[j][side, at, :])
                acc = term if acc is None else acc + term
        wide[:, at] = acc
    step = min(64, rows)

    def norms(i, carry):
        g, s = carry
        at = pl.ds(pl.multiple_of(i * step, step), step)
        e = wide[at, :]
        n, inv = norm_parts(tok[at, :].astype(F32))
        tokens_grad[at, :] = (d_residual[at, :] + norm_back(n, inv, vec[4:5, :], e)).astype(BF16)
        return g + rowsum(e * n), s + rowsum(e)

    g, s = lax.fori_loop(0, rows // step, norms, (zero, zero))
    total[4:5, :] = g
    total[8:9, :] = s
    if not rings:
        small[...] = total[...]
        return
    z, x = where[0], where[1]
    own = width // (2 * nz)
    n_bias = fc1_sum.shape[1] // width
    for o in range(2 * nz):
        slot = lax.rem(z + 2 * nz - 1 - o // 2, nz) + jnp.where(x == o % 2, nz, 0)
        small[slot, 0:N_VEC, :] = total[0:N_VEC, o * own : (o + 1) * own]
        for j in range(n_bias):
            lo = (o * n_bias + j) * own
            small[slot, N_VEC + j : N_VEC + j + 1, :] = fc1_sum[:, lo : lo + own]


def last(where, d_mixed, tokens, d_residual, vec, sums, fc1_sum, pieces):
    nz = lax.axis_size("z")
    rings = uses_rings()
    rows, width = tokens.shape
    chunks = len(d_mixed)
    small = ((2 * nz, N_VEC + fc1_sum.shape[1] // width, width // (2 * nz)), F32) if rings else ((16, width), F32)
    return call(
        functools.partial(last_kernel, nz=nz, chunks=chunks, n_pieces=len(pieces), rings=rings),
        "last",
        where,
        [b for blocks in d_mixed for b in blocks] + [tokens, d_residual, vec, sums, fc1_sum] + list(pieces),
        [ANY] * (chunks * N_SEQ) + [VMEM] * 5 + [ANY] * len(pieces),
        [((rows, width), BF16), small],
        [pltpu.VMEM((2, width, 3 * width // chunks // 2), BF16)] * chunks
        + [pltpu.VMEM((N_SEQ * rows, 3 * width // chunks // N_SEQ), BF16)] * chunks
        + [pltpu.VMEM((rows, width), F32), pltpu.VMEM((16, width), F32), pltpu.SemaphoreType.DMA((chunks, N_SEQ))]
        + [pltpu.SemaphoreType.DMA((n_copies(pieces),))] * chunks,
        cost=cost_of(12),
    )


def reduce_small(small, fc1_sum, own):
    n_dp = lax.axis_size("z") * lax.axis_size("x")
    low = jnp.concatenate(
        (small[:N_VEC].reshape(N_VEC, n_dp, own).transpose(1, 0, 2), fc1_sum.reshape(n_dp, -1, own)),
        axis=1,
    )
    part = lax.psum_scatter(low, DP_AXES, scatter_dimension=0, tiled=False)
    return lax.psum(part.astype(BF16), SEQ_AXES).astype(F32)


def exchange(blocks):
    both = [(i, i ^ 3) for i in range(4)]
    return [
        blocks[0],
        lax.ppermute(blocks[1], "c", SWAP),
        lax.ppermute(blocks[2], "y", SWAP),
        lax.ppermute(blocks[3], SEQ_AXES, both),
    ]


def per_device(
    tokens,
    out_grad,
    qkv_weight,
    qv_bias,
    proj_weight,
    fc1_weight,
    fc1_bias,
    fc2_weight,
    out_bias,
    norm_gains,
    norm_shifts,
):
    n_seq = lax.axis_size("y") * lax.axis_size("c")
    rows, width = tokens.shape
    own = qv_bias.shape[1]
    chunks = CHUNKS
    grp = width // n_seq
    part = grp // chunks
    heads = part // HD
    seq_len = n_seq * rows
    nz = lax.axis_size("z")
    where = here()
    qkv_shards = qkv_weight.reshape(-1, 3, n_seq, chunks, part).transpose(3, 0, 2, 1, 4)
    qkv_shards = qkv_shards.reshape(chunks, -1, 3 * width // chunks)
    small = jnp.concatenate(
        (qv_bias, out_bias, norm_gains, norm_shifts, fc1_bias.reshape(-1, own)), axis=0
    )
    rings = uses_rings()
    st = Stages()
    ff = fc1_weight.shape[1]
    r = proj_weight.shape[0]
    qkv_cat = jnp.concatenate([in_halves(w) for w in qkv_shards], axis=2)
    groups = fc2_weight.shape[0] // r
    if rings:
        fc2_groups = fc2_weight.reshape(groups, -1, 2, width // 2).transpose(2, 1, 0, 3)
        n_bias = small.shape[0] - N_VEC
        columns = jnp.pad(small.T, ((0, 0), (0, own - small.shape[0])))
        qkv_in = Gather(st, jnp.concatenate((qkv_cat, jnp.stack((columns, columns))), axis=2))
        up_in = Gather(st, jnp.concatenate((in_halves(proj_weight), in_halves(fc1_weight)), axis=2))
        down_in = Gather(st, fc2_groups.reshape(2, -1, groups * width // 2))
        for step in range(nz):
            if step > 0:
                st.sync()
                qkv_in.c()
            qkv_in.x()
            if step < nz - 1:
                qkv_in.z()
            else:
                up_in.z()
                up_in.x()
        qkv_pieces = qkv_in.pieces()
        vec, fc1_b = small_vectors(qkv_pieces, width, n_bias)
    else:
        vec, fc1_b = plain_vectors(small, width)
        whole = lax.all_gather(qkv_cat, DP_AXES, axis=1, tiled=True)
        qkv_pieces = [jnp.concatenate((whole[0], whole[1]), axis=1)]
        ups, downs = [
            [lax.all_gather(w, DP_AXES, axis=0, tiled=True) for w in ws]
            for ws in ((proj_weight, fc1_weight), (fc2_weight,))
        ]

    def project(j, first, vec):
        outs = [((rows, 3 * part), BF16)] * n_seq
        if j == 0:
            outs.append(((rows, width), BF16))
        return call(
            functools.partial(qkv_kernel, nz=nz, chunk=j, chunks=chunks, n_pieces=len(qkv_pieces)),
            "qkv",
            where,
            [first, vec] + qkv_pieces,
            [VMEM] * 2 + [ANY] * len(qkv_pieces),
            outs,
            [
                pltpu.VMEM((2, width, 3 * width // chunks // 2), BF16),
                pltpu.VMEM((seq_len, 3 * part), BF16),
                pltpu.SemaphoreType.DMA((n_copies(qkv_pieces),)),
                pltpu.SemaphoreType.DMA((n_seq,)),
            ],
            out_specs=[ANY] * n_seq + [VMEM] * (j == 0),
            cost=cost_of(7),
        )

    def swap(blocks):
        return st.boxes(exchange(st.begin(*blocks)))

    def hops(*some):
        for hop in some if rings else []:
            hop()

    if not rings:
        up_in = down_in = Gather(st, qkv_cat)
    got = st.boxes(project(0, tokens, vec))
    sent_a, normed_box = got[:n_seq], got[n_seq]
    st.sync()
    normed = normed_box.v
    heads_a = swap(sent_a)
    sent_b = st.boxes(project(1, normed, vec))
    hops(up_in.x, up_in.z)
    st.sync()
    heads_b = swap(sent_b)
    by_a = st.begin(*heads_a)
    out_a, cols_a, lse_a = attn_fwd(where, by_a, heads, 512)
    out_a = st.boxes(out_a)
    hops(up_in.x, up_in.z)
    st.sync()
    att_a = swap(out_a)
    by_b = st.begin(*heads_b)
    out_b, cols_b, lse_b = attn_fwd(where, by_b, heads, 512)
    out_b = st.boxes(out_b)
    hops(up_in.x, down_in.z)
    st.sync()
    att_b = swap(out_b)
    hops(*([down_in.x_pair, down_in.z] if rings else []))
    st.sync()
    if rings:
        ups = up_in.pieces()
    hops(*([down_in.c, down_in.y_pair, down_in.x, down_in.z] if rings else []))
    arrived = st.begin(*att_a, *att_b)
    kept = run_up(where, [arrived[:n_seq], arrived[n_seq:]], tokens, vec, fc1_b, ups)
    attended, branch, residual, normed_two, hidden, active = kept
    active_box = st.box(active)
    st.sync()
    hops(down_in.x)
    st.sync()
    if rings:
        downs = down_in.pieces()
    active = active_box.v
    layer_out, d_second, d_hidden, sums, fc1_sum = run_mid(
        where, active, residual, hidden, out_grad, vec, downs
    )

    hidden_box = st.box(d_hidden)

    def proj_grads():
        outs = grads(row_grad_kernel, "proj_grad", where, (attended, d_branch), r, width // 2)
        return reduction(outs, 1)

    def reduction(outs, parts):
        flow = Reduce(st, parts)
        flow.set_first(outs[:2])
        flow.set_second(outs[2:])
        return flow

    if rings:
        wide = Reduce(st, nz)

        def wide_grads(side):
            return run_wide_grad(where, normed_two, hidden_box.v, active, d_second, r, side)

        wide.set_first(wide_grads(0))
        st.sync()
        wide.c_first()
        wide.set_second(wide_grads(1))
        st.sync()
        wide.sum()
        st.sync()
        hops(wide.x, wide.c_second)
    else:
        grad_fc2 = reduce_plain(active, d_second)
        grad_fc1 = reduce_plain(normed_two, d_hidden)
    outs = run_back(where, out_grad, vec, sums, hidden_box.v, residual, branch, ups, chunks)
    d_residual, d_branch, sums = outs[:3]
    branch_box = st.box(d_branch)
    d_out = st.boxes(outs[3:])
    st.sync()
    d_heads_a = swap(d_out[:n_seq])
    d_branch = branch_box.v
    if rings:
        wide.sum(nz - 1)
        wide.add()
        wide.ready = True
    else:
        grad_proj = reduce_plain(attended, d_branch)
    st.sync()
    hops(*([wide.x, wide.z] if rings else []))
    d_heads_b = swap(d_out[n_seq:])
    d_by_a = st.boxes(attn_bwd(where, by_a, st.begin(*d_heads_a), cols_a, lse_a, heads, 512))
    st.sync()
    d_mixed_a = swap(d_by_a)
    hops(*([wide.x, wide.z] if rings else []))
    d_by_b = st.boxes(attn_bwd(where, by_b, st.begin(*d_heads_b), cols_b, lse_b, heads, 512))
    st.sync()
    d_mixed_b = swap(d_by_b)
    hops(*([wide.x, wide.z] if rings else []))

    def qkv_grads(d_mixed):
        outs = grads(
            qkv_grad_kernel,
            "qkv_grad",
            where,
            [normed] + st.begin(*d_mixed),
            r,
            n_seq // 2 * 3 * part,
            [VMEM] + [ANY] * n_seq,
            [pltpu.VMEM((seq_len, 3 * part), BF16), pltpu.SemaphoreType.DMA((n_seq,))],
        )
        return reduction(outs, 1)

    if rings:
        qkv_a = qkv_grads(d_mixed_a)
        proj = proj_grads()
        st.sync()
        hops(qkv_a.c, proj.c)
        st.sync()
        hops(qkv_a.x)
        qkv_b = qkv_grads(d_mixed_b)
    both = st.begin(*d_mixed_a, *d_mixed_b)
    d_mixed_a, d_mixed_b = both[:n_seq], both[n_seq:]
    tokens_grad, small_grads = last(
        where, [d_mixed_a, d_mixed_b], tokens, d_residual, vec, sums, fc1_sum, qkv_pieces
    )
    if rings:
        vecs = SmallReduce(st, small_grads)
        st.sync()
        hops(qkv_b.c, vecs.seq)
        qkv_a.prepare()
        wide.add()
        wide.ready = True
        st.sync()
        hops(qkv_b.x, wide.y, qkv_a.direct)
        st.sync()
        hops(wide.last_c, qkv_b.direct, qkv_a.y, proj.x)
        st.sync()
        hops(qkv_b.y, qkv_a.last_c, proj.direct)
        low = wide.finish()
        at = ff // 2
        grad_fc1 = jnp.concatenate([half[:, :at] for half in low], axis=1).astype(F32)
        grad_fc2 = jnp.stack([half[:, at:] for half in low]).reshape(2, r, groups, width // 2)
        grad_fc2 = grad_fc2.transpose(2, 1, 0, 3).reshape(groups * r, width).astype(F32)
        ffs = st.boxes((grad_fc1, grad_fc2))
        st.sync()
        grad_fc1, grad_fc2 = [b.v for b in ffs]
        hops(qkv_b.last_c, proj.y, vecs.x)
        st.sync()
        hops(proj.last_c, vecs.z)
        total_small = vecs.finish()
    else:
        total_small = reduce_small(small_grads, fc1_sum, own)
    if rings:
        grad_proj = jnp.concatenate(proj.finish(), axis=1).astype(F32)
        total_qkv = [jnp.concatenate(f.finish(), axis=1).astype(F32) for f in (qkv_a, qkv_b)]
    else:
        total_qkv = []
        order = jnp.stack([jnp.bitwise_xor(where[3], i) for i in range(n_seq)])
        for d_mixed in (d_mixed_a, d_mixed_b):
            blocks = jnp.take(jnp.stack(d_mixed), order, axis=0)
            total_qkv.append(reduce_plain(normed, blocks.transpose(1, 0, 2).reshape(rows, -1)))
    qkv_grad = jnp.stack([t.reshape(-1, n_seq, 3, part) for t in total_qkv])
    qkv_grad = qkv_grad.transpose(1, 3, 2, 0, 4).reshape(-1, 3 * width)
    return (
        layer_out,
        tokens_grad,
        qkv_grad,
        total_small[0:2],
        grad_proj,
        grad_fc1,
        total_small[N_VEC:].reshape(-1),
        grad_fc2,
        total_small[2:4],
        total_small[4:8],
        total_small[8:12],
    )


CHUNKS = 2


def solution(mesh):
    n_dp, n_seq = mesh.devices.shape
    fine = Mesh(mesh.devices.reshape(n_dp // 2, 2, n_seq // 2, 2), DP_AXES + SEQ_AXES)
    tok = P(DP_AXES + SEQ_AXES, None)
    by_row = P(DP_AXES, None)
    by_col = P(None, DP_AXES)
    weights = (by_row, by_col, by_row, by_row, P(DP_AXES), by_row, by_col, by_col, by_col)
    return jax.shard_map(
        per_device,
        mesh=fine,
        in_specs=(tok, tok) + weights,
        out_specs=(tok, tok) + weights,
        check_vma=False,
    )
```
